32 devices in a mesh: group: 2 (over core), wide: 16 (over z, y, x).
Axes of the slice: x: 2, y: 2, z: 4, core: 2. Of those that a mesh axis runs over, the one named last changes fastest.
Arguments:
- passage_ids: int32 [32, 512], P(('group', 'wide')), may hold values from 0 to 50431
- query_ids: int32 [128, 32], P(('group', 'wide')), may hold values from 0 to 50431
- passage_len: int32 [32], P(('group', 'wide')), may hold values from 128 to 512, as said below
- query_len: int32 [128], P(('group', 'wide')), may hold values from 8 to 32, as said below
- positive: int32 [128], P(('group', 'wide')), may hold values from 0 to 31
- negatives: int32 [128, 7], P(('group', 'wide')), may hold values from 0 to 31
- valid: int32 [128], P(('group', 'wide')), may hold values from 0 to 1, as said below
- step_count: int32 [1], replicated, may hold values from 1 to 20
- embedding: float32 [768, 50432], P('wide', 'group'), may hold values from -6 to 6
- embedding_m: float32 [768, 50432], P('wide', 'group'), may hold values from -1.7881393e-07 to 1.7881393e-07
- embedding_v: float32 [768, 50432], P('wide', 'group'), may hold values from 6.2269707e-17 to 2.4907883e-16
- attn_in: float32 [768, 2304], P(('group', 'wide')), may hold values from -0.21875 to 0.21875
- attn_in_m: float32 [768, 2304], P(('group', 'wide')), may hold values from -1.9073486e-06 to 1.9073486e-06
- attn_in_v: float32 [768, 2304], P(('group', 'wide')), may hold values from 8.618645e-15 to 3.447458e-14
- attn_out: float32 [768, 768], P(('group', 'wide')), may hold values from -0.875 to 0.875
- attn_out_m: float32 [768, 768], P(('group', 'wide')), may hold values from -1.9073486e-06 to 1.9073486e-06
- attn_out_v: float32 [768, 768], P(('group', 'wide')), may hold values from 8.618645e-15 to 3.447458e-14
- ffn_up: float32 [768, 3072], P(('group', 'wide')), may hold values from -0.21875 to 0.21875
- ffn_up_m: float32 [768, 3072], P(('group', 'wide')), may hold values from -1.9073486e-06 to 1.9073486e-06
- ffn_up_v: float32 [768, 3072], P(('group', 'wide')), may hold values from 8.618645e-15 to 3.447458e-14
- ffn_down: float32 [3072, 768], P(('group', 'wide')), may hold values from -0.109375 to 0.109375
- ffn_down_m: float32 [3072, 768], P(('group', 'wide')), may hold values from -1.9073486e-06 to 1.9073486e-06
- ffn_down_v: float32 [3072, 768], P(('group', 'wide')), may hold values from 8.618645e-15 to 3.447458e-14
- head: float32 [768, 768], P(('group', 'wide')), may hold values from -0.21875 to 0.21875
- head_m: float32 [768, 768], P(('group', 'wide')), may hold values from -1.9073486e-06 to 1.9073486e-06
- head_v: float32 [768, 768], P(('group', 'wide')), may hold values from 8.618645e-15 to 3.447458e-14
- vectors: float32 [11520], P(('group', 'wide')), may hold values from -0.5 to 1.5, as said below
- vectors_m: float32 [11520], P(('group', 'wide')), may hold values from -7.6293945e-06 to 7.6293945e-06
- vectors_v: float32 [11520], P(('group', 'wide')), may hold values from 1.3789832e-13 to 5.515933e-13
Outputs:
- loss: float32 [], replicated
- grad_norm: float32 [], replicated
- new_embedding: float32 [768, 50432], P('wide', 'group')
- new_embedding_m: float32 [768, 50432], P('wide', 'group')
- new_embedding_v: float32 [768, 50432], P('wide', 'group')
- new_attn_in: float32 [768, 2304], P(('group', 'wide'))
- new_attn_in_m: float32 [768, 2304], P(('group', 'wide'))
- new_attn_in_v: float32 [768, 2304], P(('group', 'wide'))
- new_attn_out: float32 [768, 768], P(('group', 'wide'))
- new_attn_out_m: float32 [768, 768], P(('group', 'wide'))
- new_attn_out_v: float32 [768, 768], P(('group', 'wide'))
- new_ffn_up: float32 [768, 3072], P(('group', 'wide'))
- new_ffn_up_m: float32 [768, 3072], P(('group', 'wide'))
- new_ffn_up_v: float32 [768, 3072], P(('group', 'wide'))
- new_ffn_down: float32 [3072, 768], P(('group', 'wide'))
- new_ffn_down_m: float32 [3072, 768], P(('group', 'wide'))
- new_ffn_down_v: float32 [3072, 768], P(('group', 'wide'))
- new_head: float32 [768, 768], P(('group', 'wide'))
- new_head_m: float32 [768, 768], P(('group', 'wide'))
- new_head_v: float32 [768, 768], P(('group', 'wide'))
- new_vectors: float32 [11520], P(('group', 'wide'))
- new_vectors_m: float32 [11520], P(('group', 'wide'))
- new_vectors_v: float32 [11520], P(('group', 'wide'))
The draws below stay inside these ranges and needn't reach their ends.
Inputs may be any that keep to these rules, and one draw needn't show every extreme that they name: `passage_len`: the first passage has all 512 slots live. `query_len`: the first query has all 32 slots live. At least one query of every aligned block of 4 queries is valid. `vectors`: gains lie near one, biases near zero.
All inputs are finite; a program needn't handle non-finite values.
Results may differ from the reference program's by a relative error of at most 0.02.
Values may be sent and summed in bfloat16 or wider, within the bound.
No kernel may reach another device: no remote copies, remote signals or barrier semaphores. Data moves between devices by JAX's collectives and lax.ppermute only.
A program may use at most 256 MiB of HBM per device.

```python
import math
import jax
import jax.numpy as jnp
import numpy as np
from jax import lax

D = 768
HEADS = 12
HEAD_DIM = 64
FF = 3072
VOCAB = 50432
PAS_LEN = 512
QRY_LEN = 32
QRY_DEV = 4
NNEG = 7
PASSAGES = 32
QUERIES = 128
NPARAM = 46411008


def draw_passage_len(key, part):
    drawn = jax.random.randint(key, (PASSAGES,), max(PAS_LEN // 4, 1), PAS_LEN + 1, dtype=jnp.int32)
    return drawn.at[0].set(PAS_LEN)


def draw_query_len(key, part):
    drawn = jax.random.randint(key, (QUERIES,), max(QRY_LEN // 4, 1), QRY_LEN + 1, dtype=jnp.int32)
    return drawn.at[0].set(QRY_LEN)


def draw_valid(key, part):
    position = jnp.arange(QUERIES, dtype=jnp.int32)
    drawn = jax.random.randint(key, (QUERIES,), 0, 2 * QUERIES, dtype=jnp.int32)
    flags = (drawn < QUERIES // 2 + position).astype(jnp.int32)
    return jnp.where(position % QRY_DEV == 0, 1, flags).astype(jnp.int32)


def draw_vectors(key, part):
    key_gain, key_bias = jax.random.split(key)
    gains = 1.0 + 0.15 * jax.random.truncated_normal(key_gain, -2.5, 2.5, (3 * D,), jnp.float32)
    biases = 0.2 * jax.random.truncated_normal(key_bias, -2.5, 2.5, (8 * D + FF,), jnp.float32)
    return jnp.concatenate([gains, biases]).astype(jnp.float32)


def touch_ends(values, stream_key, low, largest):
    longest = values.shape.index(max(values.shape))
    spots = []
    for shift in (0, 1):
        where = [jax.random.randint(jax.random.fold_in(stream_key, axis), (), 0, length) for axis, length in enumerate(values.shape)]
        where[longest] = (where[longest] + shift) % values.shape[longest]
        spots.append(tuple(where))
    return values.at[spots[0]].set(low).at[spots[1]].set(largest)


def block_levels(rng, shape, cuts, smallest, top_value):
    loudness = 1.0
    for dim, parts in cuts:
        draws = jax.random.uniform(jax.random.fold_in(jax.random.fold_in(rng, 6), dim), (parts,), jnp.float32, smallest / len(cuts), top_value / len(cuts))
        loudness = loudness * jnp.repeat(jnp.exp(draws), shape[dim] // parts).reshape((-1,) + (1,) * (len(shape) - 1 - dim))
    return loudness


def cumulative_ranks(count, skew):
    weights = [(1 << 20) // math.isqrt(rank ** skew) + 1 for rank in range(1, count + 1)]
    deviation = 1 + sum(weights) // (1 << 30)
    return np.cumsum(np.array([max(1, weight // deviation) for weight in weights]))


def ranked_ids(key, extent, amount, slope):
    table = cumulative_ranks(amount, slope)
    pick = jax.random.randint(jax.random.fold_in(key, 1), extent, 0, int(table[amount - 1]))
    standing = jnp.searchsorted(jnp.asarray(table, jnp.int32), pick, side="right")
    return jax.random.permutation(jax.random.fold_in(key, 2), amount)[standing].astype(jnp.int32)


def noise(stream_key, extent, scale, most, cuts=(), kind=jnp.bfloat16):
    level = block_levels(stream_key, extent, cuts, -0.22, 0.18) if cuts else 1.0
    entries = jax.random.normal(stream_key, extent, jnp.float32) * scale * level
    return jnp.minimum(jnp.maximum(entries, -most), most).astype(kind)


def setup_inputs(seed: int = 0) -> dict:
    key_list = jax.random.split(jax.random.key(seed), 30)
    passage_ids = touch_ends(ranked_ids(key_list[0], (PASSAGES, PAS_LEN), VOCAB, 2), jax.random.fold_in(key_list[0], 3), 0, VOCAB - 1).astype(jnp.int32)
    query_ids = touch_ends(ranked_ids(key_list[1], (QUERIES, QRY_LEN), VOCAB, 2), jax.random.fold_in(key_list[1], 3), 0, VOCAB - 1).astype(jnp.int32)
    passage_len = draw_passage_len(jax.random.fold_in(key_list[29], 71), 0)
    query_len = draw_query_len(jax.random.fold_in(key_list[29], 71), 0)
    positive = touch_ends(jax.random.randint(key_list[4], (QUERIES,), 0, PASSAGES), jax.random.fold_in(key_list[4], 1), 0, PASSAGES - 1).astype(jnp.int32)
    negatives = touch_ends(jax.random.randint(key_list[5], (QUERIES, NNEG), 0, PASSAGES), jax.random.fold_in(key_list[5], 1), 0, PASSAGES - 1).astype(jnp.int32)
    valid = draw_valid(jax.random.fold_in(key_list[29], 71), 0)
    step_count = jax.random.randint(key_list[7], (1,), 1, 21).astype(jnp.int32)
    embedding = noise(key_list[8], (D, VOCAB), 1.0, 6.0, ((0, 16), (1, 2)), jnp.float32)
    embedding_m = noise(key_list[9], (D, VOCAB), (0.111 * 0.0017 * NPARAM ** -0.5), 1.7881393432617188e-07, ((0, 16), (1, 2)), jnp.float32)
    embedding_v = jnp.clip(jnp.exp(math.log(2.490788261069548e-16) - 1.3862944 * jax.random.uniform(key_list[10], (D, VOCAB), jnp.float32) ** block_levels(key_list[10], (D, VOCAB), ((0, 16), (1, 2)), -0.2, 0.2)), 6.22697065267387e-17, 2.490788261069548e-16)
    attn_in = noise(key_list[11], (D, 3 * D), D ** -0.5, 0.21875, ((0, 32),), jnp.float32)
    attn_in_m = noise(key_list[12], (D, 3 * D), (0.111 * 0.02 * NPARAM ** -0.5), 1.9073486328125e-06, ((0, 32),), jnp.float32)
    attn_in_v = jnp.clip(jnp.exp(math.log(3.4474579766428926e-14) - 1.3862944 * jax.random.uniform(key_list[13], (D, 3 * D), jnp.float32) ** block_levels(key_list[13], (D, 3 * D), ((0, 32),), -0.2, 0.2)), 8.618644941607231e-15, 3.4474579766428926e-14)
    attn_out = noise(key_list[14], (D, D), (D // 16) ** -0.5, 0.875, ((0, 32),), jnp.float32)
    attn_out_m = noise(key_list[15], (D, D), (0.111 * 0.02 * NPARAM ** -0.5), 1.9073486328125e-06, ((0, 32),), jnp.float32)
    attn_out_v = jnp.clip(jnp.exp(math.log(3.4474579766428926e-14) - 1.3862944 * jax.random.uniform(key_list[16], (D, D), jnp.float32) ** block_levels(key_list[16], (D, D), ((0, 32),), -0.2, 0.2)), 8.618644941607231e-15, 3.4474579766428926e-14)
    ffn_up = noise(key_list[17], (D, FF), D ** -0.5, 0.21875, ((0, 32),), jnp.float32)
    ffn_up_m = noise(key_list[18], (D, FF), (0.111 * 0.02 * NPARAM ** -0.5), 1.9073486328125e-06, ((0, 32),), jnp.float32)
    ffn_up_v = jnp.clip(jnp.exp(math.log(3.4474579766428926e-14) - 1.3862944 * jax.random.uniform(key_list[19], (D, FF), jnp.float32) ** block_levels(key_list[19], (D, FF), ((0, 32),), -0.2, 0.2)), 8.618644941607231e-15, 3.4474579766428926e-14)
    ffn_down = noise(key_list[20], (FF, D), FF ** -0.5, 0.109375, ((0, 32),), jnp.float32)
    ffn_down_m = noise(key_list[21], (FF, D), (0.111 * 0.02 * NPARAM ** -0.5), 1.9073486328125e-06, ((0, 32),), jnp.float32)
    ffn_down_v = jnp.clip(jnp.exp(math.log(3.4474579766428926e-14) - 1.3862944 * jax.random.uniform(key_list[22], (FF, D), jnp.float32) ** block_levels(key_list[22], (FF, D), ((0, 32),), -0.2, 0.2)), 8.618644941607231e-15, 3.4474579766428926e-14)
    head = noise(key_list[23], (D, D), D ** -0.5, 0.21875, ((0, 32),), jnp.float32)
    head_m = noise(key_list[24], (D, D), (0.111 * 0.02 * NPARAM ** -0.5), 1.9073486328125e-06, ((0, 32),), jnp.float32)
    head_v = jnp.clip(jnp.exp(math.log(3.4474579766428926e-14) - 1.3862944 * jax.random.uniform(key_list[25], (D, D), jnp.float32) ** block_levels(key_list[25], (D, D), ((0, 32),), -0.2, 0.2)), 8.618644941607231e-15, 3.4474579766428926e-14)
    vectors = draw_vectors(jax.random.fold_in(key_list[29], 71), 0)
    vectors_m = noise(key_list[27], (11 * D + FF,), (0.111 * 0.08 * NPARAM ** -0.5), 7.62939453125e-06, ((0, 32),), jnp.float32)
    vectors_v = jnp.clip(jnp.exp(math.log(5.515932762628628e-13) - 1.3862944 * jax.random.uniform(key_list[28], (11 * D + FF,), jnp.float32) ** block_levels(key_list[28], (11 * D + FF,), ((0, 32),), -0.2, 0.2)), 1.378983190657157e-13, 5.515932762628628e-13)
    return {"passage_ids": passage_ids, "query_ids": query_ids, "passage_len": passage_len, "query_len": query_len, "positive": positive, "negatives": negatives, "valid": valid, "step_count": step_count, "embedding": embedding, "embedding_m": embedding_m, "embedding_v": embedding_v, "attn_in": attn_in, "attn_in_m": attn_in_m, "attn_in_v": attn_in_v, "attn_out": attn_out, "attn_out_m": attn_out_m, "attn_out_v": attn_out_v, "ffn_up": ffn_up, "ffn_up_m": ffn_up_m, "ffn_up_v": ffn_up_v, "ffn_down": ffn_down, "ffn_down_m": ffn_down_m, "ffn_down_v": ffn_down_v, "head": head, "head_m": head_m, "head_v": head_v, "vectors": vectors, "vectors_m": vectors_m, "vectors_v": vectors_v}


@jax.custom_vjp
def low(v):
    return lax.optimization_barrier(v.astype(jnp.bfloat16)).astype(jnp.float32)

@jax.custom_vjp
def low_back(v):
    return v

def low_keep(v):
    return (low(v), None)

def low_pass(kept, grad):
    return (grad,)

def back_keep(v):
    return (v, None)

def back_low(kept, grad):
    return (low(grad),)
low.defvjp(low_keep, low_pass)
low_back.defvjp(back_keep, back_low)
precise = lax.Precision.HIGHEST
clip_level = 0.02

def matmul(left, right):
    return jnp.dot(left, right, precision=precise, preferred_element_type=jnp.float32)

def layer_norm(resid, gain, shift):
    centred = resid - lax.optimization_barrier(jnp.mean(resid, -1, keepdims=True))
    spread = lax.optimization_barrier(jnp.mean(centred * centred, -1, keepdims=True))
    return centred * lax.rsqrt(spread + 1e-05) * gain + shift

def encode(token_ids, lengths, table, mats, vector):
    w_qkv, w_out, w_up, w_down, w_head = mats
    pieces = [vector[number * D:(number + 1) * D] for number in range(11)]
    gain_one, gain_two, gain_head, bias_query, bias_value, bias_out, shift_one, bias_down, shift_two, bias_head, shift_head = pieces
    bias_up = vector[11 * D:]
    seq_count, seq_len = token_ids.shape
    embedded = jnp.take(table, token_ids.reshape(-1), axis=1).T
    qkv_bias = jnp.concatenate([bias_query, jnp.zeros_like(bias_query), bias_value])
    qkv_proj = low_back(low(matmul(embedded, w_qkv) + qkv_bias))
    shaped = qkv_proj.reshape(seq_count, seq_len, 3, HEADS, HEAD_DIM)
    queries, keys_all, values_all = (shaped[:, :, 0], shaped[:, :, 1], shaped[:, :, 2])
    key_mask = jnp.arange(seq_len)[None, :] < lengths[:, None]
    scores = jnp.einsum('blhd,bmhd->bhlm', queries, keys_all, precision=precise) * HEAD_DIM ** (-0.5)
    scores = low_back(jnp.where(key_mask[:, None, None, :], scores, -1e+30))
    probs = low(jax.nn.softmax(scores, axis=-1))
    mixed = jnp.einsum('bhlm,bmhd->blhd', probs, values_all, precision=precise).reshape(seq_count * seq_len, D)
    mixed = low_back(low(mixed))
    attended = low_back(matmul(mixed, w_out) + bias_out)
    out_one = layer_norm(embedded + attended, gain_one, shift_one)
    hidden_pre = low_back(matmul(low(out_one), w_up) + bias_up)
    hidden = low(jax.nn.gelu(hidden_pre, approximate=False))
    ffn_out = low_back(matmul(hidden, w_down) + bias_down)
    out_two = layer_norm(out_one + ffn_out, gain_two, shift_two).reshape(seq_count, seq_len, D)
    pooled = out_two[:, 0]
    head_pre = low_back(matmul(low(pooled), w_head) + bias_head)
    return layer_norm(head_pre, gain_head, shift_head)

def adamw(weight, moment_one, moment_two, gradient, rate_value, step_float):
    first_new = 0.9 * moment_one + 0.1 * gradient
    second_new = 0.999 * moment_two + 0.001 * gradient * gradient
    first_hat = first_new / (1.0 - jnp.power(0.9, step_float))
    second_hat = second_new / (1.0 - jnp.power(0.999, step_float))
    weight_new = weight - rate_value * (first_hat / (jnp.sqrt(second_hat) + 1e-08) + 0.01 * weight)
    return (weight_new, first_new, second_new)

def reference(passage_ids, query_ids, passage_len, query_len, positive, negatives, valid, step_count, embedding, embedding_m, embedding_v, attn_in, attn_in_m, attn_in_v, attn_out, attn_out_m, attn_out_v, ffn_up, ffn_up_m, ffn_up_v, ffn_down, ffn_down_m, ffn_down_v, head, head_m, head_v, vectors, vectors_m, vectors_v):
    query_block = QRY_DEV * 8

    def forward(table, w_qkv, w_out, w_up, w_down, w_head, vector):
        table = low(table)
        mats = (low(w_qkv), low(w_out), low(w_up), low(w_down), low(w_head))
        vector = low(vector)

        def encode_block(blocks):
            return encode(blocks[0], blocks[1], table, mats, vector)
        checked = jax.checkpoint(encode_block)
        passage_vecs = lax.map(checked, (passage_ids.reshape(PASSAGES, 1, PAS_LEN), passage_len.reshape(PASSAGES, 1)))
        passage_vecs = low(passage_vecs.reshape(PASSAGES, D))
        query_vecs = lax.map(checked, (query_ids.reshape(QUERIES // query_block, query_block, QRY_LEN), query_len.reshape(QUERIES // query_block, query_block)))
        query_vecs = low(query_vecs.reshape(QUERIES, D))
        picks = jnp.concatenate([positive[:, None], negatives], 1)
        chosen = jnp.take(passage_vecs, picks, axis=0)
        scores = low_back(jnp.einsum('qd,qjd->qj', query_vecs, chosen, precision=precise) * D ** (-0.5))
        per_query = jax.nn.logsumexp(scores, axis=1) - scores[:, 0]
        valid_flags = valid.astype(jnp.float32)
        return jnp.sum(valid_flags * per_query) / jnp.sum(valid_flags)
    params = (embedding, attn_in, attn_out, ffn_up, ffn_down, head, vectors)
    loss, pullback = jax.vjp(forward, *params)
    grads = pullback(jnp.ones((), jnp.float32))
    squares = sum((jnp.sum(gradient * gradient) for gradient in grads))
    grad_norm = jnp.sqrt(squares)
    factor = jnp.minimum(1.0, clip_level / (grad_norm + 1e-06))
    rates = (0.5, 0.5 * D ** (-0.5), 0.5 * (D // 16) ** (-0.5), 0.5 * D ** (-0.5), 0.5 * FF ** (-0.5), 0.5 * D ** (-0.5), 0.2)
    firsts = (embedding_m, attn_in_m, attn_out_m, ffn_up_m, ffn_down_m, head_m, vectors_m)
    seconds = (embedding_v, attn_in_v, attn_out_v, ffn_up_v, ffn_down_v, head_v, vectors_v)
    step_float = step_count[0].astype(jnp.float32)
    result = [adamw(params[number], firsts[number], seconds[number], grads[number] * factor, rates[number], step_float) for number in range(7)]
    return (loss, grad_norm, result[0][0], result[0][1], result[0][2], result[1][0], result[1][1], result[1][2], result[2][0], result[2][1], result[2][2], result[3][0], result[3][1], result[3][2], result[4][0], result[4][1], result[4][2], result[5][0], result[5][1], result[5][2], result[6][0], result[6][1], result[6][2])
```

```python
from functools import partial

import jax
import jax.numpy as jnp
import numpy as np
from jax import lax
from jax.sharding import PartitionSpec as P

D = 768
HEADS = 12
HEAD_DIM = 64
FF = 3072
ROWS = 8
ALL = ("group", "wide")
clip_level = 0.02
f32 = jnp.float32
bf16 = jnp.bfloat16


def dot(a, b, ca=1, cb=0):
    return lax.dot_general(a, b, (((ca,), (cb,)), ((), ())), preferred_element_type=f32)


def split(x):
    high = x.astype(bf16)
    return high, (x - high.astype(f32)).astype(bf16)


def dot_split(x, w, cb=0):
    high, rest = split(x)
    return dot(high, w, 1, cb) + dot(rest, w, 1, cb)


def layer_norm(resid):
    centred = resid - jnp.mean(resid, -1, keepdims=True)
    inv_std = lax.rsqrt(jnp.mean(centred * centred, -1, keepdims=True) + 1e-05)
    return centred * inv_std, inv_std


def norm_back(grad_out, normed, inv_std, gain):
    scaled = grad_out * gain
    return inv_std * (
        scaled
        - jnp.mean(scaled, -1, keepdims=True)
        - normed * jnp.mean(scaled * normed, -1, keepdims=True)
    )


def head_tables(rows):
    count = -(-rows * HEADS // 16) * 16
    a = np.arange(count)
    live = a < rows * HEADS
    seq_of = np.where(live, a // HEADS, 99).astype(np.float32)[:, None]
    spread = ((seq_of == np.arange(ROWS)[None, :])).astype(np.float32)
    head_cols = ((np.arange(D)[None, :] // HEAD_DIM == a[:, None] % HEADS) & live[:, None]).astype(np.float32)
    by_head = ((np.arange(16)[:, None] == a[None, :] % HEADS) & live[None, :]).astype(np.float32)
    return seq_of, spread, head_cols, by_head


def partition(values, first):
    count = values.shape[1]
    left = lax.broadcasted_iota(jnp.int32, (count, count), 0)
    right = lax.broadcasted_iota(jnp.int32, (count, count), 1)
    first_row = jnp.broadcast_to(first, (ROWS, count)).astype(bf16)
    before = dot((right < left).astype(bf16), first_row, 1, 1)[:, :1]
    mine = dot((right == left).astype(bf16), first_row, 1, 1)[:, :1]
    total = jnp.sum(first, 1, keepdims=True)
    index = lax.broadcasted_iota(jnp.int32, (count, 1), 0).astype(f32)
    target = jnp.where(mine > 0.5, before, total + index - before)
    moves = (target.astype(jnp.int32) == right).astype(bf16)
    return dot(values.astype(bf16), moves), total


def attend(xt, w_q, w_k, w_v, w_o, vec, seq_id, live, slot0, seq_of, spread, head_cols):
    g1, bq, bv, bo, be1 = vec[0:1], vec[3:4], vec[4:5], vec[5:6], vec[6:7]
    rows = lax.broadcasted_iota(jnp.int32, (ROWS, xt.shape[1]), 0).astype(f32)
    pick0 = jnp.where((rows == seq_id) & (slot0 > 0.5), 1.0, 0.0).astype(bf16)
    x00 = dot(pick0, xt, 1, 1)
    q = (dot(x00.astype(bf16), w_q) + bq).astype(bf16)
    q_wide = (dot(spread.astype(bf16), q) * head_cols).astype(bf16)
    qk = dot(q_wide, w_k, 1, 1) * HEAD_DIM ** (-0.5)
    mask = (seq_of == seq_id) & (live > 0.5)
    scores = jnp.where(mask, dot_split(qk, xt), -1e30)
    raw = jnp.where(mask, jnp.exp(scores - jnp.max(scores, 1, keepdims=True)), 0.0)
    total = jnp.sum(raw, 1, keepdims=True)
    probs = raw / jnp.where(total > 0.0, total, 1.0)
    probs_low = probs.astype(bf16)
    y = dot(probs_low, xt, 1, 1)
    psum = jnp.sum(probs_low.astype(f32), 1, keepdims=True)
    mixed = dot_split(y, w_v) + psum * bv
    o = dot(spread.astype(bf16), (mixed * head_cols).astype(bf16), 0, 0).astype(bf16)
    normed, inv = layer_norm(x00 + dot(o, w_o) + bo)
    x1 = normed * g1 + be1
    return x00, q, qk, probs, y, psum, o, normed, inv, x1


def attend_back(dx1, normed, inv, probs, psum, xt, w_q, w_k, w_v, w_o, vec, spread, head_cols, by_head):
    g1, bv = vec[0:1], vec[4:5]
    d_res = norm_back(dx1, normed, inv, g1)
    d_a = d_res.astype(bf16)
    d_o = dot(d_a, w_o, 1, 1).astype(bf16)
    d_o_wide = dot(spread.astype(bf16), d_o) * head_cols
    vd = dot(d_o_wide.astype(bf16), w_v, 1, 1)
    dp = dot_split(vd, xt) + jnp.sum(d_o_wide * bv, 1, keepdims=True)
    ds = (probs * (dp - jnp.sum(probs * dp, 1, keepdims=True))).astype(bf16)
    z = dot(ds, xt, 1, 1)
    zw = dot_split(z, w_k) * (HEAD_DIM ** (-0.5)) * head_cols
    d_q = dot(spread.astype(bf16), zw.astype(bf16), 0, 0).astype(bf16)
    extra = d_res + dot(d_q, w_q, 1, 1)
    sums = jnp.concatenate(
        [
            jnp.sum(dx1 * normed, 0, keepdims=True),
            jnp.sum(dx1, 0, keepdims=True),
            jnp.sum(d_a.astype(f32), 0, keepdims=True),
            jnp.sum(d_q.astype(f32), 0, keepdims=True),
            jnp.sum(d_o_wide * psum, 0, keepdims=True),
        ],
        0,
    )
    ds_heads = dot(by_head.astype(bf16), ds)
    p_heads = dot(by_head.astype(bf16), probs.astype(bf16))
    return d_a, d_o, vd, z, d_q, extra, sums, ds_heads, p_heads


def ffn_up(x1, w_up, bias):
    u = dot(x1.astype(bf16), w_up) + bias
    return u, (0.5 * u * (1.0 + lax.erf(u * 0.5**0.5))).astype(bf16)


def middle(x1, f, u, h, w_up, w_down, w_head, vec, picks, valid):
    g2, gc, b2, be2, bc, bec = vec[1:2], vec[2:3], vec[7:8], vec[8:9], vec[9:10], vec[10:11]
    count = x1.shape[0]
    normed2, inv2 = layer_norm(x1 + (f + b2))
    pooled = (normed2 * g2 + be2).astype(bf16)
    normed_c, inv_c = layer_norm(dot(pooled, w_head) + bc)
    e = (normed_c * gc + bec).astype(bf16)
    scores = dot(e, e, 1, 1) * D ** (-0.5)
    col = lax.broadcasted_iota(jnp.int32, (count, count), 1)
    is_pos = jnp.where(col == picks[:, 0:1], 1.0, 0.0)
    negs = jnp.zeros_like(is_pos)
    for number in range(1, picks.shape[1]):
        negs = negs + jnp.where(col == picks[:, number : number + 1], 1.0, 0.0)
    taken = (is_pos + negs) > 0.0
    top = jnp.max(jnp.where(taken, scores, -1e30), 1, keepdims=True)
    raw = jnp.where(taken, jnp.exp(scores - top), 0.0)
    total = jnp.sum(raw * (is_pos + negs), 1, keepdims=True)
    total = jnp.where(total > 0.0, total, 1.0)
    share = raw / total
    valid_count = jnp.sum(valid, 0, keepdims=True)
    per_query = top + jnp.log(total) - jnp.sum(is_pos * scores, 1, keepdims=True)
    loss = jnp.sum(jnp.where(valid > 0.0, valid * per_query, 0.0), 0, keepdims=True) / valid_count
    weight = valid / valid_count
    d_pos = (weight * (share - 1.0)).astype(bf16).astype(f32)
    d_neg = (weight * share).astype(bf16).astype(f32)
    d_scores = d_pos * is_pos + d_neg * negs
    high, rest = split(d_scores)
    d_e = (dot(high, e) + dot(rest, e) + dot(high, e, 0, 0) + dot(rest, e, 0, 0)) * D ** (-0.5)
    d_c = norm_back(d_e, normed_c, inv_c, gc).astype(bf16)
    d_head = dot(pooled, d_c, 0, 0)
    d_x2 = dot(d_c, w_head, 1, 1)
    d_res2 = norm_back(d_x2, normed2, inv2, g2)
    d_f = d_res2.astype(bf16)
    d_down = dot(h, d_f, 0, 0)
    d_h = dot(d_f, w_down, 1, 1)
    slope = 0.5 * (1.0 + lax.erf(u * 0.5**0.5)) + u * jnp.exp(-0.5 * u * u) * (2.0 * np.pi) ** (-0.5)
    d_u = (d_h * slope).astype(bf16)
    d_up = dot(x1.astype(bf16), d_u, 0, 0)
    d_x1 = dot(d_u, w_up, 1, 1)
    sums = jnp.concatenate(
        [
            jnp.sum(d_x2 * normed2, 0, keepdims=True),
            jnp.sum(d_e * normed_c, 0, keepdims=True),
            jnp.sum(d_f.astype(f32), 0, keepdims=True),
            jnp.sum(d_x2, 0, keepdims=True),
            jnp.sum(d_c.astype(f32), 0, keepdims=True),
            jnp.sum(d_e, 0, keepdims=True),
        ],
        0,
    )
    return loss, d_head, d_down, d_up, d_res2, d_x1, sums, jnp.sum(d_u.astype(f32), 0, keepdims=True)


def adamw(weight, moment_one, moment_two, gradient, rate_value, step_float):
    first_new = 0.9 * moment_one + 0.1 * gradient
    second_new = 0.999 * moment_two + 0.001 * gradient * gradient
    first_hat = first_new / (1.0 - jnp.power(0.9, step_float))
    second_hat = second_new / (1.0 - jnp.power(0.999, step_float))
    weight_new = weight - rate_value * (first_hat / (jnp.sqrt(second_hat) + 1e-08) + 0.01 * weight)
    return (weight_new, first_new, second_new)


def swap(x):
    return lax.ppermute(x, "group", [(0, 1), (1, 0)])


def exchange(x):
    return lax.all_to_all(x, "wide", split_axis=0, concat_axis=0, tiled=True)


def gather_rows(x, wide):
    own = exchange(jnp.broadcast_to(x[None], (wide,) + x.shape))
    return jnp.concatenate([own, swap(own)], 0)


def in_order(pair, group):
    half = pair.shape[0] // 2
    return jnp.where(group == 0, pair, jnp.concatenate([pair[half:], pair[:half]], 0))


def sum_to_owner(parts, wide):
    half = wide * ROWS
    mine = parts[:half] + swap(parts[half:])
    got = exchange(mine.astype(bf16).reshape(wide, ROWS, -1))
    return jnp.sum(got.astype(f32), 0)


def body(wide, passage_ids, query_ids, passage_len, query_len, positive, negatives, valid, step_count, *state):
    params, firsts, seconds = state[0::3], state[1::3], state[2::3]
    embedding, attn_in, attn_out, w_ffn_up, w_ffn_down, head, vectors = params
    group = lax.axis_index("group")
    place = lax.axis_index("wide")
    device = group * wide + place
    devices = 2 * wide
    feats, half_rows = embedding.shape
    block = D // devices
    hidden = FF // devices
    pas_count, pas_len = passage_ids.shape
    qry_count, qry_len = query_ids.shape
    rows = pas_count + qry_count
    tokens = pas_count * pas_len + qry_count * qry_len
    seq_of, spread, head_cols, by_head = (jnp.asarray(t) for t in head_tables(rows))
    fan = seq_of.shape[0]

    ids = jnp.concatenate([passage_ids.reshape(1, -1), query_ids.reshape(1, -1)], 1)
    seq_np = np.concatenate([np.repeat(np.arange(pas_count), pas_len), pas_count + np.repeat(np.arange(qry_count), qry_len)])
    pos_np = np.concatenate([np.tile(np.arange(pas_len), pas_count), np.tile(np.arange(qry_len), qry_count)])
    lens = jnp.concatenate([jnp.repeat(passage_len, pas_len), jnp.repeat(query_len, qry_len)])
    values = jnp.concatenate(
        [
            (ids // 256).astype(f32),
            (ids % 256).astype(f32),
            jnp.asarray(seq_np, f32)[None],
            jnp.asarray(pos_np == 0, f32)[None],
            (jnp.asarray(pos_np) < lens).astype(f32)[None],
            jnp.zeros((3, tokens), f32),
        ],
        0,
    )
    moved, first_count = partition(values, (ids < half_rows).astype(f32))
    seq_id, slot0, live = moved[2:3], moved[3:4], moved[4:5]
    sent_ids = moved[0:1] * 256.0 + moved[1:2]
    sent_code = seq_id + 8.0 * slot0
    note = jnp.concatenate(
        [first_count.reshape(-1), valid.astype(f32), positive.astype(f32), negatives.astype(f32).reshape(-1)]
    )
    low_vectors = vectors.astype(bf16).astype(f32)
    lanes = 128
    pad = lambda v: jnp.pad(v, (0, -v.shape[0] % lanes)).reshape(-1, lanes)
    packet = jnp.concatenate([sent_ids.reshape(-1, lanes), sent_code.reshape(-1, lanes), pad(note), pad(low_vectors)], 0)
    packet = jnp.pad(packet, ((0, -packet.shape[0] % 8), (0, 0)))
    packets = gather_rows(packet, wide)
    id_rows = tokens // lanes
    all_ids = packets[:, :id_rows].reshape(devices, tokens).astype(jnp.int32)
    all_code = packets[:, id_rows : 2 * id_rows].reshape(devices, tokens).astype(jnp.int32)
    notes = packets[:, 2 * id_rows]
    vec_rows = -(-vectors.shape[0] // lanes)
    vec_all = packets[:, 2 * id_rows + 1 : 2 * id_rows + 1 + vec_rows].reshape(devices, -1)[:, : vectors.shape[0]]
    vec = in_order(vec_all, group).reshape(-1, D)
    valid_rows = jnp.pad(notes[:, 1 : 1 + qry_count], ((0, 0), (pas_count, ROWS - rows))).reshape(-1, 1)
    picked = jnp.concatenate(
        [notes[:, 1 + qry_count : 1 + 2 * qry_count, None], notes[:, 1 + 2 * qry_count : 1 + 2 * qry_count + qry_count * negatives.shape[1]].reshape(devices, qry_count, -1)],
        2,
    ).astype(jnp.int32)
    pick_dev = picked // pas_count
    pick_row = (((pick_dev // wide) ^ group) * wide + pick_dev % wide) * ROWS + picked % pas_count
    pick_rows = jnp.pad(pick_row, ((0, 0), (pas_count, ROWS - rows), (0, 0)), constant_values=-1).reshape(devices * ROWS, -1)

    low_mats = jnp.concatenate([attn_in, attn_out, head], 1).astype(bf16)
    mats = lax.all_gather(low_mats, ALL, axis=0, tiled=True)
    w_q, w_k, w_v, w_o, w_head = (mats[:, k * D : (k + 1) * D] for k in range(5))
    up_cols = lax.all_to_all(
        w_ffn_up.astype(bf16).reshape(block, devices, hidden).transpose(1, 0, 2), ALL, split_axis=0, concat_axis=0, tiled=True
    ).reshape(D, hidden)
    down_rows = w_ffn_down.astype(bf16)
    bias_up = lax.dynamic_slice(vec.reshape(-1), (11 * D + device * hidden,), (hidden,))[None]

    local = all_ids - group * half_rows
    inside = (local >= 0) & (local < half_rows)
    local = jnp.clip(local, 0, half_rows - 1)
    looked = jnp.where(inside.reshape(1, -1), jnp.take(embedding.astype(bf16), local.reshape(-1), axis=1), jnp.zeros((), bf16))
    looked = looked.reshape(feats, devices, tokens).transpose(1, 0, 2)
    xt = exchange(looked[:wide] + swap(looked[wide:])).reshape(D, tokens)

    x00, q, qk, probs, y, psum, o, normed1, inv1, x1 = attend(
        xt, w_q, w_k, w_v, w_o, vec, seq_id, live, slot0, seq_of, spread, head_cols
    )
    x1_all = gather_rows(x1, wide).reshape(devices * ROWS, D)
    u, h = ffn_up(x1_all, up_cols, bias_up)
    f_own = sum_to_owner(dot(h, down_rows), wide)
    f_all = gather_rows(f_own.astype(bf16), wide).reshape(devices * ROWS, D).astype(f32)
    loss, d_head, d_down, d_up_cols, d_res2, d_x1_part, sums_mid, sums_up = middle(
        x1_all, f_all, u, h, up_cols, down_rows, w_head, vec, pick_rows, valid_rows
    )
    d_x1 = lax.dynamic_slice(d_res2, (place * ROWS, 0), (ROWS, D)) + sum_to_owner(d_x1_part, wide)
    d_a, d_o, vd, z, d_q, extra, sums_att, ds_heads, p_heads = attend_back(
        d_x1, normed1, inv1, probs, psum, xt, w_q, w_k, w_v, w_o, vec, spread, head_cols, by_head
    )

    def to_features(t):
        return jnp.concatenate([exchange(t.T.astype(bf16).reshape(wide, feats, -1))], 0)

    def both(t):
        return jnp.concatenate([t, swap(t)], 0)

    def to_blocks(t):
        parts = t.T.astype(bf16).reshape(2, wide, block, -1).transpose(1, 0, 2, 3)
        got = both(exchange(parts.reshape(wide, 2 * block, -1))).reshape(devices, 2, block, -1)
        return lax.dynamic_index_in_dim(got, group, 1, keepdims=False)

    facts = lax.all_gather(jnp.concatenate([x00.astype(bf16), q, o, d_q, d_o, d_a], 0), ALL, axis=0, tiled=False)
    facts = facts.reshape(devices, 6, ROWS, D).transpose(1, 0, 2, 3).reshape(6, devices * ROWS, D)
    fact = lambda k: facts[k].reshape(devices, ROWS, HEADS, HEAD_DIM)[:, :rows]
    y_own = in_order(to_blocks(y), group)[:, :, : rows * HEADS].reshape(devices, block, rows, HEADS)
    z_own = in_order(to_blocks(z), group)[:, :, : rows * HEADS].reshape(devices, block, rows, HEADS)
    own_cols = lambda m: lax.dynamic_slice(m, (0, device * block), (devices * ROWS, block))
    d_wq = dot(own_cols(facts[0]), facts[3], 0, 0)
    d_wk = jnp.einsum("nfrh,nrhd->fhd", z_own, fact(1), preferred_element_type=f32).reshape(block, D) * HEAD_DIM ** (-0.5)
    d_wv = jnp.einsum("nfrh,nrhd->fhd", y_own, fact(4), preferred_element_type=f32).reshape(block, D)
    d_wo = dot(own_cols(facts[2]), facts[5], 0, 0)
    d_attn_in = jnp.concatenate([d_wq, d_wk, d_wv], 1)
    d_wup = lax.all_to_all(d_up_cols.astype(bf16).reshape(devices, block, hidden), ALL, split_axis=0, concat_axis=0, tiled=True)
    d_wup = d_wup.astype(f32).transpose(1, 0, 2).reshape(block, FF)
    d_whead = lax.dynamic_slice(d_head, (device * block, 0), (block, D))
    sent = jnp.concatenate([sums_att, jnp.pad(sums_up, ((0, 0), (0, D - hidden))), jnp.zeros((2, D), f32)], 0)
    sums_all = in_order(gather_rows(sent, wide), group)
    s_att = jnp.sum(sums_all[:, :5], 0)
    d_vec = jnp.concatenate(
        [
            s_att[0], sums_mid[0], sums_mid[1], s_att[3], s_att[4], s_att[2], s_att[1],
            sums_mid[2], sums_mid[3], sums_mid[4], sums_mid[5], sums_all[:, 5, :hidden].reshape(-1),
        ]
    )
    d_vec = lax.dynamic_slice(d_vec, (device * vectors.shape[0],), vectors.shape)

    qk_f, vd_f, ex_f = both(to_features(qk)), both(to_features(vd)), both(to_features(extra))
    ds_all, p_all = gather_rows(ds_heads.astype(bf16), wide), gather_rows(p_heads.astype(bf16), wide)
    seq_all = (all_code % 8).astype(f32)[:, None, :]
    here = (seq_of[None] == seq_all)
    wide_of = lambda c: jnp.where(here, jnp.einsum("ha,nht->nat", by_head.astype(bf16), c, preferred_element_type=f32), 0.0).astype(bf16)
    first = ((lax.broadcasted_iota(jnp.int32, (1, ROWS, 1), 1).astype(f32) == seq_all) & (all_code[:, None, :] >= 8)).astype(bf16)
    coef = jnp.concatenate([wide_of(ds_all), wide_of(p_all), first], 1)
    basis = jnp.concatenate([qk_f, vd_f, ex_f], 2)
    d_tok = jnp.einsum("nfa,nat->fnt", basis, coef, preferred_element_type=f32).reshape(feats, -1)
    d_tok = jnp.where(inside.reshape(1, -1), d_tok, 0.0)
    d_table = jnp.zeros((feats, half_rows), f32).at[:, local.reshape(-1)].add(d_tok)

    grads = (d_table, d_attn_in, d_wo, d_wup, d_down, d_whead, d_vec)
    squares = sum(jnp.sum(g * g) for g in grads)
    grad_norm = jnp.sqrt(jnp.sum(gather_rows(jnp.full((8, 128), squares), wide)[:, 0, 0]))
    factor = jnp.minimum(1.0, clip_level / (grad_norm + 1e-06))
    rates = (0.5, 0.5 * D**-0.5, 0.5 * (D // 16) ** -0.5, 0.5 * D**-0.5, 0.5 * FF**-0.5, 0.5 * D**-0.5, 0.2)
    step_float = step_count[0].astype(f32)
    result = [adamw(params[k], firsts[k], seconds[k], grads[k] * factor, rates[k], step_float) for k in range(7)]
    return (loss[0, 0], grad_norm) + tuple(t for r in result for t in r)


def solution(mesh):
    split_rows = P(ALL, None)
    flat = P(ALL)
    table = P("wide", "group")
    mats = (table,) * 3 + (split_rows,) * 15 + (flat,) * 3
    in_specs = (split_rows, split_rows, flat, flat, flat, split_rows, flat, P()) + mats
    return jax.shard_map(
        partial(body, mesh.shape["wide"]), mesh=mesh, in_specs=in_specs, out_specs=(P(), P()) + mats, check_vma=False
    )
```

```python
from functools import partial

import jax
import jax.numpy as jnp
import numpy as np
from jax import lax
from jax.experimental import pallas as pl
from jax.experimental.pallas import tpu as pltpu
from jax.sharding import PartitionSpec as P

D = 768
HEADS = 12
HEAD_DIM = 64
FF = 3072
ROWS = 8
LANES = 128
SIDE = 64
Z_AT = 68
KEEP = 24
ALL = ("group", "wide")
clip_level = 0.02
f32 = jnp.float32
bf16 = jnp.bfloat16
RATES = (0.5, 0.5 * D**-0.5, 0.5 * (D // 16) ** -0.5, 0.5 * D**-0.5, 0.5 * FF**-0.5, 0.5 * D**-0.5, 0.2)


def dot(a, b, ca=1, cb=0):
    return lax.dot_general(a, b, (((ca,), (cb,)), ((), ())), preferred_element_type=f32)


def split(x):
    high = x.astype(bf16)
    return high, (x - high.astype(f32)).astype(bf16)


def dot_split(x, w, cb=0):
    high, rest = split(x)
    return dot(high, w, 1, cb) + dot(rest, w, 1, cb)


def iota(shape, dim):
    return lax.broadcasted_iota(jnp.int32, shape, dim)


def stack_rows(rows):
    index = iota((ROWS, rows[0].shape[1]), 0)
    total = jnp.zeros(index.shape, f32)
    for number, row in enumerate(rows):
        total = jnp.where(index == number, row, total)
    return total


def layer_norm(resid):
    centred = resid - jnp.mean(resid, -1, keepdims=True)
    inv_std = lax.rsqrt(jnp.mean(centred * centred, -1, keepdims=True) + 1e-05)
    return centred * inv_std, inv_std


def norm_back(grad_out, normed, inv_std, gain):
    scaled = grad_out * gain
    return inv_std * (
        scaled
        - jnp.mean(scaled, -1, keepdims=True)
        - normed * jnp.mean(scaled * normed, -1, keepdims=True)
    )


def flag(condition):
    return jnp.where(condition, 1.0, 0.0)


def sequence_of(a, rows):
    assert HEADS == 12
    return jnp.where((a >= 0) & (a < rows * HEADS), lax.shift_right_logical(a * 43, 9), 99)


def head_of(a, rows):
    return a - HEADS * sequence_of(a, rows)


def spread_table(rows):
    return flag(sequence_of(iota((SIDE, ROWS), 0), rows) == iota((SIDE, ROWS), 1)).astype(bf16)


def column_table(rows):
    return flag(head_of(iota((SIDE, D), 0), rows) == lax.shift_right_logical(iota((SIDE, D), 1), 6))


def heads_table(rows):
    return flag(head_of(iota((16, SIDE), 1), rows) == iota((16, SIDE), 0)).astype(bf16)


def place_table(rows, first, count=None):
    count = rows * HEADS if count is None else count
    size = SIDE if count > ROWS else ROWS
    a = iota((LANES, size), 1)
    return flag((iota((LANES, size), 0) == first + a) & (a < count)).astype(bf16)


def expand_table(rows, first, r):
    return flag(iota((LANES, D), 0) == first + r * HEADS + lax.shift_right_logical(iota((LANES, D), 1), 6)).astype(bf16)


def prepare(ids, lens, seq, pos, group_rows):
    count = ids.shape[1]
    live = flag(pos < lens)
    first = jnp.where(ids < group_rows, 1.0, 0.0)
    high = lax.shift_right_logical(ids, 8)
    index = iota((ROWS, count), 0)
    values = jnp.zeros((ROWS, count), f32)
    pieces = (high.astype(f32), (ids - high * 256).astype(f32), seq.astype(f32), jnp.where(pos == 0, 1.0, 0.0), live)
    for number, row in enumerate(pieces):
        values = jnp.where(index == number, row, values)
    left, right = iota((count, count), 0), iota((count, count), 1)
    ahead = jnp.where(right < left, 1.0, 0.0).astype(bf16)
    same = jnp.where(right == left, 1.0, 0.0).astype(bf16)
    marks = jnp.broadcast_to(first, (ROWS, count)).astype(bf16)
    before = dot(ahead, marks, 1, 1)[:, :1]
    mine = dot(same, marks, 1, 1)[:, :1]
    total = jnp.sum(first, 1, keepdims=True)
    target = jnp.where(mine > 0.5, before, total + iota((count, 1), 0).astype(f32) - before)
    moves = jnp.where(target.astype(jnp.int32) == right, 1.0, 0.0).astype(bf16)
    return dot(values.astype(bf16), moves), total


def attend(xt, w, vec, moved, rows):
    g1, bq, bv, bo, be1 = vec[0:1], vec[3:4], vec[4:5], vec[5:6], vec[6:7]
    seq_id, slot0, live = moved[2:3], moved[3:4], moved[4:5]
    spread, columns = spread_table(rows), column_table(rows)
    index = iota((ROWS, xt.shape[1]), 0).astype(f32)
    pick0 = flag((index == seq_id) & (slot0 > 0.5)).astype(bf16)
    x00 = dot(pick0, xt, 1, 1)
    q = (dot(x00.astype(bf16), w(0)) + bq).astype(bf16)
    q_wide = (dot(spread, q) * columns).astype(bf16)
    qk = dot(q_wide, w(1), 1, 1) * HEAD_DIM ** (-0.5)
    mask = (sequence_of(iota((SIDE, 1), 0), rows).astype(f32) == seq_id) & (live > 0.5)
    scores = jnp.where(mask, dot_split(qk, xt), -1e30)
    raw = jnp.where(mask, jnp.exp(scores - jnp.max(scores, 1, keepdims=True)), 0.0)
    total = jnp.sum(raw, 1, keepdims=True)
    probs = raw / jnp.where(total > 0.0, total, 1.0)
    probs_low = probs.astype(bf16)
    y = dot(probs_low, xt, 1, 1)
    psum = jnp.sum(probs_low.astype(f32), 1, keepdims=True)
    mixed = dot_split(y, w(2)) + psum * bv
    o = dot(spread, (mixed * columns).astype(bf16), 0, 0).astype(bf16)
    normed, inv = layer_norm(x00 + dot(o, w(3)) + bo)
    p_heads = dot(heads_table(rows), probs_low).astype(bf16)
    return normed * g1 + be1, x00.astype(bf16), q, o, probs, psum, normed, inv, qk, y, p_heads


def attend_back(dx1, normed, inv, probs, psum, xt, w, vec, rows):
    g1, bv = vec[0:1], vec[4:5]
    spread, columns = spread_table(rows), column_table(rows)
    d_res = norm_back(dx1, normed, inv, g1)
    d_a = d_res.astype(bf16)
    d_o = dot(d_a, w(3), 1, 1).astype(bf16)
    d_o_wide = dot(spread, d_o) * columns
    vd = dot(d_o_wide.astype(bf16), w(2), 1, 1)
    dp = dot_split(vd, xt) + jnp.sum(d_o_wide * bv, 1, keepdims=True)
    ds = (probs * (dp - jnp.sum(probs * dp, 1, keepdims=True))).astype(bf16)
    z = dot(ds, xt, 1, 1)
    zw = dot_split(z, w(1)) * (HEAD_DIM ** (-0.5)) * columns
    d_q = dot(spread, zw.astype(bf16), 0, 0).astype(bf16)
    extra = d_res + dot(d_q, w(0), 1, 1)
    sums = [
        jnp.sum(dx1 * normed, 0, keepdims=True),
        jnp.sum(dx1, 0, keepdims=True),
        jnp.sum(d_a.astype(f32), 0, keepdims=True),
        jnp.sum(d_q.astype(f32), 0, keepdims=True),
        jnp.sum(d_o_wide * psum, 0, keepdims=True),
    ]
    return d_a, d_o, d_q, sums, vd, z, extra, dot(heads_table(rows), ds).astype(bf16)


def late_parts(vd, z, extra, rows):
    by_table = dot(place_table(rows, 0), vd.astype(bf16)) + dot(place_table(rows, rows * HEADS, rows), extra.astype(bf16))
    return by_table.T, dot(place_table(rows, Z_AT), z.astype(bf16)).T


def early_parts(qk, y, rows):
    return dot(place_table(rows, 0), qk).T, dot(place_table(rows, SIDE), y).T


def block_of(parts, dest, wide):
    by_table, by_rows = parts
    block = D // (2 * wide)
    return by_table[2 * block * dest : 2 * block * (dest + 1)] + jnp.concatenate(
        [by_rows[block * dest : block * (dest + 1)], by_rows[block * (wide + dest) : block * (wide + dest + 1)]], 0
    )


def in_chunks(heads):
    return jnp.concatenate([heads[:, k : k + LANES] for k in range(0, heads.shape[1], LANES)], 0)


def to_tiles(value):
    return jnp.concatenate([value[:, k : k + LANES] for k in range(0, value.shape[1], LANES)], 0)


def from_tiles(got, first, lines=ROWS):
    pieces = [got[:, first + k * lines : first + (k + 1) * lines, :] for k in range(D // LANES)]
    return jnp.concatenate([p.reshape(-1, LANES) for p in pieces], 1)


def ffn(x1, w_up, w_down, bias):
    u = dot(x1.astype(bf16), w_up) + bias
    h = (0.5 * u * (1.0 + lax.erf(u * 0.5**0.5))).astype(bf16)
    return u, h, dot(h, w_down)


def middle(x1, f, u, w_up, w_down, w, vec, picks, valid):
    g2, gc, b2, be2, bc, bec = vec[1:2], vec[2:3], vec[7:8], vec[8:9], vec[9:10], vec[10:11]
    count = x1.shape[0]
    normed2, inv2 = layer_norm(x1 + (f + b2))
    pooled = (normed2 * g2 + be2).astype(bf16)
    normed_c, inv_c = layer_norm(dot(pooled, w(4)) + bc)
    e = (normed_c * gc + bec).astype(bf16)
    scores = dot(e, e, 1, 1) * D ** (-0.5)
    col = iota((count, count), 1)
    is_pos = jnp.where(col == picks[:, 0:1], 1.0, 0.0)
    negs = jnp.zeros_like(is_pos)
    for number in range(1, picks.shape[1]):
        negs = negs + jnp.where(col == picks[:, number : number + 1], 1.0, 0.0)
    taken = (is_pos + negs) > 0.0
    top = jnp.max(jnp.where(taken, scores, -1e30), 1, keepdims=True)
    raw = jnp.where(taken, jnp.exp(scores - top), 0.0)
    total = jnp.sum(raw * (is_pos + negs), 1, keepdims=True)
    total = jnp.where(total > 0.0, total, 1.0)
    share = raw / total
    valid_count = jnp.sum(valid, 0, keepdims=True)
    per_query = top + jnp.log(total) - jnp.sum(is_pos * scores, 1, keepdims=True)
    loss = jnp.sum(jnp.where(valid > 0.0, valid * per_query, 0.0), 0, keepdims=True) / valid_count
    weight = valid / valid_count
    d_pos = (weight * (share - 1.0)).astype(bf16).astype(f32)
    d_neg = (weight * share).astype(bf16).astype(f32)
    d_scores = d_pos * is_pos + d_neg * negs
    high, rest = split(d_scores)
    d_e = (dot(high, e) + dot(rest, e) + dot(high, e, 0, 0) + dot(rest, e, 0, 0)) * D ** (-0.5)
    d_c = norm_back(d_e, normed_c, inv_c, gc).astype(bf16)
    d_x2 = dot(d_c, w(4), 1, 1)
    d_res2 = norm_back(d_x2, normed2, inv2, g2)
    d_f = d_res2.astype(bf16)
    d_h = dot(d_f, w_down, 1, 1)
    slope = 0.5 * (1.0 + lax.erf(u * 0.5**0.5)) + u * jnp.exp(-0.5 * u * u) * (2.0 * np.pi) ** (-0.5)
    d_u = (d_h * slope).astype(bf16)
    d_x1 = dot(d_u, w_up, 1, 1)
    sums = [
        jnp.sum(d_x2 * normed2, 0, keepdims=True),
        jnp.sum(d_e * normed_c, 0, keepdims=True),
        jnp.sum(d_f.astype(f32), 0, keepdims=True),
        jnp.sum(d_x2, 0, keepdims=True),
        jnp.sum(d_c.astype(f32), 0, keepdims=True),
        jnp.sum(d_e, 0, keepdims=True),
    ]
    return loss, pooled, d_c, d_res2, d_f, d_u, d_x1, sums


def update(weight, first, second, gradient, rate, scale_one, scale_two):
    first_new = 0.9 * first + 0.1 * gradient
    second_new = 0.999 * second + 0.001 * gradient * gradient
    first_hat = first_new * scale_one
    second_hat = second_new * scale_two
    return weight - rate * (first_hat / (jnp.sqrt(second_hat) + 1e-08) + 0.01 * weight), first_new, second_new


def shape(dims, kind=f32):
    return jax.ShapeDtypeStruct(dims, kind)


MIB = 1 << 20


def full_block(dims):
    return pl.BlockSpec(dims, lambda i: (0,) * len(dims), pipeline_mode=pl.Buffered(1))


def pinned(x):
    return pltpu.with_memory_space_constraint(x, pltpu.HBM)


def call(kernel, outs, *args, scalars=(), far=(), far_outs=(), after=(), near=(), near_outs=(), scratch=(), vmem=24, name=None, flops=0):
    anywhere = pl.BlockSpec(memory_space=pl.ANY)
    in_specs = [pl.BlockSpec(memory_space=pltpu.SMEM)] * len(scalars) + [anywhere] * len(far)
    in_specs += [full_block(a.shape) for a in args] + [anywhere] * len(after)
    moved = sum(int(np.prod(a.shape)) * a.dtype.itemsize for a in list(args) + list(far) + list(outs) + list(far_outs))
    used = len(scalars) + len(far) + len(args)

    def run(*refs):
        kernel(*refs[:used], *refs[used + len(after) :])

    shapes = [o if k in near_outs else pltpu.HBM(o.shape, o.dtype) for k, o in enumerate(outs)]
    shapes += [pltpu.HBM(o.shape, o.dtype) for o in far_outs]
    args = [a if k in near else pinned(a) for k, a in enumerate(args)]
    return pl.pallas_call(
        run,
        grid=(1,),
        out_shape=shapes,
        in_specs=in_specs,
        out_specs=[full_block(o.shape) for o in outs] + [anywhere] * len(far_outs),
        scratch_shapes=list(scratch),
        compiler_params=pltpu.CompilerParams(vmem_limit_bytes=vmem * MIB),
        cost_estimate=pl.CostEstimate(flops=int(flops), bytes_accessed=moved, transcendentals=0),
        name=name,
    )(*scalars, *(pinned(a) for a in far), *args, *after)


def square_weights(mats, first, buffers, signals, order):
    copies = {
        k: pltpu.make_async_copy(mats.at[:, pl.ds(k * D, D)], buffers.at[k - first], signals.at[k - first]) for k in order
    }
    for k in order:
        copies[k].start()
    ready = {}

    def get(k):
        if k not in ready:
            copies[k].wait()
            ready[k] = buffers[k - first]
        return ready[k]

    return get


def weight_scratch(count):
    return [pltpu.VMEM((count, D, D), bf16), pltpu.SemaphoreType.DMA((count,))]


def prepare_kernel(group_rows, count, base, seq, pos, packet, moved):
    chunks = count // LANES
    line = lambda first: jnp.concatenate([base[first + k : first + k + 1, :] for k in range(chunks)], 1).astype(jnp.int32)
    got, total = prepare(line(0), line(chunks), seq[...], pos[...], group_rows)
    moved[...] = got
    sent, code = got[0:1] * 256.0 + got[1:2], got[2:3] + 8.0 * got[3:4]
    lines = [sent[:, k * LANES : (k + 1) * LANES] for k in range(chunks)]
    lines += [code[:, k * LANES : (k + 1) * LANES] for k in range(chunks)]
    whole = base[...]
    index = iota(whole.shape, 0)
    for number, value in enumerate(lines):
        whole = jnp.where(index == number, value, whole)
    whole = jnp.where((index == 2 * chunks) & (iota(whole.shape, 1) == 0), total, whole)
    whole = jnp.where(index > 2 * chunks, whole.astype(bf16).astype(f32), whole)
    for dest in range(packet.shape[0]):
        packet[dest] = whole


def cast_kernel(attn_in, attn_out, head, out):
    out[:, : 3 * D] = attn_in[...].astype(bf16)
    out[:, 3 * D : 4 * D] = attn_out[...].astype(bf16)
    out[:, 4 * D :] = head[...].astype(bf16)


def build_kernel(emb, table):
    feats, vocab = emb.shape
    half = table.shape[0]
    blocks, second = half // LANES, (vocab - half) // LANES
    gap = jnp.zeros((SIDE - feats, LANES), f32)

    def build(b, both):
        start = pl.multiple_of(b * LANES, LANES)
        low = emb[:, pl.ds(start, LANES)]
        high = jnp.zeros_like(low)
        if both:
            high = emb[:, pl.ds(pl.multiple_of(half + start, LANES), LANES)]
        table[pl.ds(start, LANES), :] = jnp.concatenate([low, gap, high, gap], 0).astype(bf16).T.astype(f32)

    unroll = 7

    def step(i, carry):
        for k in range(unroll):
            build(i * unroll + k, True)
        return carry

    lax.fori_loop(0, second // unroll, step, 0)
    for b in range(second // unroll * unroll, blocks):
        build(jnp.int32(b), b < second)


def side_of(ids, group, half_rows, half):
    local = ids - (group * half_rows).astype(f32)
    inside = (local >= 0.0) & (local < float(half_rows))
    return jnp.where(inside, jnp.where(local >= float(half), 2.0, 1.0), 0.0)


def own_span(first, group, count):
    return jnp.where(group == 0, 0, first), jnp.where(group == 0, first, count)


def lookup_kernel(half_rows, per, unroll, add, where, numbers, firsts, packet, table, *refs):
    out, buf = refs[-2:]
    feats, count = out.shape[1:]
    group = where[0]
    chunks = count // LANES
    half = table.shape[0]
    eye = jnp.where(iota((LANES, LANES), 0) == iota((LANES, LANES), 1), 1.0, 0.0).astype(bf16)
    at = pl.program_id(0) * per
    for s in range(per):
        low, high = own_span(firsts[at + s], group, count)
        base = (at + s) * count

        def step(i, carry):
            for k in range(unroll):
                t = i * unroll + k
                buf[pl.ds(s * count + t, 1), :] = table[pl.ds(numbers[base + t], 1), :]
            return carry

        lax.fori_loop(low // unroll, (high + unroll - 1) // unroll, step, 0)
    for s in range(per):
        side = side_of(lanes_of(packet, s, 0, chunks), group, half_rows, half)
        turned = dot(eye, buf[s * count : (s + 1) * count, :].astype(bf16), 1, 1)
        pick = jnp.where(side > 1.5, turned[SIDE : SIDE + feats], turned[:feats])
        value = jnp.where(side > 0.5, pick, 0.0)
        if add:
            value = value + refs[0][s].astype(f32)
        out[s] = value.astype(bf16)


def lanes_of(packet, s, first, chunks):
    return jnp.concatenate([packet[s, first + c : first + c + 1, :] for c in range(chunks)], 1)


def lookup(where, numbers, firsts, packets, table, half_rows, feats, count, add=None, per=4, unroll=32):
    sources = packets.shape[0]
    some = lambda dims: pl.BlockSpec((per,) + dims, lambda i, *s: (i, 0, 0))
    extra = [] if add is None else [add]
    return pl.pallas_call(
        partial(lookup_kernel, half_rows, per, unroll, add is not None),
        out_shape=shape((sources, feats, count), bf16),
        grid_spec=pltpu.PrefetchScalarGridSpec(
            num_scalar_prefetch=3,
            grid=(sources // per,),
            in_specs=[some(packets.shape[1:]), pl.BlockSpec(table.shape, lambda i, *s: (0, 0), pipeline_mode=pl.Buffered(1))] + [some((feats, count)) for _ in extra],
            out_specs=some((feats, count)),
            scratch_shapes=[pltpu.VMEM((per * count, LANES), f32)],
        ),
        compiler_params=pltpu.CompilerParams(vmem_limit_bytes=16 * MIB),
        cost_estimate=pl.CostEstimate(flops=10**9, bytes_accessed=10**7, transcendentals=0),
        name="lookup" if add is None else "lookup_add",
    )(where, numbers, firsts, packets, pinned(table), *extra)


def spread_kernel(rows, half_rows, feats, per, unroll, copies, at_early, at_heads, where, numbers, firsts, packet, early_own, early_other, late_own, late_other, p_own, p_other, out, square, *scratch):
    parts, buf = scratch[:copies], scratch[copies]
    group = where[0]
    chunks = buf.shape[0] // (per * LANES)
    count = chunks * LANES
    half = parts[0].shape[0]
    vocab = out.shape[1]
    blocks = half // LANES
    step_at = pl.program_id(0)

    @pl.when(step_at == 0)
    def _():
        def clear(i, carry):
            for part in parts:
                part[pl.ds(pl.multiple_of(i * LANES, LANES), LANES), :] = jnp.zeros((LANES, LANES), f32)
            return carry

        lax.fori_loop(0, blocks, clear, 0)

    eye = jnp.where(iota((LANES, LANES), 0) == iota((LANES, LANES), 1), 1.0, 0.0).astype(bf16)
    gap = jnp.zeros((SIDE - feats, count), f32)
    lane = iota((LANES, 16), 0)
    low_heads = flag(head_of(lane, rows) == iota((LANES, 16), 1)).astype(bf16)
    lane = iota((LANES, 1), 0)
    seq_low = sequence_of(lane, rows).astype(f32)
    seq_extra = jnp.where((lane >= rows * HEADS) & (lane < rows * HEADS + rows), lane - rows * HEADS, 99).astype(f32)

    is_own = step_at < pl.num_programs(0) // 2

    def early(s, first, lines):
        return jnp.where(is_own, early_own[s, first : first + lines, :], early_other[s, first : first + lines, :])

    def late(s, first, lines):
        return jnp.where(is_own, late_own[s, first : first + lines, :], late_other[s, first : first + lines, :])

    def heads(s, first, lines):
        return jnp.where(is_own, p_own[s, first : first + lines, :], p_other[s, first : first + lines, :])

    def side_by_side(lines):
        return jnp.concatenate([lines[16 * c : 16 * (c + 1)] for c in range(chunks)], 1)

    for s in range(per):
        code = lanes_of(packet, s, chunks, chunks)
        slot0 = code >= 8.0
        seq = jnp.where(slot0, code - 8.0, code)
        here = seq_low == seq
        score_part = jnp.where(here, dot(low_heads, side_by_side(late(s, feats, 16 * chunks))), 0.0)
        value_part = jnp.where(here, dot(low_heads, side_by_side(heads(s, at_heads, 16 * chunks))), 0.0)
        value_part = jnp.where((seq_extra == seq) & slot0, 1.0, value_part)
        basis = jnp.concatenate([early(s, at_early, feats), late(s, 0, feats)], 1)
        x = dot(basis, jnp.concatenate([score_part, value_part], 0).astype(bf16))
        side = side_of(lanes_of(packet, s, 0, chunks), group, half_rows, half)
        tall = jnp.concatenate([jnp.where(side == 1.0, x, 0.0), gap, jnp.where(side == 2.0, x, 0.0), gap], 0).astype(bf16)
        for c in range(chunks):
            start = s * count + c * LANES
            buf[start : start + LANES, :] = dot(eye, tall[:, c * LANES : (c + 1) * LANES], 1, 1)
    for s in range(per):
        low, high = own_span(firsts[step_at * per + s], group, count)
        base = (step_at * per + s) * count

        def step(i, carry):
            for k in range(unroll):
                t = i * unroll + k
                part = parts[k % copies]
                row = numbers[base + t]
                part[pl.ds(row, 1), :] = part[pl.ds(row, 1), :] + buf[pl.ds(s * count + t, 1), :]
            return carry

        lax.fori_loop(low // unroll, (high + unroll - 1) // unroll, step, 0)

    @pl.when(step_at == pl.num_programs(0) - 1)
    def _():
        def emit(b, total, both):
            start = pl.multiple_of(b * LANES, LANES)
            lines = parts[0][pl.ds(start, LANES), :]
            for part in parts[1:]:
                lines = lines + part[pl.ds(start, LANES), :]
            turned = lines.T
            out[:, pl.ds(start, LANES)] = turned[:feats]
            if both:
                out[:, pl.ds(pl.multiple_of(half + start, LANES), LANES)] = turned[SIDE : SIDE + feats]
            return total + lines * lines

        second = (vocab - half) // LANES
        total = lax.fori_loop(0, second, lambda b, t: emit(b, t, True), jnp.zeros((LANES, LANES), f32))
        for b in range(second, blocks):
            total = emit(jnp.int32(b), total, False)
        square[...] = jnp.sum(total.reshape(LANES // ROWS, ROWS, LANES), 0)


def spread_tokens(where, numbers, firsts, packets, early, late, p_heads, at_early, rows, half_rows, feats, count, per=8, unroll=32, copies=4):
    devices = packets.shape[0]
    block = packets.shape[1:]
    half = -(-half_rows // (2 * LANES)) * LANES
    some = lambda dims: pl.BlockSpec((per,) + dims, lambda i, *s: (i, 0, 0))
    steps = devices // per
    mine = lambda pair: pl.BlockSpec((per,) + pair[0].shape[1:], lambda i, *s: (jnp.minimum(i, steps // 2 - 1), 0, 0))
    theirs = lambda pair: pl.BlockSpec((per,) + pair[0].shape[1:], lambda i, *s: (jnp.maximum(i - steps // 2, 0), 0, 0))
    return pl.pallas_call(
        partial(spread_kernel, rows, half_rows, feats, per, unroll, copies, at_early, at_early),
        out_shape=[pltpu.HBM((feats, half_rows), f32), pltpu.HBM((ROWS, LANES), f32)],
        grid_spec=pltpu.PrefetchScalarGridSpec(
            num_scalar_prefetch=3,
            grid=(steps,),
            in_specs=[some(block), mine(early), theirs(early), mine(late), theirs(late), mine(p_heads), theirs(p_heads)],
            out_specs=[pl.BlockSpec((feats, half_rows), lambda i, *s: (0, 0), pipeline_mode=pl.Buffered(1)), pl.BlockSpec((ROWS, LANES), lambda i, *s: (0, 0))],
            scratch_shapes=[pltpu.VMEM((half, LANES), f32)] * copies + [pltpu.VMEM((per * count, LANES), f32)],
        ),
        compiler_params=pltpu.CompilerParams(vmem_limit_bytes=44 * MIB),
        cost_estimate=pl.CostEstimate(flops=10**9, bytes_accessed=3 * 10**7, transcendentals=0),
        name="spread_tokens",
    )(where, numbers, firsts, packets, *early, *late, *p_heads)


def attend_kernel(rows, mats, xt, vec, moved, sent, heads_out, facts, probs_out, psum_out, normed_out, inv_out, *scratch):
    w = square_weights(mats, 0, *scratch, (0, 1, 2, 3))
    x1, x00, q, o, probs, psum, normed, inv, qk, y, p_heads = attend(xt[...], w, vec[...], moved[...], rows)
    tiles = to_tiles(x1)
    parts = early_parts(qk.astype(bf16), y.astype(bf16), rows)
    for dest in range(sent.shape[0]):
        sent[dest] = jnp.concatenate([tiles, block_of(parts, dest, sent.shape[0])], 0).astype(bf16)
    heads_out[...] = in_chunks(p_heads)
    facts[...] = jnp.concatenate([to_tiles(value.astype(f32)) for value in (x00, q, o)], 0).astype(bf16)
    probs_out[...], psum_out[...], normed_out[...], inv_out[...] = probs, psum, normed, inv


def attend_back_kernel(rows, place, mats, got, d_res2, sums_up, normed, inv, probs, psum, xt, vec, late_out, last, *scratch):
    w = square_weights(mats, 0, *scratch, (3, 2, 1, 0))
    wide = late_out.shape[0]
    dx1 = d_res2[pl.ds(pl.multiple_of(place[0] * ROWS, ROWS), ROWS), :]
    for k in range(wide):
        dx1 = dx1 + got[k].astype(f32)
    d_a, d_o, d_q, sums, vd, z, extra, ds_heads = attend_back(
        dx1, normed[...], inv[...], probs[...], psum[...], xt[...], w, vec[...], rows
    )
    parts = late_parts(vd, z, extra, rows)
    chunks = in_chunks(ds_heads)
    tail = stack_rows(sums + [sums_up[...]])
    for dest in range(wide):
        late_out[dest] = jnp.concatenate([block_of(parts, dest, wide).astype(bf16), chunks], 0)
    last[...] = jnp.concatenate([to_tiles(value.astype(f32)) for value in (d_q, d_o, d_a, tail)], 0).astype(bf16)


def pack_kernel(facts, last, d_up, out):
    wide = out.shape[0]
    block = d_up.shape[0] // (2 * wide)
    values = jnp.concatenate([facts[...], last[...]], 0)
    gap = jnp.zeros((block, LANES - d_up.shape[1]), f32)
    for dest in range(wide):
        pieces = [d_up[block * n : block * (n + 1), :].astype(f32) for n in (dest, wide + dest)]
        pieces = [jnp.concatenate([piece, gap], 1) for piece in pieces]
        out[dest] = jnp.concatenate([values, jnp.concatenate(pieces, 0).astype(bf16)], 0)


def rows_of(own, other):
    return jnp.concatenate([from_tiles(own[...], 0), from_tiles(other[...], 0)], 0)


def ffn_kernel(x_own, x_other, w_up, w_down, bias, u_out, h_out, own, other):
    u, h, f = ffn(rows_of(x_own, x_other), w_up[...], w_down[...], bias[...])
    half = own.shape[0]
    u_out[...], h_out[...] = u, h
    own[...] = f[:half]
    other[...] = f[half:].astype(bf16)


def total_kernel(got, heads, out):
    total = got[0].astype(f32)
    for k in range(1, got.shape[0]):
        total = total + got[k].astype(f32)
    lines = jnp.concatenate([to_tiles(total).astype(bf16), heads[...]], 0)
    for k in range(out.shape[0]):
        out[k] = lines


def middle_kernel(mats, x_own, x_other, f_own, f_other, u, w_up, w_down, vec, picks, valid, loss, pooled, d_c, d_res2, d_f, d_u, own, other, sums, sums_up, *scratch):
    w = square_weights(mats, 4, *scratch, (4,))
    x1 = rows_of(x_own, x_other).astype(f32)
    f = rows_of(f_own, f_other).astype(f32)
    got = middle(x1, f, u[...], w_up[...], w_down[...], w, vec[...], picks[...], valid[...])
    half = own.shape[0]
    loss[...], pooled[...], d_c[...], d_res2[...], d_f[...], d_u[...] = got[:6]
    own[...] = got[6][:half]
    other[...] = got[6][half:].astype(bf16)
    sums[...] = stack_rows(got[7])
    su = jnp.sum(got[5].astype(f32), 0, keepdims=True)
    sums_up[...] = jnp.concatenate([su, jnp.zeros((1, D - su.shape[1]), f32)], 1)


def own_cols(device, block):
    index = iota((D, LANES), 1)
    return jnp.where((iota((D, LANES), 0) == device * block + index) & (index < block), 1.0, 0.0).astype(bf16)


def own_rows(left, right, mine, block):
    return dot(dot(left, mine).astype(bf16), right, 0, 0)[:block]


def up_grad_kernel(x_own, x_other, d_u, d_up):
    x1 = rows_of(x_own, x_other)
    d_up[...] = dot(x1, d_u[...], 0, 0).astype(bf16)


def ffn_grads_kernel(where, h, d_f, pooled, d_c, d_down, d_head):
    d_down[...] = dot(h[...], d_f[...], 0, 0)
    block = d_head.shape[0]
    d_head[...] = own_rows(pooled[...], d_c[...], own_cols(where[1], block), block)


def grads_kernel(rows, at_early, where, early_own, early_other, late_own, late_other, facts_own, facts_other, d_wh, d_down, sums, square, in_out, out_out, up_out, vec_out, square_out, x00, q_all, o_all, d_q, d_o, d_a, y, z, wide_z):
    group, device = where[0], where[1]
    wide = facts_own.shape[0]
    devices = 2 * wide
    block = in_out.shape[0]
    first = group == 0
    for n in range(devices):
        at = slice(n * block, (n + 1) * block)
        early = (early_own, early_other)[n // wide]
        mine = [early[n % wide, at_early + k * block : at_early + (k + 1) * block, :].astype(f32) for k in range(2)]
        y[at, :] = jnp.where(first, *mine)
        late = (late_own, late_other)[n // wide]
        mine = [late[n % wide, k * block : (k + 1) * block, :].astype(f32) for k in range(2)]
        z[at, :] = jnp.where(first, *mine)
    for base, facts in ((0, facts_own), (1, facts_other)):
        at = slice(base * wide * ROWS, (base + 1) * wide * ROWS)
        lines = ROWS * (D // LANES)
        for k, out in enumerate((x00, q_all, o_all, d_q, d_o, d_a)):
            out[at, :] = from_tiles(facts, k * lines).astype(f32)
        hidden = FF // devices
        lines = 7 * lines
        for n in range(wide):
            piece = jnp.where(first, facts[n, lines : lines + block, :].astype(f32), facts[n, lines + block : lines + 2 * block, :].astype(f32))
            here, there = n * hidden, (wide + n) * hidden

            @pl.when(group == base)
            def _():
                up_out[:, here : here + hidden] = piece[:, :hidden]

            @pl.when(group != base)
            def _():
                up_out[:, there : there + hidden] = piece[:, :hidden]

    def by_heads(source, first, values):
        total = jnp.zeros((block, D), f32)
        low = source[...].astype(bf16)
        for r in range(rows):
            wide_z[...] = dot(low, expand_table(rows, first, r))
            for n in range(devices):
                total = total + wide_z[n * block : (n + 1) * block, :] * values[n * ROWS + r : n * ROWS + r + 1, :]
        return total

    d_wk = by_heads(z, Z_AT, q_all) * HEAD_DIM ** (-0.5)
    d_wv = by_heads(y, SIDE, d_o)
    mine = own_cols(device, block)
    d_wq = own_rows(x00[...].astype(bf16), d_q[...].astype(bf16), mine, block)
    d_wo = own_rows(o_all[...].astype(bf16), d_a[...].astype(bf16), mine, block)
    square_now = square[...]

    def fold(square_now, value):
        tiles = value * value
        total = jnp.sum(tiles.reshape(tiles.shape[0] // ROWS, ROWS, tiles.shape[1]), 0)
        for k in range(total.shape[1] // LANES):
            square_now = square_now + total[:, k * LANES : (k + 1) * LANES]
        return square_now

    in_out[:, :D], in_out[:, D : 2 * D], in_out[:, 2 * D :] = d_wq, d_wk, d_wv
    out_out[...] = d_wo
    for value in (d_wq, d_wk, d_wv, d_wo, d_wh[...], up_out[...], d_down[...]):
        square_now = fold(square_now, value)
    tails = jnp.concatenate([from_tiles(facts, 6 * ROWS * (D // LANES)) for facts in (facts_own, facts_other)], 0).astype(f32)
    tail = jnp.sum(tails.reshape(devices, ROWS, D), 0)
    mids = sums[...]
    pieces = [tail[0:1], mids[0:1], mids[1:2], tail[3:4], tail[4:5], tail[2:3], tail[1:2]] + [mids[k : k + 1] for k in range(2, 6)]
    index = iota((16, D), 0)
    total = jnp.zeros((16, D), f32)
    for number, row in enumerate(pieces):
        total = jnp.where(index == number, row, total)
    each = D // hidden
    for base in range(2):
        for k in range(wide):
            line = (base * wide + k) * ROWS + 5
            row = tails[line : line + 1]
            shift = hidden * (k % each)
            row = pltpu.roll(row, shift, 1) if shift else row
            number = 11 + (k // each) + jnp.where(group == base, 0, wide // each)
            total = total + jnp.where(index == number, row, 0.0)
    vec_out[...] = total
    square_now = square_now + fold(jnp.zeros((ROWS, LANES), f32), total) / devices
    for k in range(wide):
        square_out[k] = square_now


def adam_kernel(count, scales, weight, first, second, d_table, own, other, *refs):
    grads, state = refs[:count], refs[count : 4 * count]
    norm_out, factor_out = refs[4 * count : 4 * count + 2]
    outs = refs[4 * count + 2 : 7 * count + 2]
    far = refs[7 * count + 2 : 7 * count + 5]
    loads, stores, got, sent = refs[7 * count + 5 :]
    slots, lines = loads.shape[0], loads.shape[2]
    jobs = weight.shape[0] // lines
    sources = (weight, first, second, d_table)

    def load(j):
        return [pltpu.make_async_copy(ref.at[pl.ds(j * lines, lines), :], loads.at[j % slots, k], got.at[j % slots, k]) for k, ref in enumerate(sources)]

    def store(j):
        return [pltpu.make_async_copy(stores.at[j % slots, k], ref.at[pl.ds(j * lines, lines), :], sent.at[j % slots, k]) for k, ref in enumerate(far)]

    for j in range(min(slots, jobs)):
        for copy in load(j):
            copy.start()
    total = own[0] + other[0]
    for k in range(1, own.shape[0]):
        total = total + own[k] + other[k]
    total = jnp.sum(jnp.sum(total, 0, keepdims=True), 1, keepdims=True)
    norm = jnp.sqrt(total)
    factor = jnp.minimum(1.0, clip_level / (norm + 1e-06))
    norm_out[...], factor_out[...] = norm, factor
    one, two = scales[0], scales[1]
    for j in range(jobs):
        for copy in load(j):
            copy.wait()
        if j >= slots:
            for copy in store(j - slots):
                copy.wait()
        old = [loads[j % slots, k] for k in range(3)]
        new = update(*old, loads[j % slots, 3] * factor, RATES[0], one, two)
        for k in range(3):
            stores[j % slots, k] = new[k]
        for copy in store(j):
            copy.start()
        if j + slots < jobs:
            for copy in load(j + slots):
                copy.start()
    for number in range(count):
        old = [state[3 * number + k][...] for k in range(3)]
        new = update(*old, grads[number][...] * factor, RATES[number + 1], one, two)
        for k in range(3):
            outs[3 * number + k][...] = new[k]
    for j in range(max(0, jobs - slots), jobs):
        for copy in store(j):
            copy.wait()


def swap(x):
    return lax.ppermute(x, "group", [(0, 1), (1, 0)])


def exchange(x):
    return lax.all_to_all(x, "wide", split_axis=0, concat_axis=0, tiled=True)


def tie(*values):
    return lax.optimization_barrier(values)


def pair(x):
    own = exchange(x)
    return own, swap(own)


def in_order(own, other, group):
    return jnp.where(group == 0, jnp.concatenate([own, other], 0), jnp.concatenate([other, own], 0))


def plain_body(wide, passage_ids, query_ids, passage_len, query_len, positive, negatives, valid, step_count, *state):
    params, firsts, seconds = state[0::3], state[1::3], state[2::3]
    embedding, attn_in, attn_out, w_ffn_up, w_ffn_down, head, vectors = params
    group, place = lax.axis_index("group"), lax.axis_index("wide")
    device, devices = group * wide + place, 2 * wide
    feats, half_rows = embedding.shape
    block, hidden = D // devices, FF // devices
    pas_count, pas_len = passage_ids.shape
    qry_count, qry_len = query_ids.shape
    rows = pas_count + qry_count
    tokens = pas_count * pas_len + qry_count * qry_len
    live = rows * HEADS
    both = lambda x: jnp.concatenate(pair(x), 0)
    gather = lambda x: both(jnp.broadcast_to(x[None], (wide,) + x.shape))
    ids = jnp.concatenate([passage_ids.reshape(-1), query_ids.reshape(-1)])
    seq_np = np.concatenate([np.repeat(np.arange(pas_count), pas_len), pas_count + np.repeat(np.arange(qry_count), qry_len)])
    pos_np = np.concatenate([np.tile(np.arange(pas_len), pas_count), np.tile(np.arange(qry_len), qry_count)])
    lens = jnp.concatenate([jnp.repeat(passage_len, pas_len), jnp.repeat(query_len, qry_len)])
    moved = jnp.zeros((ROWS, tokens), f32).at[2].set(jnp.asarray(seq_np, f32)).at[3].set(jnp.asarray(pos_np == 0, f32))
    moved = moved.at[4].set(flag(jnp.asarray(pos_np) < lens))
    note = jnp.concatenate([ids, valid, positive, negatives.reshape(-1)])
    notes = gather(jnp.pad(note, (0, -note.shape[0] % LANES)).reshape(-1, LANES)).reshape(devices, -1)
    low_vectors = gather(jnp.pad(vectors.astype(bf16), (0, -vectors.shape[0] % LANES)).reshape(-1, LANES))
    vec = in_order(low_vectors[:wide], low_vectors[wide:], group).reshape(devices, -1)[:, : vectors.shape[0]].astype(f32).reshape(-1, D)
    all_ids = notes[:, :tokens]
    valid_rows = jnp.pad(notes[:, tokens : tokens + qry_count].astype(f32), ((0, 0), (pas_count, ROWS - rows))).reshape(-1, 1)
    at = tokens + qry_count
    picked = jnp.concatenate(
        [notes[:, at : at + qry_count, None], notes[:, at + qry_count : at + qry_count + negatives.size].reshape(devices, qry_count, -1)], 2
    )
    pick_dev = picked // pas_count
    pick_row = (((pick_dev // wide) ^ group) * wide + pick_dev % wide) * ROWS + picked % pas_count
    pick_rows = jnp.pad(pick_row, ((0, 0), (pas_count, ROWS - rows), (0, 0)), constant_values=-1).reshape(devices * ROWS, -1)
    mats = lax.all_gather(jnp.concatenate([attn_in, attn_out, head], 1).astype(bf16), ALL, axis=0, tiled=True)
    w = lambda k: mats[:, k * D : (k + 1) * D]
    w_up = lax.all_to_all(
        w_ffn_up.astype(bf16).reshape(block, devices, hidden).transpose(1, 0, 2), ALL, split_axis=0, concat_axis=0, tiled=True
    ).reshape(D, hidden)
    w_down = w_ffn_down.astype(bf16)
    bias_up = lax.dynamic_slice(vec.reshape(-1), (11 * D + device * hidden,), (hidden,))[None]
    local = all_ids - group * half_rows
    inside = ((local >= 0) & (local < half_rows)).reshape(1, -1)
    local = jnp.clip(local, 0, half_rows - 1).reshape(-1)
    looked = jnp.where(inside, jnp.take(embedding.astype(bf16), local, axis=1), jnp.zeros((), bf16))
    looked = looked.reshape(feats, devices, tokens).transpose(1, 0, 2)
    xt = exchange(looked[:wide] + swap(looked[wide:])).reshape(D, tokens)
    x1, x00, q, o, probs, psum, normed1, inv1, qk, y, p_heads = attend(xt, w, vec, moved, rows)
    x1_all = gather(x1.astype(bf16)).reshape(devices * ROWS, D)

    def to_owner(parts):
        mine = parts[: wide * ROWS] + swap(parts[wide * ROWS :])
        return jnp.sum(exchange(mine.astype(bf16).reshape(wide, ROWS, D)).astype(f32), 0)

    u, h, f_part = ffn(x1_all, w_up, w_down, bias_up)
    f_all = gather(to_owner(f_part).astype(bf16)).reshape(devices * ROWS, D).astype(f32)
    loss, pooled, d_c, d_res2, d_f, d_u, d_x1, sums = middle(x1_all.astype(f32), f_all, u, w_up, w_down, w, vec, pick_rows, valid_rows)
    d_x1 = lax.dynamic_slice(d_res2, (place * ROWS, 0), (ROWS, D)) + to_owner(d_x1)
    d_a, d_o, d_q, sums_back, vd, z, extra, ds_heads = attend_back(d_x1, normed1, inv1, probs, psum, xt, w, vec, rows)

    to_features = lambda t: both(t.T.astype(bf16).reshape(wide, feats, -1))

    def to_blocks(t):
        parts = t.T.astype(bf16).reshape(2, wide, block, -1).transpose(1, 0, 2, 3).reshape(wide, 2 * block, -1)
        got = both(parts).reshape(devices, 2, block, -1)
        return lax.dynamic_index_in_dim(got, group, 1, keepdims=False)[:, :, :live].reshape(devices, block, rows, HEADS)

    facts = gather(jnp.concatenate([x00, q, o, d_q, d_o, d_a], 0)).reshape(devices, 6, ROWS, D)
    flat_fact = lambda k: facts[:, k].reshape(devices * ROWS, D)
    by_head = lambda k: facts[:, k].reshape(devices, ROWS, HEADS, HEAD_DIM)[:, :rows]
    cut = lambda m: lax.dynamic_slice(m, (0, device * block), (devices * ROWS, block))
    d_wq = dot(cut(flat_fact(0)), flat_fact(3), 0, 0)
    d_wk = jnp.einsum("nfrh,nrhd->fhd", to_blocks(z), by_head(1), preferred_element_type=f32).reshape(block, D) * HEAD_DIM ** (-0.5)
    d_wv = jnp.einsum("nfrh,nrhd->fhd", to_blocks(y), by_head(4), preferred_element_type=f32).reshape(block, D)
    d_wo = dot(cut(flat_fact(2)), flat_fact(5), 0, 0)
    d_wup = dot(x1_all, d_u, 0, 0).astype(bf16).reshape(devices, block, hidden)
    d_wup = lax.all_to_all(d_wup, ALL, split_axis=0, concat_axis=0, tiled=True).astype(f32).transpose(1, 0, 2).reshape(block, FF)
    sums_up = jnp.pad(jnp.sum(d_u.astype(f32), 0, keepdims=True), ((0, 0), (0, D - hidden)))
    tails = gather(stack_rows(sums_back + [sums_up]))
    tail = jnp.sum(tails, 0)
    ups = in_order(tails[:wide], tails[wide:], group)[:, 5, :hidden].reshape(-1)
    mids = [row[0] for row in sums]
    d_vec = jnp.concatenate([tail[0], mids[0], mids[1], tail[3], tail[4], tail[2], tail[1]] + mids[2:] + [ups])
    d_vec = lax.dynamic_slice(d_vec, (device * vectors.shape[0],), vectors.shape)
    basis = jnp.concatenate([to_features(qk), to_features(vd), to_features(extra)], 2)
    lanes = gather(jnp.concatenate([ds_heads, p_heads], 0))
    seq = jnp.asarray(seq_np, jnp.int32)[None]
    here = sequence_of(iota((SIDE, 1), 0), rows) == seq
    widen = lambda t: jnp.where(here[None], jnp.einsum("ha,nht->nat", heads_table(rows), t, preferred_element_type=f32), 0.0).astype(bf16)
    first = ((iota((ROWS, 1), 0) == seq) & jnp.asarray(pos_np == 0)[None]).astype(bf16)
    coef = jnp.concatenate([widen(lanes[:, :16]), widen(lanes[:, 16:]), jnp.broadcast_to(first[None], (devices,) + first.shape)], 1)
    d_tok = jnp.einsum("nfa,nat->fnt", basis, coef, preferred_element_type=f32).reshape(feats, -1)
    d_table = jnp.zeros((feats, half_rows), f32).at[:, local].add(jnp.where(inside, d_tok, 0.0))
    d_head = dot(cut(pooled), d_c, 0, 0)
    grads = (d_table, jnp.concatenate([d_wq, d_wk, d_wv], 1), d_wo, d_wup, dot(h, d_f, 0, 0), d_head, d_vec)
    squares = sum(jnp.sum(g * g) for g in grads)
    grad_norm = jnp.sqrt(jnp.sum(gather(jnp.full((ROWS, LANES), squares))[:, 0, 0]))
    factor = jnp.minimum(1.0, clip_level / (grad_norm + 1e-06))
    step_float = step_count[0].astype(f32)
    one, two = 1.0 / (1.0 - jnp.power(0.9, step_float)), 1.0 / (1.0 - jnp.power(0.999, step_float))
    new = [update(params[k], firsts[k], seconds[k], grads[k] * factor, RATES[k], one, two) for k in range(7)]
    return (loss[0, 0], grad_norm) + tuple(t for group_of in new for t in group_of)


def body(wide, passage_ids, query_ids, passage_len, query_len, positive, negatives, valid, step_count, *state):
    embedding, attn_in, attn_out, w_ffn_up, w_ffn_down, head, vectors = state[0::3]
    group = lax.axis_index("group")
    place = lax.axis_index("wide")
    device = group * wide + place
    devices = 2 * wide
    feats, half_rows = embedding.shape
    block = D // devices
    hidden = FF // devices
    pas_count, pas_len = passage_ids.shape
    qry_count, qry_len = query_ids.shape
    rows = pas_count + qry_count
    tokens = pas_count * pas_len + qry_count * qry_len
    chunks = tokens // LANES
    half = -(-half_rows // (2 * LANES)) * LANES
    where = jnp.stack([group, device]).astype(jnp.int32)
    place_at = place.astype(jnp.int32)[None]
    lines = wide * ROWS

    seq_np = np.concatenate([np.repeat(np.arange(pas_count), pas_len), pas_count + np.repeat(np.arange(qry_count), qry_len)])
    pos_np = np.concatenate([np.tile(np.arange(pas_len), pas_count), np.tile(np.arange(qry_len), qry_count)])
    vec_lines = -(-vectors.shape[0] // LANES)
    packet_lines = -(-(2 * chunks + 1 + vec_lines) // ROWS) * ROWS
    note = [valid.astype(f32), positive.astype(f32), negatives.astype(f32).reshape(-1)]
    note_size = sum(t.shape[0] for t in note)
    assert 1 + note_size <= LANES
    pieces = [passage_ids.astype(f32).reshape(-1), query_ids.astype(f32).reshape(-1)]
    pieces += [jnp.repeat(passage_len.astype(f32), pas_len), jnp.repeat(query_len.astype(f32), qry_len)]
    pieces += [jnp.zeros((1,), f32)] + note + [jnp.zeros((LANES - 1 - note_size,), f32), vectors]
    pieces.append(jnp.zeros((packet_lines * LANES - sum(t.shape[0] for t in pieces),), f32))
    packet, moved = call(
        partial(prepare_kernel, half_rows, tokens),
        [shape((wide, packet_lines, LANES)), shape((ROWS, tokens))],
        jnp.concatenate(pieces).reshape(packet_lines, LANES), jnp.asarray(seq_np, jnp.int32)[None], jnp.asarray(pos_np, jnp.int32)[None],
        near_outs=(0,), name="prepare",
    )
    packet_own = exchange(packet)
    (table,) = call(build_kernel, [shape((half, LANES))], embedding, name="build", flops=10**8)
    packet_own, table = tie(packet_own, table)
    packet_other = swap(packet_own)
    (low_mats,) = call(cast_kernel, [shape((block, 5 * D), bf16)], attn_in, attn_out, head, near_outs=(0,), name="cast")
    mats = lax.all_gather(low_mats, ALL, axis=0, tiled=True)
    w_ffn_up, w_ffn_down, _ = tie(w_ffn_up, w_ffn_down, packet)
    w_up = lax.all_to_all(
        w_ffn_up.astype(bf16).reshape(block, devices, hidden).transpose(1, 0, 2), ALL, split_axis=0, concat_axis=0, tiled=True
    ).reshape(D, hidden)
    w_down = w_ffn_down.astype(bf16)

    def numbers_of(packets):
        local = packets[:, :chunks] - (group * half_rows).astype(f32)
        row_at = jnp.clip(jnp.where(local >= half, local - half, local), 0, half - 1)
        return row_at.astype(jnp.int32).reshape(-1), packets[:, 2 * chunks, 0].astype(jnp.int32)

    look = partial(lookup, half_rows=half_rows, feats=feats, count=tokens)
    num_own, num_other = numbers_of(packet_own), numbers_of(packet_other)
    theirs = look(where, *num_other, packet_other, table)
    xt = exchange(look(where, *num_own, packet_own, table, add=swap(theirs))).reshape(D, tokens)
    numbers = jnp.concatenate([num_own[0], num_other[0]])
    firsts = jnp.concatenate([num_own[1], num_other[1]])
    packets = jnp.concatenate([packet_own, packet_other], 0)

    vec = in_order(packet_own, packet_other, group)[:, 2 * chunks + 1 : 2 * chunks + 1 + vec_lines].reshape(devices, -1)
    vec = vec[:, : vectors.shape[0]].reshape(-1, D)
    bias_up = lax.dynamic_slice(vec.reshape(-1), (11 * D + device * hidden,), (hidden,))[None]
    notes = packets[:, 2 * chunks]
    valid_rows = jnp.pad(notes[:, 1 : 1 + qry_count], ((0, 0), (pas_count, ROWS - rows))).reshape(-1, 1)
    at = 1 + qry_count
    picked = jnp.concatenate(
        [notes[:, at : at + qry_count, None], notes[:, at + qry_count : at + qry_count + negatives.size].reshape(devices, qry_count, -1)], 2
    ).astype(jnp.int32)
    pick_dev = picked // pas_count
    pick_row = (((pick_dev // wide) ^ group) * wide + pick_dev % wide) * ROWS + picked % pas_count
    pick_rows = jnp.pad(pick_row, ((0, 0), (pas_count, ROWS - rows), (0, 0)), constant_values=-1).reshape(devices * ROWS, -1)

    xt, vec, bias_up, valid_rows, pick_rows, w_up, w_down, packets, numbers, firsts = tie(
        xt, vec, bias_up, valid_rows, pick_rows, w_up, w_down, packets, numbers, firsts
    )
    tile_lines = ROWS * (D // LANES)
    sent, p_heads, facts, probs, psum, normed1, inv1 = call(
        partial(attend_kernel, rows),
        [
            shape((wide, tile_lines + 2 * block, LANES), bf16), shape((16 * chunks, LANES), bf16),
            shape((3 * tile_lines, LANES), bf16),
            shape((SIDE, tokens)), shape((SIDE, 1)), shape((ROWS, D)), shape((ROWS, 1)),
        ],
        xt, vec, moved,
        far=(mats,), near=(0,), near_outs=(0,), scratch=weight_scratch(4), name="attend", flops=10**9,
    )
    x_own, x_other = pair(sent)
    u, h, f_mine, f_theirs = call(
        ffn_kernel,
        [shape((devices * ROWS, hidden)), shape((devices * ROWS, hidden), bf16), shape((lines, D)), shape((lines, D), bf16)],
        x_own, x_other, w_up, w_down, bias_up,
        near=(0, 1), near_outs=(2, 3), name="ffn", flops=10**8, vmem=16,
    )
    f_parts = exchange((f_mine + swap(f_theirs)).astype(bf16).reshape(wide, ROWS, D))
    (f_sum,) = call(
        total_kernel, [shape((wide, tile_lines + 16 * chunks, LANES), bf16)], f_parts, p_heads, near=(0,), near_outs=(0,), name="total"
    )
    f_own, f_other = pair(f_sum)
    loss, pooled, d_c, d_res2, d_f, d_u, d_mine, d_theirs, sums, sums_up = call(
        middle_kernel,
        [
            shape((1, 1)), shape((devices * ROWS, D), bf16), shape((devices * ROWS, D), bf16), shape((devices * ROWS, D)),
            shape((devices * ROWS, D), bf16), shape((devices * ROWS, hidden), bf16), shape((lines, D)), shape((lines, D), bf16),
            shape((ROWS, D)), shape((1, D)),
        ],
        x_own, x_other, f_own, f_other, u, w_up, w_down, vec, pick_rows, valid_rows,
        far=(mats,), scratch=weight_scratch(1), near=(0, 1, 2, 3), near_outs=(6, 7), name="middle", flops=10**9, vmem=32,
    )
    d_sum = (d_mine + swap(d_theirs)).astype(bf16).reshape(wide, ROWS, D)
    got = exchange(d_sum)
    (d_up,) = call(up_grad_kernel, [shape((D, hidden), bf16)], x_own, x_other, d_u, after=(d_sum,), near=(0, 1), name="up_grad", flops=10**8)
    late, last = call(
        partial(attend_back_kernel, rows),
        [shape((wide, 2 * block + 16 * chunks, LANES), bf16), shape((4 * tile_lines, LANES), bf16)],
        got, d_res2, sums_up, normed1, inv1, probs, psum, xt, vec,
        scalars=(place_at,), far=(mats,), near=(0,), near_outs=(0,), scratch=weight_scratch(4), name="attend_back", flops=10**9,
    )
    late_own, late_other = pair(late)
    d_down, d_whead = call(
        ffn_grads_kernel, [shape((hidden, D)), shape((block, D))], h, d_f, pooled, d_c,
        scalars=(where,), after=(late,), name="ffn_grads", flops=10**8,
    )
    (packed,) = call(
        pack_kernel, [shape((wide, 7 * tile_lines + 2 * block, LANES), bf16)], facts, last, d_up, after=(late_own,), near_outs=(0,), name="pack",
    )
    last_own = exchange(packed)
    d_table, square = spread_tokens(
        where, numbers, firsts, packets, (x_own, x_other), (late_own, late_other), (f_own, f_other), tile_lines, rows, half_rows, feats, tokens
    )
    last_own = last_own + (square[0, 0] * 0.0).astype(bf16)
    last_other = swap(last_own)
    d_attn_in, d_wo, d_wup, d_vec, squares = call(
        partial(grads_kernel, rows, tile_lines),
        [shape((block, 3 * D)), shape((block, D)), shape((block, FF)), shape((16, D)), shape((wide, ROWS, LANES))],
        x_own, x_other, late_own, late_other, last_own, last_other, d_whead, d_down, sums, square,
        scalars=(where,),
        scratch=[pltpu.VMEM((devices * ROWS, D), f32)] * 6 + [pltpu.VMEM((D, LANES), f32)] * 2 + [pltpu.VMEM((D, D), f32)],
        near=(4, 5), near_outs=(4,), name="grads", flops=10**9, vmem=32,
    )
    squares_own, squares_other = pair(squares)
    d_vectors = lax.dynamic_slice(d_vec.reshape(-1), (device * vectors.shape[0],), vectors.shape)
    step_float = step_count[0].astype(f32)
    scales = jnp.stack([1.0 / (1.0 - jnp.power(0.9, step_float)), 1.0 / (1.0 - jnp.power(0.999, step_float))])
    grads = (d_attn_in, d_wo, d_wup, d_down, d_whead)
    middle_state = state[3:18]
    slots, step_rows = 3, ROWS
    norm, factor, *new = call(
        partial(adam_kernel, len(grads)),
        [shape((1, 1)), shape((1, 1))] + [shape(t.shape) for t in middle_state],
        squares_own, squares_other, *grads, *middle_state,
        scalars=(scales,), far=(*state[:3], d_table), far_outs=[shape(embedding.shape)] * 3,
        scratch=[
            pltpu.VMEM((slots, 4, step_rows, half_rows), f32), pltpu.VMEM((slots, 3, step_rows, half_rows), f32),
            pltpu.SemaphoreType.DMA((slots, 4)), pltpu.SemaphoreType.DMA((slots, 3)),
        ],
        near=(0, 1), name="adam", vmem=40,
    )
    new_vectors = update(*state[18:], d_vectors * factor[0, 0], RATES[6], scales[0], scales[1])
    return (loss[0, 0], norm[0, 0]) + tuple(new[15:]) + tuple(new[:15]) + new_vectors


def solution(mesh):
    split_rows = P(ALL, None)
    flat = P(ALL)
    table = P("wide", "group")
    mats = (table,) * 3 + (split_rows,) * 15 + (flat,) * 3
    in_specs = (split_rows, split_rows, flat, flat, flat, split_rows, flat, P()) + mats
    wide = mesh.shape["wide"]
    thick = D % (2 * wide * ROWS) == 0 and wide * ROWS <= LANES
    return jax.shard_map(
        partial(body if thick else plain_body, wide), mesh=mesh, in_specs=in_specs, out_specs=(P(), P()) + mats, check_vma=False
    )
```

```python
from functools import partial

import jax
import jax.numpy as jnp
import numpy as np
from jax import lax
from jax.experimental import pallas as pl
from jax.experimental.pallas import tpu as pltpu
from jax.sharding import PartitionSpec as P

D = 768
HEADS = 12
HEAD_DIM = 64
FF = 3072
ROWS = 8
LANES = 128
SIDE = 64
STEP = 16
ALL = ("group", "wide")
clip_level = 0.02
f32 = jnp.float32
bf16 = jnp.bfloat16
RATES = (0.5, 0.5 * D**-0.5, 0.5 * (D // 16) ** -0.5, 0.5 * D**-0.5, 0.5 * FF**-0.5, 0.5 * D**-0.5, 0.2)


def dot(a, b, ca=1, cb=0):
    return lax.dot_general(a, b, (((ca,), (cb,)), ((), ())), preferred_element_type=f32)


def split(x):
    high = x.astype(bf16)
    return high, (x - high.astype(f32)).astype(bf16)


def dot_split(x, w, cb=0):
    high, rest = split(x)
    return dot(high, w, 1, cb) + dot(rest, w, 1, cb)


def iota(shape, dim):
    return lax.broadcasted_iota(jnp.int32, shape, dim)


def stack_rows(rows):
    index = iota((ROWS, rows[0].shape[1]), 0)
    total = jnp.zeros(index.shape, f32)
    for number, row in enumerate(rows):
        total = jnp.where(index == number, row, total)
    return total


def layer_norm(resid):
    centred = resid - jnp.mean(resid, -1, keepdims=True)
    inv_std = lax.rsqrt(jnp.mean(centred * centred, -1, keepdims=True) + 1e-05)
    return centred * inv_std, inv_std


def norm_back(grad_out, normed, inv_std, gain):
    scaled = grad_out * gain
    return inv_std * (
        scaled
        - jnp.mean(scaled, -1, keepdims=True)
        - normed * jnp.mean(scaled * normed, -1, keepdims=True)
    )


def flag(condition):
    return jnp.where(condition, 1.0, 0.0)


def sequence_of(a, rows):
    assert HEADS == 12
    return jnp.where((a >= 0) & (a < rows * HEADS), lax.shift_right_logical(a * 43, 9), 99)


def head_of(a, rows):
    return a - HEADS * sequence_of(a, rows)


def spread_table(rows):
    return flag(sequence_of(iota((SIDE, ROWS), 0), rows) == iota((SIDE, ROWS), 1)).astype(bf16)


def column_table(rows):
    return flag(head_of(iota((SIDE, D), 0), rows) == lax.shift_right_logical(iota((SIDE, D), 1), 6))


def heads_table(rows):
    return flag(head_of(iota((16, SIDE), 1), rows) == iota((16, SIDE), 0)).astype(bf16)


def place_table(rows, first):
    a = iota((LANES, SIDE), 1)
    return flag((iota((LANES, SIDE), 0) == first + a) & (a < rows * HEADS)).astype(bf16)


def expand_table(rows, first, r):
    return flag(iota((LANES, D), 0) == first + r * HEADS + lax.shift_right_logical(iota((LANES, D), 1), 6)).astype(bf16)


def prepare(ids, live, seq, pos, group_rows):
    count = ids.shape[1]
    first = jnp.where(ids < group_rows, 1.0, 0.0)
    high = lax.shift_right_logical(ids, 8)
    index = iota((ROWS, count), 0)
    values = jnp.zeros((ROWS, count), f32)
    pieces = (high.astype(f32), (ids - high * 256).astype(f32), seq.astype(f32), jnp.where(pos == 0, 1.0, 0.0), live)
    for number, row in enumerate(pieces):
        values = jnp.where(index == number, row, values)
    left, right = iota((count, count), 0), iota((count, count), 1)
    ahead = jnp.where(right < left, 1.0, 0.0).astype(bf16)
    same = jnp.where(right == left, 1.0, 0.0).astype(bf16)
    marks = jnp.broadcast_to(first, (ROWS, count)).astype(bf16)
    before = dot(ahead, marks, 1, 1)[:, :1]
    mine = dot(same, marks, 1, 1)[:, :1]
    total = jnp.sum(first, 1, keepdims=True)
    target = jnp.where(mine > 0.5, before, total + iota((count, 1), 0).astype(f32) - before)
    moves = jnp.where(target.astype(jnp.int32) == right, 1.0, 0.0).astype(bf16)
    return dot(values.astype(bf16), moves), total


def attend(xt, w, vec, moved, rows):
    g1, bq, bv, bo, be1 = vec[0:1], vec[3:4], vec[4:5], vec[5:6], vec[6:7]
    seq_id, slot0, live = moved[2:3], moved[3:4], moved[4:5]
    spread, columns = spread_table(rows), column_table(rows)
    index = iota((ROWS, xt.shape[1]), 0).astype(f32)
    pick0 = flag((index == seq_id) & (slot0 > 0.5)).astype(bf16)
    x00 = dot(pick0, xt, 1, 1)
    q = (dot(x00.astype(bf16), w(0)) + bq).astype(bf16)
    q_wide = (dot(spread, q) * columns).astype(bf16)
    qk = dot(q_wide, w(1), 1, 1) * HEAD_DIM ** (-0.5)
    mask = (sequence_of(iota((SIDE, 1), 0), rows).astype(f32) == seq_id) & (live > 0.5)
    scores = jnp.where(mask, dot_split(qk, xt), -1e30)
    raw = jnp.where(mask, jnp.exp(scores - jnp.max(scores, 1, keepdims=True)), 0.0)
    total = jnp.sum(raw, 1, keepdims=True)
    probs = raw / jnp.where(total > 0.0, total, 1.0)
    probs_low = probs.astype(bf16)
    y = dot(probs_low, xt, 1, 1)
    psum = jnp.sum(probs_low.astype(f32), 1, keepdims=True)
    mixed = dot_split(y, w(2)) + psum * bv
    o = dot(spread, (mixed * columns).astype(bf16), 0, 0).astype(bf16)
    normed, inv = layer_norm(x00 + dot(o, w(3)) + bo)
    return normed * g1 + be1, x00.astype(bf16), q, o, probs, psum, normed, inv, qk, y


def attend_back(dx1, normed, inv, probs, psum, xt, w, vec, rows):
    g1, bv = vec[0:1], vec[4:5]
    spread, columns = spread_table(rows), column_table(rows)
    d_res = norm_back(dx1, normed, inv, g1)
    d_a = d_res.astype(bf16)
    d_o = dot(d_a, w(3), 1, 1).astype(bf16)
    d_o_wide = dot(spread, d_o) * columns
    vd = dot(d_o_wide.astype(bf16), w(2), 1, 1)
    dp = dot_split(vd, xt) + jnp.sum(d_o_wide * bv, 1, keepdims=True)
    ds = (probs * (dp - jnp.sum(probs * dp, 1, keepdims=True))).astype(bf16)
    z = dot(ds, xt, 1, 1)
    zw = dot_split(z, w(1)) * (HEAD_DIM ** (-0.5)) * columns
    d_q = dot(spread, zw.astype(bf16), 0, 0).astype(bf16)
    extra = d_res + dot(d_q, w(0), 1, 1)
    sums = [
        jnp.sum(dx1 * normed, 0, keepdims=True),
        jnp.sum(dx1, 0, keepdims=True),
        jnp.sum(d_a.astype(f32), 0, keepdims=True),
        jnp.sum(d_q.astype(f32), 0, keepdims=True),
        jnp.sum(d_o_wide * psum, 0, keepdims=True),
    ]
    return d_a, d_o, d_q, sums, vd, z, extra, ds


def both_halves(value, rows):
    low = value.astype(bf16)
    return dot(place_table(rows, 0), low).T, dot(place_table(rows, SIDE), low).T


def table_block(halves, dest, block):
    first = 2 * block * dest
    return halves[0][first : first + block] + halves[1][first + block : first + 2 * block]


def weight_block(halves, dest, block, wide):
    return halves[0][block * dest : block * (dest + 1)] + halves[1][block * (wide + dest) : block * (wide + dest + 1)]


HEAD_LINES = 8


def pack_heads(value, rows):
    row, head = iota((HEAD_LINES, SIDE), 0), head_of(iota((HEAD_LINES, SIDE), 1), rows)
    most = dot(flag(row == head).astype(bf16), value)
    rest = [dot(flag((row - 4 * k + 8 == head) & (head >= 8) & (head < HEADS)).astype(bf16), value) for k in range(2)]
    cut = lambda t, k: t[:, k * LANES : (k + 1) * LANES]
    chunks = value.shape[1] // LANES
    tiles = [cut(most, k) for k in range(chunks)]
    for k in range(0, chunks, 2):
        tiles.append(cut(rest[0], k) + cut(rest[1], k + 1) if k + 1 < chunks else cut(rest[0], k))
    return jnp.concatenate(tiles, 0).astype(bf16)


def unpack_heads(lines, chunks):
    tile = lambda k: lines[k * HEAD_LINES : (k + 1) * HEAD_LINES].astype(f32)
    most = jnp.concatenate([tile(k) for k in range(chunks)], 1)
    rest = []
    for k in range(chunks):
        value = tile(chunks + k // 2)
        rest.append(pltpu.roll(value, 4, 0) if k % 2 else value)
    rest = jnp.concatenate(rest, 1)
    return jnp.concatenate([most, jnp.where(iota(rest.shape, 0) < HEADS - 8, rest, 0.0)], 0)


def head_lines(chunks):
    return HEAD_LINES * (chunks + (chunks + 1) // 2)


def to_tiles(value):
    return jnp.concatenate([value[:, k : k + LANES] for k in range(0, value.shape[1], LANES)], 0)


def from_tiles(got, first, lines=ROWS):
    pieces = [got[:, first + k * lines : first + (k + 1) * lines, :] for k in range(D // LANES)]
    return jnp.concatenate([p.reshape(-1, LANES) for p in pieces], 1)


def ffn(x1, w_up, w_down, bias):
    u = dot(x1.astype(bf16), w_up) + bias
    h = (0.5 * u * (1.0 + lax.erf(u * 0.5**0.5))).astype(bf16)
    return u, h, dot(h, w_down)


def middle(x1, f, u, w_up, w_down, w, vec, picks):
    g2, gc, b2, be2, bc, bec = vec[1:2], vec[2:3], vec[7:8], vec[8:9], vec[9:10], vec[10:11]
    count = x1.shape[0]
    valid, picks = picks[:, :1].astype(f32), picks[:, 1:]
    normed2, inv2 = layer_norm(x1 + (f + b2))
    pooled = (normed2 * g2 + be2).astype(bf16)
    normed_c, inv_c = layer_norm(dot(pooled, w(4)) + bc)
    e = (normed_c * gc + bec).astype(bf16)
    scores = dot(e, e, 1, 1) * D ** (-0.5)
    col = iota((count, count), 1)
    is_pos = jnp.where(col == picks[:, 0:1], 1.0, 0.0)
    negs = jnp.zeros_like(is_pos)
    for number in range(1, picks.shape[1]):
        negs = negs + jnp.where(col == picks[:, number : number + 1], 1.0, 0.0)
    taken = (is_pos + negs) > 0.0
    top = jnp.max(jnp.where(taken, scores, -1e30), 1, keepdims=True)
    raw = jnp.where(taken, jnp.exp(scores - top), 0.0)
    total = jnp.sum(raw * (is_pos + negs), 1, keepdims=True)
    total = jnp.where(total > 0.0, total, 1.0)
    share = raw / total
    valid_count = jnp.sum(valid, 0, keepdims=True)
    per_query = top + jnp.log(total) - jnp.sum(is_pos * scores, 1, keepdims=True)
    loss = jnp.sum(jnp.where(valid > 0.0, valid * per_query, 0.0), 0, keepdims=True) / valid_count
    weight = valid / valid_count
    d_pos = (weight * (share - 1.0)).astype(bf16).astype(f32)
    d_neg = (weight * share).astype(bf16).astype(f32)
    d_scores = d_pos * is_pos + d_neg * negs
    high, rest = split(d_scores)
    d_e = (dot(high, e) + dot(rest, e) + dot(high, e, 0, 0) + dot(rest, e, 0, 0)) * D ** (-0.5)
    d_c = norm_back(d_e, normed_c, inv_c, gc).astype(bf16)
    d_x2 = dot(d_c, w(4), 1, 1)
    d_res2 = norm_back(d_x2, normed2, inv2, g2)
    d_f = d_res2.astype(bf16)
    lines = u.shape[0]
    d_h = dot(d_f[:lines], w_down, 1, 1)
    slope = 0.5 * (1.0 + lax.erf(u * 0.5**0.5)) + u * jnp.exp(-0.5 * u * u) * (2.0 * np.pi) ** (-0.5)
    d_u = (d_h * slope).astype(bf16)
    d_x1 = dot(d_u, w_up, 1, 1)
    sums = [
        jnp.sum(d_x2 * normed2, 0, keepdims=True),
        jnp.sum(d_e * normed_c, 0, keepdims=True),
        jnp.sum(d_f.astype(f32), 0, keepdims=True),
        jnp.sum(d_x2, 0, keepdims=True),
        jnp.sum(d_c.astype(f32), 0, keepdims=True),
        jnp.sum(d_e, 0, keepdims=True),
    ]
    return loss, pooled, d_c, d_res2, d_f, d_u, d_x1, sums


def update(weight, first, second, gradient, rate, scale_one, scale_two):
    first_new = 0.9 * first + 0.1 * gradient
    second_new = 0.999 * second + 0.001 * gradient * gradient
    first_hat = first_new * scale_one
    second_hat = second_new * scale_two
    return weight - rate * (first_hat / (jnp.sqrt(second_hat) + 1e-08) + 0.01 * weight), first_new, second_new


def shape(dims, kind=f32):
    return jax.ShapeDtypeStruct(dims, kind)


MIB = 1 << 20


def full_block(dims):
    return pl.BlockSpec(dims, lambda i: (0,) * len(dims), pipeline_mode=pl.Buffered(1))


def pinned(x):
    return pltpu.with_memory_space_constraint(x, pltpu.HBM)


def call(kernel, outs, *args, scalars=(), far=(), far_outs=(), after=(), near=(), near_outs=(), scratch=(), vmem=24, name=None, flops=0):
    anywhere = pl.BlockSpec(memory_space=pl.ANY)
    in_specs = [pl.BlockSpec(memory_space=pltpu.SMEM)] * len(scalars) + [anywhere] * len(far)
    in_specs += [full_block(a.shape) for a in args] + [anywhere] * len(after)
    moved = sum(int(np.prod(a.shape)) * a.dtype.itemsize for a in list(args) + list(far) + list(outs) + list(far_outs))
    used = len(scalars) + len(far) + len(args)

    def run(*refs):
        kernel(*refs[:used], *refs[used + len(after) :])

    shapes = [o if k in near_outs else pltpu.HBM(o.shape, o.dtype) for k, o in enumerate(outs)]
    shapes += [pltpu.HBM(o.shape, o.dtype) for o in far_outs]
    args = [a if k in near else pinned(a) for k, a in enumerate(args)]
    return pl.pallas_call(
        run,
        grid=(1,),
        out_shape=shapes,
        in_specs=in_specs,
        out_specs=[full_block(o.shape) for o in outs] + [anywhere] * len(far_outs),
        scratch_shapes=list(scratch),
        compiler_params=pltpu.CompilerParams(vmem_limit_bytes=vmem * MIB),
        cost_estimate=pl.CostEstimate(flops=int(flops), bytes_accessed=moved, transcendentals=0),
        name=name,
    )(*scalars, *(pinned(a) for a in far), *args, *after)


def square_weights(mats, first, buffers, signals, order):
    copies = {
        k: pltpu.make_async_copy(mats.at[:, pl.ds(k * D, D)], buffers.at[k - first], signals.at[k - first]) for k in order
    }
    for k in order:
        copies[k].start()
    ready = {}

    def get(k):
        if k not in ready:
            copies[k].wait()
            ready[k] = buffers[k - first]
        return ready[k]

    return get


def weight_scratch(count):
    return [pltpu.VMEM((count, D, D), bf16), pltpu.SemaphoreType.DMA((count,))]


def prepare_kernel(group_rows, count, rows, base, vectors, seq, pos, up, packet, moved):
    chunks = count // LANES
    ids = jnp.concatenate([base[k : k + 1, :] for k in range(chunks)], 1)
    entries = base[chunks : chunks + 1, :]
    live = jnp.zeros((1, count), f32)
    for number in range(rows):
        live = jnp.where((seq[...] == number) & (pos[...] < entries[:, number : number + 1]), 1.0, live)
    got, total = prepare(ids, live, seq[...], pos[...], group_rows)
    moved[...] = got
    code = got[2:3] + 8.0 * got[3:4]
    lane = iota((1, LANES), 1)
    note = pltpu.roll(entries.astype(f32), LANES - rows + 1, 1)
    high = lax.shift_right_logical(total.astype(jnp.int32), 8)
    note = jnp.where(lane == 0, total - 256.0 * high.astype(f32), jnp.where(lane == LANES - 1, high.astype(f32), note))
    lines = [line[:, k * LANES : (k + 1) * LANES] for line in (got[0:1], got[1:2], code) for k in range(chunks)]
    lines += [note] + [vectors[k : k + 1, :] for k in range(vectors.shape[0])]
    wide, block = packet.shape[0], up.shape[0]
    hidden = up.shape[1] // (2 * wide)
    first = packet.shape[1] - 2 * block
    index = iota((first, LANES), 0)
    whole = jnp.zeros((first, LANES), f32)
    for number, line in enumerate(lines):
        whole = jnp.where(index == number, line, whole)
    gap = jnp.zeros((block, LANES - hidden), f32)
    for dest in range(wide):
        pieces = [jnp.concatenate([up[:, n * hidden : (n + 1) * hidden], gap], 1) for n in (dest, wide + dest)]
        packet[dest] = jnp.concatenate([whole] + pieces, 0).astype(bf16)


def cast_kernel(attn_in, attn_out, head, out, head_out):
    out[:, : 3 * D] = attn_in[...].astype(bf16)
    out[:, 3 * D : 4 * D] = attn_out[...].astype(bf16)
    head_out[...] = head[...].astype(bf16)


def build_kernel(emb, table):
    feats, vocab = emb.shape
    half = table.shape[0]
    blocks, second = half // LANES, (vocab - half) // LANES
    gap = jnp.zeros((SIDE - feats, LANES), f32)

    def build(b, both):
        start = pl.multiple_of(b * LANES, LANES)
        low = emb[:, pl.ds(start, LANES)]
        high = jnp.zeros_like(low)
        if both:
            high = emb[:, pl.ds(pl.multiple_of(half + start, LANES), LANES)]
        table[pl.ds(start, LANES), :] = jnp.concatenate([low, gap, high, gap], 0).astype(bf16).T.astype(f32)

    unroll = 7

    def step(i, carry):
        for k in range(unroll):
            build(i * unroll + k, True)
        return carry

    lax.fori_loop(0, second // unroll, step, 0)
    for b in range(second // unroll * unroll, blocks):
        build(jnp.int32(b), b < second)


def side_of(packet, s, chunks, group, half_rows, half):
    ids = lanes_of(packet, s, 0, chunks) * 256.0 + lanes_of(packet, s, chunks, chunks)
    local = ids - (group * half_rows).astype(f32)
    inside = (local >= 0.0) & (local < float(half_rows))
    return jnp.where(inside, jnp.where(local >= float(half), 2.0, 1.0), 0.0)


def own_span(first, group, count):
    return jnp.where(group == 0, 0, first), jnp.where(group == 0, first, count)


def number_block(per, count):
    return pl.BlockSpec((1, 1, per * count), lambda i, *s: (i, 0, 0), memory_space=pltpu.SMEM)


def lookup_kernel(half_rows, per, unroll, add, where, firsts, numbers, packet, table, *refs):
    out, buf = refs[-2:]
    feats, count = out.shape[1:]
    group = where[0]
    chunks = count // LANES
    half = table.shape[0]
    eye = jnp.where(iota((LANES, LANES), 0) == iota((LANES, LANES), 1), 1.0, 0.0).astype(bf16)
    at = pl.program_id(0) * per
    for s in range(per):
        low, high = own_span(firsts[at + s], group, count)

        def step(i, carry):
            for k in range(unroll):
                t = i * unroll + k
                buf[pl.ds(s * count + t, 1), :] = table[pl.ds(numbers[0, 0, s * count + t], 1), :]
            return carry

        lax.fori_loop(low // unroll, (high + unroll - 1) // unroll, step, 0)
    for s in range(per):
        side = side_of(packet, s, chunks, group, half_rows, half)
        turned = dot(eye, buf[s * count : (s + 1) * count, :].astype(bf16), 1, 1)
        pick = jnp.where(side > 1.5, turned[SIDE : SIDE + feats], turned[:feats])
        value = jnp.where(side > 0.5, pick, 0.0)
        if add:
            value = value + refs[0][s].astype(f32)
        out[s] = value.astype(bf16)


def lanes_of(packet, s, first, chunks):
    return jnp.concatenate([packet[s, first + c : first + c + 1, :].astype(f32) for c in range(chunks)], 1)


def lookup(where, numbers, firsts, packets, table, half_rows, feats, count, add=None, per=4, unroll=32):
    sources = packets.shape[0]
    some = lambda dims: pl.BlockSpec((per,) + dims, lambda i, *s: (i, 0, 0))
    extra = [] if add is None else [add]
    return pl.pallas_call(
        partial(lookup_kernel, half_rows, per, unroll, add is not None),
        out_shape=shape((sources, feats, count), bf16),
        grid_spec=pltpu.PrefetchScalarGridSpec(
            num_scalar_prefetch=2,
            grid=(sources // per,),
            in_specs=[number_block(per, count), some(packets.shape[1:]), pl.BlockSpec(table.shape, lambda i, *s: (0, 0), pipeline_mode=pl.Buffered(1))] + [some((feats, count)) for _ in extra],
            out_specs=some((feats, count)),
            scratch_shapes=[pltpu.VMEM((per * count, LANES), f32)],
        ),
        compiler_params=pltpu.CompilerParams(vmem_limit_bytes=16 * MIB),
        cost_estimate=pl.CostEstimate(flops=10**9, bytes_accessed=10**7, transcendentals=0),
        name="lookup" if add is None else "lookup_add",
    )(where, firsts, numbers.reshape(-1, 1, per * count), packets, pinned(table), *extra)


def spread_kernel(rows, half_rows, feats, per, unroll, copies, at_early, at_heads, where, firsts, numbers, packet, early_own, early_other, late_own, late_other, p_own, p_other, out, square, *scratch):
    parts, buf = scratch[:copies], scratch[copies]
    group = where[0]
    chunks = buf.shape[0] // (per * LANES)
    count = chunks * LANES
    half = parts[0].shape[0]
    vocab = out.shape[1]
    blocks = half // LANES
    step_at = pl.program_id(0)

    @pl.when(step_at == 0)
    def _():
        def clear(i, carry):
            for part in parts:
                part[pl.ds(pl.multiple_of(i * LANES, LANES), LANES), :] = jnp.zeros((LANES, LANES), f32)
            return carry

        lax.fori_loop(0, blocks, clear, 0)

    eye = flag(iota((LANES, LANES), 0) == iota((LANES, LANES), 1)).astype(bf16)
    gap = jnp.zeros((SIDE - feats, count), f32)
    block = feats // 2
    lane, slot = iota((LANES, 2 * LANES), 0), iota((LANES, 2 * LANES), 1)
    half_of = lax.shift_right_logical(slot, 7)
    slot = slot - half_of * LANES
    seq_of, head = lax.shift_right_logical(slot, 4), slot - lax.shift_right_logical(slot, 4) * STEP
    relane = flag((lane == half_of * SIDE + seq_of * HEADS + head) & (head < HEADS) & (seq_of < rows)).astype(bf16)
    empty = jnp.zeros((LANES - rows * STEP, count), f32)
    is_own = step_at < pl.num_programs(0) // 2

    def pick(own, other, s, first, lines):
        return jnp.where(is_own, own[s, first : first + lines, :], other[s, first : first + lines, :])

    for s in range(per):
        code = lanes_of(packet, s, 2 * chunks, chunks)
        slot0 = code >= 8.0
        seq = jnp.where(slot0, code - 8.0, code)
        scores = unpack_heads(pick(late_own, late_other, s, block + ROWS, head_lines(chunks)), chunks)
        values = unpack_heads(pick(p_own, p_other, s, at_heads, head_lines(chunks)), chunks)
        parts_of = [jnp.where(seq == float(r), scores, 0.0) for r in range(rows)] + [empty]
        parts_of += [jnp.where(seq == float(r), values, 0.0) for r in range(rows)] + [empty]
        both = jnp.concatenate([pick(early_own, early_other, s, at_early, block), pick(late_own, late_other, s, 0, block)], 0)
        wide_rows = dot(both, relane).astype(bf16)
        basis = [jnp.concatenate([wide_rows[k : k + block, :LANES], wide_rows[k : k + block, LANES:]], 0) for k in (0, block)]
        x = dot(jnp.concatenate(basis, 1), jnp.concatenate(parts_of, 0).astype(bf16))
        first = flag((iota((ROWS, count), 0).astype(f32) == seq) & slot0).astype(bf16)
        x = x + dot(pick(late_own, late_other, s, block, ROWS), first, 0, 0)[:feats]
        side = side_of(packet, s, chunks, group, half_rows, half)
        tall = jnp.concatenate([jnp.where(side == 1.0, x, 0.0), gap, jnp.where(side == 2.0, x, 0.0), gap], 0).astype(bf16)
        for c in range(chunks):
            start = s * count + c * LANES
            buf[start : start + LANES, :] = dot(eye, tall[:, c * LANES : (c + 1) * LANES], 1, 1)
    for s in range(per):
        low, high = own_span(firsts[step_at * per + s], group, count)

        def step(i, carry):
            for k in range(unroll):
                t = i * unroll + k
                part = parts[k % copies]
                row = numbers[0, 0, s * count + t]
                part[pl.ds(row, 1), :] = part[pl.ds(row, 1), :] + buf[pl.ds(s * count + t, 1), :]
            return carry

        lax.fori_loop(low // unroll, (high + unroll - 1) // unroll, step, 0)

    @pl.when(step_at == pl.num_programs(0) - 1)
    def _():
        def emit(b, total, both):
            start = pl.multiple_of(b * LANES, LANES)
            lines = parts[0][pl.ds(start, LANES), :]
            for part in parts[1:]:
                lines = lines + part[pl.ds(start, LANES), :]
            turned = lines.T
            out[:, pl.ds(start, LANES)] = turned[:feats]
            if both:
                out[:, pl.ds(pl.multiple_of(half + start, LANES), LANES)] = turned[SIDE : SIDE + feats]
            return total + lines * lines

        second = (vocab - half) // LANES
        group_of = 7

        def several(i, total):
            for k in range(group_of):
                total = emit(i * group_of + k, total, True)
            return total

        total = lax.fori_loop(0, second // group_of, several, jnp.zeros((LANES, LANES), f32))
        for b in range(second // group_of * group_of, blocks):
            total = emit(jnp.int32(b), total, b < second)
        square[...] = jnp.sum(total.reshape(LANES // ROWS, ROWS, LANES), 0)


def spread_tokens(where, numbers, firsts, packets, early, late, p_heads, at_early, rows, half_rows, feats, count, per=8, unroll=40, copies=5):
    devices = packets.shape[0]
    block = packets.shape[1:]
    half = -(-half_rows // (2 * LANES)) * LANES
    some = lambda dims: pl.BlockSpec((per,) + dims, lambda i, *s: (i, 0, 0))
    steps = devices // per
    mine = lambda pair: pl.BlockSpec((per,) + pair[0].shape[1:], lambda i, *s: (jnp.minimum(i, steps // 2 - 1), 0, 0))
    theirs = lambda pair: pl.BlockSpec((per,) + pair[0].shape[1:], lambda i, *s: (jnp.maximum(i - steps // 2, 0), 0, 0))
    return pl.pallas_call(
        partial(spread_kernel, rows, half_rows, feats, per, unroll, copies, at_early, at_early),
        out_shape=[pltpu.HBM((feats, half_rows), f32), pltpu.HBM((ROWS, LANES), f32)],
        grid_spec=pltpu.PrefetchScalarGridSpec(
            num_scalar_prefetch=2,
            grid=(steps,),
            in_specs=[number_block(per, count), some(block), mine(early), theirs(early), mine(late), theirs(late), mine(p_heads), theirs(p_heads)],
            out_specs=[pl.BlockSpec((feats, half_rows), lambda i, *s: (0, 0), pipeline_mode=pl.Buffered(1)), pl.BlockSpec((ROWS, LANES), lambda i, *s: (0, 0))],
            scratch_shapes=[pltpu.VMEM((half, LANES), f32)] * copies + [pltpu.VMEM((per * count, LANES), f32)],
        ),
        compiler_params=pltpu.CompilerParams(vmem_limit_bytes=52 * MIB),
        cost_estimate=pl.CostEstimate(flops=10**9, bytes_accessed=3 * 10**7, transcendentals=0),
        name="spread_tokens",
    )(where, firsts, numbers.reshape(-1, 1, per * count), packets, *early, *late, *p_heads)


def attend_kernel(rows, mats, xt, vec, moved, sent, heads_out, facts, y_out, probs_out, psum_out, normed_out, inv_out, *scratch):
    w = square_weights(mats, 0, *scratch, (0, 1, 2, 3))
    x1, x00, q, o, probs, psum, normed, inv, qk, y = attend(xt[...], w, vec[...], moved[...], rows)
    tiles = to_tiles(x1)
    halves = both_halves(qk, rows)
    wide = sent.shape[0]
    block = D // (2 * wide)
    for dest in range(wide):
        sent[dest] = jnp.concatenate([tiles, table_block(halves, dest, block)], 0).astype(bf16)
    heads_out[...] = pack_heads(probs.astype(bf16), rows)
    facts[...] = jnp.concatenate([to_tiles(value.astype(f32)) for value in (x00, q, o)], 0).astype(bf16)
    y_out[...] = y.astype(bf16)
    probs_out[...], psum_out[...], normed_out[...], inv_out[...] = probs, psum, normed, inv


def attend_back_kernel(rows, place, mats, got, d_res2, sums_up, normed, inv, probs, psum, xt, vec, late_out, last, z_out, *scratch):
    w = square_weights(mats, 0, *scratch, (3, 2, 1, 0))
    wide = late_out.shape[0]
    block = D // (2 * wide)
    feats = 2 * block
    dx1 = d_res2[pl.ds(pl.multiple_of(place[0] * ROWS, ROWS), ROWS), :]
    for k in range(wide):
        dx1 = dx1 + got[k].astype(f32)
    d_a, d_o, d_q, sums, vd, z, extra, ds = attend_back(
        dx1, normed[...], inv[...], probs[...], psum[...], xt[...], w, vec[...], rows
    )
    halves = both_halves(vd, rows)
    heads = pack_heads(ds, rows)
    gap = jnp.zeros((ROWS, LANES - feats), f32)
    for dest in range(wide):
        row_part = jnp.concatenate([extra[:, feats * dest : feats * (dest + 1)], gap], 1)
        late_out[dest] = jnp.concatenate([jnp.concatenate([table_block(halves, dest, block), row_part], 0).astype(bf16), heads], 0)
    z_out[...] = z.astype(bf16)
    sums = sums + [sums_up[...]]
    index = iota((ROWS, D), 0)
    spare = ROWS - rows
    values = [d_q.astype(f32), d_o.astype(f32), d_a.astype(f32)]
    for number, row in enumerate(sums):
        values[number // spare] = jnp.where(index == rows + number % spare, row, values[number // spare])
    last[...] = jnp.concatenate([to_tiles(value) for value in values], 0).astype(bf16)


def pack_kernel(rows, facts, last, y, z, d_up, d_up_other, out):
    wide = out.shape[0]
    block = d_up.shape[0] // wide
    hidden = d_up.shape[1] // 2
    values = jnp.concatenate([facts[...], last[...]], 0)
    halves_y, halves_z = both_halves(y[...], rows), both_halves(z[...], rows)
    up = d_up[...] + d_up_other[...].astype(f32)
    gap = jnp.zeros((block, LANES - hidden), f32)
    for dest in range(wide):
        mine = up[block * dest : block * (dest + 1), :]
        pieces = [jnp.concatenate([mine[:, k * hidden : (k + 1) * hidden], gap], 1) for k in range(2)]
        pieces += [weight_block(halves_y, dest, block, wide), weight_block(halves_z, dest, block, wide)]
        out[dest] = jnp.concatenate([values, jnp.concatenate(pieces, 0).astype(bf16)], 0)


def rows_of(own, other):
    return jnp.concatenate([from_tiles(own[...], 0), from_tiles(other[...], 0)], 0)


def ffn_kernel(x_own, w_up, w_down, bias, u_out, h_out, out):
    u, h, f = ffn(from_tiles(x_own[...], 0), w_up[...], w_down[...], bias[...])
    u_out[...], h_out[...] = u, h
    out[...] = f.astype(bf16)


def total_kernel(got, heads, out):
    total = got[0].astype(f32)
    for k in range(1, got.shape[0]):
        total = total + got[k].astype(f32)
    lines = jnp.concatenate([to_tiles(total).astype(bf16), heads[...]], 0)
    for k in range(out.shape[0]):
        out[k] = lines


def middle_kernel(mats, x_own, x_other, f_own, f_other, u, w_up, w_down, vec, picks, loss, pooled, d_c, d_res2, d_f, d_u, out, sums, sums_up, *scratch):
    get = square_weights(mats, 0, *scratch, (0,))
    w = lambda k: get(0)
    x1 = rows_of(x_own, x_other).astype(f32)
    f = rows_of(f_own, f_other).astype(f32)
    got = middle(x1, f, u[...], w_up[...], w_down[...], w, vec[...], picks[...])
    lines = u.shape[0]
    loss[...], pooled[...], d_c[...], d_res2[...] = got[:4]
    d_f[...], d_u[...] = got[4][:lines], got[5]
    out[...] = got[6].astype(bf16)
    sums[...] = stack_rows(got[7])
    su = jnp.sum(got[5].astype(f32), 0, keepdims=True)
    sums_up[...] = jnp.concatenate([su, jnp.zeros((1, D - su.shape[1]), f32)], 1)


def own_cols(device, block):
    index = iota((D, LANES), 1)
    return flag((iota((D, LANES), 0) == device * block + index) & (index < block)).astype(bf16)


def own_rows(left, right, mine, block):
    return dot(dot(left, mine).astype(bf16), right, 0, 0)[:block]


def ffn_grads_kernel(where, x_own, h, d_f, d_u, pooled, d_c, down_mine, down_theirs, d_head, up_mine, up_theirs):
    first = where[0] == 0
    hidden = down_mine.shape[0]
    half = up_mine.shape[0]
    d_up = dot(from_tiles(x_own[...], 0), d_u[...], 0, 0)
    up_mine[...] = jnp.where(first, d_up[:half], d_up[half:])
    up_theirs[...] = jnp.where(first, d_up[half:], d_up[:half]).astype(bf16)
    d_down = dot(h[...], d_f[...], 0, 0)
    down_mine[...] = jnp.where(first, d_down[:hidden], d_down[hidden:])
    down_theirs[...] = jnp.where(first, d_down[hidden:], d_down[:hidden]).astype(bf16)
    block = d_head.shape[0]
    d_head[...] = own_rows(pooled[...], d_c[...], own_cols(where[1], block), block)


def grads_kernel(rows, where, facts_own, facts_other, d_wh, down_mine, down_other, sums, square, in_out, out_out, up_out, down_out, vec_out, square_out, x00, q_all, o_all, d_q, d_o, d_a, y, z, wide_z):
    group, device = where[0], where[1]
    wide = facts_own.shape[0]
    devices = 2 * wide
    block = in_out.shape[0]
    hidden = FF // devices
    first = group == 0
    lines = ROWS * (D // LANES)
    at_up = 6 * lines
    for base, facts in ((0, facts_own), (1, facts_other)):
        at = slice(base * wide * ROWS, (base + 1) * wide * ROWS)
        for k, out in enumerate((x00, q_all, o_all, d_q, d_o, d_a)):
            out[at, :] = from_tiles(facts, k * lines).astype(f32)
        for n in range(wide):
            at = slice((base * wide + n) * block, (base * wide + n + 1) * block)
            y[at, :] = facts[n, at_up + 2 * block : at_up + 3 * block, :].astype(f32)
            z[at, :] = facts[n, at_up + 3 * block : at_up + 4 * block, :].astype(f32)
    for n in range(wide):
        for k in range(2):
            piece = facts_own[n, at_up + k * block : at_up + (k + 1) * block, :].astype(f32)
            at = (k * wide + n) * hidden
            up_out[:, at : at + hidden] = piece[:, :hidden]
    down_out[...] = down_mine[...] + down_other[...].astype(f32)

    def by_heads(source, values):
        total = jnp.zeros((block, D), f32)
        low = source[...].astype(bf16)
        for r in range(rows):
            wide_z[...] = dot(low, expand_table(rows, jnp.where(group == 0, 0, SIDE), r))
            for n in range(devices):
                total = total + wide_z[n * block : (n + 1) * block, :] * values[n * ROWS + r : n * ROWS + r + 1, :]
        return total

    d_wk = by_heads(z, q_all) * HEAD_DIM ** (-0.5)
    d_wv = by_heads(y, d_o)
    mine = own_cols(device, block)
    d_wq = own_rows(x00[...].astype(bf16), d_q[...].astype(bf16), mine, block)
    d_wo = own_rows(o_all[...].astype(bf16), d_a[...].astype(bf16), mine, block)
    square_now = square[...]

    def fold(square_now, value):
        tiles = value * value
        total = jnp.sum(tiles.reshape(tiles.shape[0] // ROWS, ROWS, tiles.shape[1]), 0)
        for k in range(total.shape[1] // LANES):
            square_now = square_now + total[:, k * LANES : (k + 1) * LANES]
        return square_now

    in_out[:, :D], in_out[:, D : 2 * D], in_out[:, 2 * D :] = d_wq, d_wk, d_wv
    out_out[...] = d_wo
    for value in (d_wq, d_wk, d_wv, d_wo, d_wh[...], up_out[...], down_out[...]):
        square_now = fold(square_now, value)
    spare = ROWS - rows
    grouped = [jnp.sum(t[...].reshape(devices, ROWS, D), 0) for t in (d_q, d_o)]
    tail = [grouped[k // spare][rows + k % spare : rows + k % spare + 1] for k in range(5)]
    mids = sums[...]
    pieces = [tail[0], mids[0:1], mids[1:2], tail[3], tail[4], tail[2], tail[1]] + [mids[k : k + 1] for k in range(2, 6)]
    index = iota((16, D), 0)
    total = jnp.zeros((16, D), f32)
    for number, row in enumerate(pieces):
        total = jnp.where(index == number, row, total)
    each = D // hidden
    for k in range(wide):
        lines_of = [(base * wide + k) * ROWS + rows + 5 % spare for base in range(2)]
        source = (d_q, d_o)[5 // spare]
        row = source[lines_of[0] : lines_of[0] + 1, :] + source[lines_of[1] : lines_of[1] + 1, :]
        for core in range(2):
            shift = (hidden * (k % each) - hidden * core) % D
            turned = pltpu.roll(row, shift, 1) if shift else row
            col = iota((1, D), 1)
            turned = jnp.where((col >= hidden * (k % each)) & (col < hidden * (k % each + 1)), turned, 0.0)
            total = total + jnp.where(index == 11 + (core * wide + k) // each, turned, 0.0)
    vec_out[...] = total
    square_now = square_now + fold(jnp.zeros((ROWS, LANES), f32), total) / devices
    for k in range(devices):
        square_out[k] = square_now


def adam_kernel(count, scales, weight, first, second, d_table, got, *refs):
    grads, state = refs[:count], refs[count : 4 * count]
    norm_out, factor_out = refs[4 * count : 4 * count + 2]
    outs = refs[4 * count + 2 : 7 * count + 2]
    far = refs[7 * count + 2 : 7 * count + 5]
    loads, stores, got_in, sent = refs[7 * count + 5 :]
    slots, lines = loads.shape[0], loads.shape[2]
    jobs = weight.shape[0] // lines
    sources = (weight, first, second, d_table)

    def load(j):
        return [pltpu.make_async_copy(ref.at[pl.ds(j * lines, lines), :], loads.at[j % slots, k], got_in.at[j % slots, k]) for k, ref in enumerate(sources)]

    def store(j):
        return [pltpu.make_async_copy(stores.at[j % slots, k], ref.at[pl.ds(j * lines, lines), :], sent.at[j % slots, k]) for k, ref in enumerate(far)]

    for j in range(min(slots, jobs)):
        for copy in load(j):
            copy.start()
    total = got[0]
    for k in range(1, got.shape[0]):
        total = total + got[k]
    total = jnp.sum(jnp.sum(total, 0, keepdims=True), 1, keepdims=True)
    norm = jnp.sqrt(total)
    factor = jnp.minimum(1.0, clip_level / (norm + 1e-06))
    norm_out[...], factor_out[...] = norm, factor
    one, two = scales[0], scales[1]
    for j in range(jobs):
        for copy in load(j):
            copy.wait()
        if j >= slots:
            for copy in store(j - slots):
                copy.wait()
        old = [loads[j % slots, k] for k in range(3)]
        new = update(*old, loads[j % slots, 3] * factor, RATES[0], one, two)
        for k in range(3):
            stores[j % slots, k] = new[k]
        for copy in store(j):
            copy.start()
        if j + slots < jobs:
            for copy in load(j + slots):
                copy.start()
    for number in range(count):
        old = [state[3 * number + k][...] for k in range(3)]
        new = update(*old, grads[number][...] * factor, RATES[number + 1], one, two)
        for k in range(3):
            outs[3 * number + k][...] = new[k]
    for j in range(max(0, jobs - slots), jobs):
        for copy in store(j):
            copy.wait()


def swap(x):
    return lax.ppermute(x, "group", [(0, 1), (1, 0)])


def exchange(x):
    return lax.all_to_all(x, "wide", split_axis=0, concat_axis=0, tiled=True)


def tie(*values):
    return lax.optimization_barrier(values)


def pair(x):
    own = exchange(x)
    return own, swap(own)


def in_order(own, other, group):
    return jnp.where(group == 0, jnp.concatenate([own, other], 0), jnp.concatenate([other, own], 0))


def plain_body(wide, passage_ids, query_ids, passage_len, query_len, positive, negatives, valid, step_count, *state):
    params, firsts, seconds = state[0::3], state[1::3], state[2::3]
    embedding, attn_in, attn_out, w_ffn_up, w_ffn_down, head, vectors = params
    group, place = lax.axis_index("group"), lax.axis_index("wide")
    device, devices = group * wide + place, 2 * wide
    feats, half_rows = embedding.shape
    block, hidden = D // devices, FF // devices
    pas_count, pas_len = passage_ids.shape
    qry_count, qry_len = query_ids.shape
    rows = pas_count + qry_count
    tokens = pas_count * pas_len + qry_count * qry_len
    live = rows * HEADS
    both = lambda x: jnp.concatenate(pair(x), 0)
    gather = lambda x: both(jnp.broadcast_to(x[None], (wide,) + x.shape))
    ids = jnp.concatenate([passage_ids.reshape(-1), query_ids.reshape(-1)])
    seq_np = np.concatenate([np.repeat(np.arange(pas_count), pas_len), pas_count + np.repeat(np.arange(qry_count), qry_len)])
    pos_np = np.concatenate([np.tile(np.arange(pas_len), pas_count), np.tile(np.arange(qry_len), qry_count)])
    lens = jnp.concatenate([jnp.repeat(passage_len, pas_len), jnp.repeat(query_len, qry_len)])
    moved = jnp.zeros((ROWS, tokens), f32).at[2].set(jnp.asarray(seq_np, f32)).at[3].set(jnp.asarray(pos_np == 0, f32))
    moved = moved.at[4].set(flag(jnp.asarray(pos_np) < lens))
    note = jnp.concatenate([ids, valid, positive, negatives.reshape(-1)])
    notes = gather(jnp.pad(note, (0, -note.shape[0] % LANES)).reshape(-1, LANES)).reshape(devices, -1)
    low_vectors = gather(jnp.pad(vectors.astype(bf16), (0, -vectors.shape[0] % LANES)).reshape(-1, LANES))
    vec = in_order(low_vectors[:wide], low_vectors[wide:], group).reshape(devices, -1)[:, : vectors.shape[0]].astype(f32).reshape(-1, D)
    all_ids = notes[:, :tokens]
    valid_rows = jnp.pad(notes[:, tokens : tokens + qry_count].astype(f32), ((0, 0), (pas_count, ROWS - rows))).reshape(-1, 1)
    at = tokens + qry_count
    picked = jnp.concatenate(
        [notes[:, at : at + qry_count, None], notes[:, at + qry_count : at + qry_count + negatives.size].reshape(devices, qry_count, -1)], 2
    )
    pick_dev = picked // pas_count
    pick_row = (((pick_dev // wide) ^ group) * wide + pick_dev % wide) * ROWS + picked % pas_count
    pick_rows = jnp.pad(pick_row, ((0, 0), (pas_count, ROWS - rows), (0, 0)), constant_values=-1).reshape(devices * ROWS, -1)
    mats = lax.all_gather(jnp.concatenate([attn_in, attn_out, head], 1).astype(bf16), ALL, axis=0, tiled=True)
    w = lambda k: mats[:, k * D : (k + 1) * D]
    w_up = lax.all_to_all(
        w_ffn_up.astype(bf16).reshape(block, devices, hidden).transpose(1, 0, 2), ALL, split_axis=0, concat_axis=0, tiled=True
    ).reshape(D, hidden)
    w_down = w_ffn_down.astype(bf16)
    bias_up = lax.dynamic_slice(vec.reshape(-1), (11 * D + device * hidden,), (hidden,))[None]
    local = all_ids - group * half_rows
    inside = ((local >= 0) & (local < half_rows)).reshape(1, -1)
    local = jnp.clip(local, 0, half_rows - 1).reshape(-1)
    looked = jnp.where(inside, jnp.take(embedding.astype(bf16), local, axis=1), jnp.zeros((), bf16))
    looked = looked.reshape(feats, devices, tokens).transpose(1, 0, 2)
    xt = exchange(looked[:wide] + swap(looked[wide:])).reshape(D, tokens)
    x1, x00, q, o, probs, psum, normed1, inv1, qk, y = attend(xt, w, vec, moved, rows)
    p_heads = dot(heads_table(rows), probs.astype(bf16)).astype(bf16)
    x1_all = gather(x1.astype(bf16)).reshape(devices * ROWS, D)

    def to_owner(parts):
        mine = parts[: wide * ROWS] + swap(parts[wide * ROWS :])
        return jnp.sum(exchange(mine.astype(bf16).reshape(wide, ROWS, D)).astype(f32), 0)

    u, h, f_part = ffn(x1_all, w_up, w_down, bias_up)
    f_all = gather(to_owner(f_part).astype(bf16)).reshape(devices * ROWS, D).astype(f32)
    loss, pooled, d_c, d_res2, d_f, d_u, d_x1, sums = middle(x1_all.astype(f32), f_all, u, w_up, w_down, w, vec, jnp.concatenate([valid_rows.astype(jnp.int32), pick_rows], 1))
    d_x1 = lax.dynamic_slice(d_res2, (place * ROWS, 0), (ROWS, D)) + to_owner(d_x1)
    d_a, d_o, d_q, sums_back, vd, z, extra, ds = attend_back(d_x1, normed1, inv1, probs, psum, xt, w, vec, rows)

    to_features = lambda t: both(t.T.astype(bf16).reshape(wide, feats, -1))

    def to_blocks(t):
        parts = t.T.astype(bf16).reshape(2, wide, block, -1).transpose(1, 0, 2, 3).reshape(wide, 2 * block, -1)
        got = both(parts).reshape(devices, 2, block, -1)
        return lax.dynamic_index_in_dim(got, group, 1, keepdims=False)[:, :, :live].reshape(devices, block, rows, HEADS)

    facts = gather(jnp.concatenate([x00, q, o, d_q, d_o, d_a], 0)).reshape(devices, 6, ROWS, D)
    flat_fact = lambda k: facts[:, k].reshape(devices * ROWS, D)
    by_head = lambda k: facts[:, k].reshape(devices, ROWS, HEADS, HEAD_DIM)[:, :rows]
    cut = lambda m: lax.dynamic_slice(m, (0, device * block), (devices * ROWS, block))
    d_wq = dot(cut(flat_fact(0)), flat_fact(3), 0, 0)
    d_wk = jnp.einsum("nfrh,nrhd->fhd", to_blocks(z), by_head(1), preferred_element_type=f32).reshape(block, D) * HEAD_DIM ** (-0.5)
    d_wv = jnp.einsum("nfrh,nrhd->fhd", to_blocks(y), by_head(4), preferred_element_type=f32).reshape(block, D)
    d_wo = dot(cut(flat_fact(2)), flat_fact(5), 0, 0)
    d_wup = dot(x1_all, d_u, 0, 0).astype(bf16).reshape(devices, block, hidden)
    d_wup = lax.all_to_all(d_wup, ALL, split_axis=0, concat_axis=0, tiled=True).astype(f32).transpose(1, 0, 2).reshape(block, FF)
    sums_up = jnp.pad(jnp.sum(d_u.astype(f32), 0, keepdims=True), ((0, 0), (0, D - hidden)))
    tails = gather(stack_rows(sums_back + [sums_up]))
    tail = jnp.sum(tails, 0)
    ups = in_order(tails[:wide], tails[wide:], group)[:, 5, :hidden].reshape(-1)
    mids = [row[0] for row in sums]
    d_vec = jnp.concatenate([tail[0], mids[0], mids[1], tail[3], tail[4], tail[2], tail[1]] + mids[2:] + [ups])
    d_vec = lax.dynamic_slice(d_vec, (device * vectors.shape[0],), vectors.shape)
    basis = jnp.concatenate([to_features(qk), to_features(vd), to_features(extra)], 2)
    lanes = gather(jnp.concatenate([dot(heads_table(rows), ds).astype(bf16), p_heads], 0))
    seq = jnp.asarray(seq_np, jnp.int32)[None]
    here = sequence_of(iota((SIDE, 1), 0), rows) == seq
    widen = lambda t: jnp.where(here[None], jnp.einsum("ha,nht->nat", heads_table(rows), t, preferred_element_type=f32), 0.0).astype(bf16)
    first = ((iota((ROWS, 1), 0) == seq) & jnp.asarray(pos_np == 0)[None]).astype(bf16)
    coef = jnp.concatenate([widen(lanes[:, :16]), widen(lanes[:, 16:]), jnp.broadcast_to(first[None], (devices,) + first.shape)], 1)
    d_tok = jnp.einsum("nfa,nat->fnt", basis, coef, preferred_element_type=f32).reshape(feats, -1)
    d_table = jnp.zeros((feats, half_rows), f32).at[:, local].add(jnp.where(inside, d_tok, 0.0))
    d_head = dot(cut(pooled), d_c, 0, 0)
    grads = (d_table, jnp.concatenate([d_wq, d_wk, d_wv], 1), d_wo, d_wup, dot(h, d_f, 0, 0), d_head, d_vec)
    squares = sum(jnp.sum(g * g) for g in grads)
    grad_norm = jnp.sqrt(jnp.sum(gather(jnp.full((ROWS, LANES), squares))[:, 0, 0]))
    factor = jnp.minimum(1.0, clip_level / (grad_norm + 1e-06))
    step_float = step_count[0].astype(f32)
    one, two = 1.0 / (1.0 - jnp.power(0.9, step_float)), 1.0 / (1.0 - jnp.power(0.999, step_float))
    new = [update(params[k], firsts[k], seconds[k], grads[k] * factor, RATES[k], one, two) for k in range(7)]
    return (loss[0, 0], grad_norm) + tuple(t for group_of in new for t in group_of)


def body(wide, passage_ids, query_ids, passage_len, query_len, positive, negatives, valid, step_count, *state):
    embedding, attn_in, attn_out, w_ffn_up, w_ffn_down, head, vectors = state[0::3]
    group = lax.axis_index("group")
    place = lax.axis_index("wide")
    device = group * wide + place
    devices = 2 * wide
    feats, half_rows = embedding.shape
    block = D // devices
    hidden = FF // devices
    pas_count, pas_len = passage_ids.shape
    qry_count, qry_len = query_ids.shape
    rows = pas_count + qry_count
    tokens = pas_count * pas_len + qry_count * qry_len
    chunks = tokens // LANES
    half = -(-half_rows // (2 * LANES)) * LANES
    where = jnp.stack([group, device]).astype(jnp.int32)
    place_at = place.astype(jnp.int32)[None]
    lines = wide * ROWS

    seq_np = np.concatenate([np.repeat(np.arange(pas_count), pas_len), pas_count + np.repeat(np.arange(qry_count), qry_len)])
    pos_np = np.concatenate([np.tile(np.arange(pas_len), pas_count), np.tile(np.arange(qry_len), qry_count)])
    vec_lines = -(-vectors.shape[0] // LANES)
    packet_lines = -(-(3 * chunks + 1 + vec_lines) // ROWS) * ROWS + 2 * block
    at_note = 3 * chunks
    pieces = [passage_ids.reshape(-1), query_ids.reshape(-1), passage_len, query_len, valid, positive, negatives.reshape(-1)]
    size = sum(t.shape[0] for t in pieces)
    assert size < tokens + LANES
    base = jnp.concatenate(pieces + [jnp.zeros((-size % (ROWS * LANES),), jnp.int32)]).reshape(-1, LANES)
    vec_pad = jnp.concatenate([vectors, jnp.zeros((-vectors.shape[0] % LANES,), f32)]).reshape(-1, LANES)
    packet, moved = call(
        partial(prepare_kernel, half_rows, tokens, rows),
        [shape((wide, packet_lines, LANES), bf16), shape((ROWS, tokens))],
        base, vec_pad, jnp.asarray(seq_np, jnp.int32)[None], jnp.asarray(pos_np, jnp.int32)[None], w_ffn_up,
        near_outs=(0,), name="prepare",
    )
    packet_own = exchange(packet)
    (table,) = call(build_kernel, [shape((half, LANES))], embedding, name="build", flops=10**8)
    packet_own, table = tie(packet_own, table)
    packet_other = swap(packet_own)
    low_mats, low_head = call(cast_kernel, [shape((block, 4 * D), bf16), shape((block, D), bf16)], attn_in, attn_out, head, near_outs=(0, 1), name="cast")
    mats = lax.all_gather(low_mats, ALL, axis=0, tiled=True)
    w_head = lax.all_gather(low_head, ALL, axis=0, tiled=True)
    down_low = w_ffn_down.astype(bf16)
    w_down = in_order(down_low, swap(down_low), group)

    def numbers_of(packets):
        ids = packets[:, :chunks].astype(f32) * 256.0 + packets[:, chunks : 2 * chunks].astype(f32)
        local = ids - (group * half_rows).astype(f32)
        row_at = jnp.clip(jnp.where(local >= half, local - half, local), 0, half - 1)
        first = packets[:, at_note, 0].astype(f32) + 256.0 * packets[:, at_note, LANES - 1].astype(f32)
        return row_at.astype(jnp.int32).reshape(-1), first.astype(jnp.int32)

    look = partial(lookup, half_rows=half_rows, feats=feats, count=tokens)
    num_own, num_other = numbers_of(packet_own), numbers_of(packet_other)
    theirs = look(where, *num_other, packet_other, table)
    xt = exchange(look(where, *num_own, packet_own, table, add=swap(theirs))).reshape(D, tokens)
    numbers = jnp.concatenate([num_own[0], num_other[0]])
    firsts = jnp.concatenate([num_own[1], num_other[1]])
    packets = jnp.concatenate([packet_own, packet_other], 0)
    ordered = in_order(packet_own, packet_other, group)
    w_up = ordered[:, packet_lines - 2 * block :, :hidden].reshape(devices, 2, block, hidden).transpose(0, 2, 1, 3).reshape(D, 2 * hidden)
    vec = ordered[:, at_note + 1 : at_note + 1 + vec_lines].astype(f32).reshape(devices, -1)
    vec = vec[:, : vectors.shape[0]].reshape(-1, D)
    bias_all = vec[11:].reshape(2, wide, hidden)
    bias_up = lax.dynamic_slice(bias_all, (0, place, 0), (2, 1, hidden)).reshape(1, 2 * hidden)
    notes = packets[:, at_note].astype(f32)
    at = 1 + qry_count
    picked = jnp.concatenate(
        [notes[:, at : at + qry_count, None], notes[:, at + qry_count : at + qry_count + negatives.size].reshape(devices, qry_count, -1)], 2
    ).astype(jnp.int32)
    pick_dev = picked // pas_count
    pick_row = (((pick_dev // wide) ^ group) * wide + pick_dev % wide) * ROWS + picked % pas_count
    pick_row = jnp.concatenate([notes[:, 1 : 1 + qry_count, None].astype(jnp.int32), pick_row], 2)
    pick_rows = jnp.pad(pick_row, ((0, 0), (pas_count, ROWS - rows), (0, 0))).reshape(devices * ROWS, -1)

    xt, vec, bias_up, pick_rows, w_up, w_down, packets, numbers, firsts = tie(
        xt, vec, bias_up, pick_rows, w_up, w_down, packets, numbers, firsts
    )
    tile_lines = ROWS * (D // LANES)
    heads_at, units = head_lines(chunks), 2 * hidden
    sent, p_heads, facts, y, probs, psum, normed1, inv1 = call(
        partial(attend_kernel, rows),
        [
            shape((wide, tile_lines + block, LANES), bf16), shape((heads_at, LANES), bf16), shape((3 * tile_lines, LANES), bf16),
            shape((SIDE, D), bf16), shape((SIDE, tokens)), shape((SIDE, 1)), shape((ROWS, D)), shape((ROWS, 1)),
        ],
        xt, vec, moved,
        far=(mats,), near=(0,), near_outs=(0,), scratch=weight_scratch(4), name="attend", flops=10**9,
    )
    x_own, x_other = pair(sent)
    u, h, f_mine = call(
        ffn_kernel, [shape((lines, units)), shape((lines, units), bf16), shape((lines, D), bf16)], x_own, w_up, w_down, bias_up,
        near=(0,), near_outs=(2,), name="ffn", flops=10**8, vmem=16,
    )
    f_parts = exchange(f_mine.reshape(wide, ROWS, D))
    (f_sum,) = call(total_kernel, [shape((wide, tile_lines + heads_at, LANES), bf16)], f_parts, p_heads, near=(0,), near_outs=(0,), name="total")
    f_own, f_other = pair(f_sum)
    loss, pooled, d_c, d_res2, d_f, d_u, d_sum, sums, sums_up = call(
        middle_kernel,
        [
            shape((1, 1)), shape((devices * ROWS, D), bf16), shape((devices * ROWS, D), bf16), shape((devices * ROWS, D)),
            shape((lines, D), bf16), shape((lines, units), bf16), shape((lines, D), bf16), shape((ROWS, D)), shape((1, D)),
        ],
        x_own, x_other, f_own, f_other, u, w_up, w_down, vec, pick_rows,
        far=(w_head,), scratch=weight_scratch(1), near=(0, 1, 2, 3), near_outs=(6,), name="middle", flops=10**9, vmem=32,
    )
    got = exchange(d_sum.reshape(wide, ROWS, D))
    down_mine, down_theirs, d_whead, up_mine, up_theirs = call(
        ffn_grads_kernel,
        [shape((hidden, D)), shape((hidden, D), bf16), shape((block, D)), shape((D // 2, units)), shape((D // 2, units), bf16)],
        x_own, h, d_f, d_u, pooled, d_c,
        scalars=(where,), after=(d_sum,), near=(0,), name="ffn_grads", flops=10**8,
    )
    late, last, z = call(
        partial(attend_back_kernel, rows),
        [shape((wide, block + ROWS + heads_at, LANES), bf16), shape((3 * tile_lines, LANES), bf16), shape((SIDE, D), bf16)],
        got, d_res2, sums_up, normed1, inv1, probs, psum, xt, vec,
        scalars=(place_at,), far=(mats,), after=(up_mine,), near=(0,), near_outs=(0,), scratch=weight_scratch(4), name="attend_back", flops=10**9,
    )
    late_own, late_other = pair(late)
    (packed,) = call(
        partial(pack_kernel, rows), [shape((wide, 6 * tile_lines + 4 * block, LANES), bf16)], facts, last, y, z, up_mine, swap(up_theirs),
        after=(late,), near_outs=(0,), name="pack",
    )
    piece = packed[:1, :ROWS] + late_own[:1, :ROWS] * jnp.zeros((), bf16)
    last_own = exchange(lax.dynamic_update_slice(packed, piece, (0, 0, 0)))
    d_table, square = spread_tokens(
        where, numbers, firsts, packets, (x_own, x_other), (late_own, late_other), (f_own, f_other), tile_lines, rows, half_rows, feats, tokens
    )
    piece = last_own[:1, :ROWS] + (square[None] * 0.0).astype(bf16)
    last_own = lax.dynamic_update_slice(last_own, piece, (0, 0, 0))
    last_other = swap(last_own)
    d_attn_in, d_wo, d_wup, d_down, d_vec, squares = call(
        partial(grads_kernel, rows),
        [shape((block, 3 * D)), shape((block, D)), shape((block, FF)), shape((hidden, D)), shape((16, D)), shape((devices, ROWS, LANES))],
        last_own, last_other, d_whead, down_mine, swap(down_theirs), sums, square,
        scalars=(where,),
        scratch=[pltpu.VMEM((devices * ROWS, D), f32)] * 6 + [pltpu.VMEM((D, LANES), f32)] * 2 + [pltpu.VMEM((D, D), f32)],
        near=(0, 1), near_outs=(5,), name="grads", flops=10**9, vmem=32,
    )
    squares_got = lax.all_to_all(squares, ALL, split_axis=0, concat_axis=0, tiled=True)
    d_vectors = lax.dynamic_slice(d_vec.reshape(-1), (device * vectors.shape[0],), vectors.shape)
    step_float = step_count[0].astype(f32)
    scales = jnp.stack([1.0 / (1.0 - jnp.power(0.9, step_float)), 1.0 / (1.0 - jnp.power(0.999, step_float))])
    grads = (d_attn_in, d_wo, d_wup, d_down, d_whead)
    middle_state = state[3:18]
    slots, step_rows = 3, ROWS
    norm, factor, *new = call(
        partial(adam_kernel, len(grads)),
        [shape((1, 1)), shape((1, 1))] + [shape(t.shape) for t in middle_state],
        squares_got, *grads, *middle_state,
        scalars=(scales,), far=(*state[:3], d_table), far_outs=[shape(embedding.shape)] * 3,
        scratch=[
            pltpu.VMEM((slots, 4, step_rows, half_rows), f32), pltpu.VMEM((slots, 3, step_rows, half_rows), f32),
            pltpu.SemaphoreType.DMA((slots, 4)), pltpu.SemaphoreType.DMA((slots, 3)),
        ],
        near=(0,), name="adam", vmem=40,
    )
    new_vectors = update(*state[18:], d_vectors * factor[0, 0], RATES[6], scales[0], scales[1])
    return (loss[0, 0], norm[0, 0]) + tuple(new[15:]) + tuple(new[:15]) + new_vectors


def solution(mesh):
    split_rows = P(ALL, None)
    flat = P(ALL)
    table = P("wide", "group")
    mats = (table,) * 3 + (split_rows,) * 15 + (flat,) * 3
    in_specs = (split_rows, split_rows, flat, flat, flat, split_rows, flat, P()) + mats
    wide = mesh.shape["wide"]
    thick = D % (2 * wide * ROWS) == 0 and wide * ROWS <= LANES
    return jax.shard_map(
        partial(body if thick else plain_body, wide), mesh=mesh, in_specs=in_specs, out_specs=(P(), P()) + mats, check_vma=False
    )
```

```python
from functools import partial

import jax
import jax.numpy as jnp
import numpy as np
from jax import lax
from jax.experimental import pallas as pl
from jax.experimental.pallas import tpu as pltpu
from jax.sharding import PartitionSpec as P

D = 768
HEADS = 12
HEAD_DIM = 64
FF = 3072
ROWS = 8
LANES = 128
SIDE = 64
STEP = 16
ALL = ("group", "wide")
clip_level = 0.02
f32 = jnp.float32
bf16 = jnp.bfloat16
RATES = (0.5, 0.5 * D**-0.5, 0.5 * (D // 16) ** -0.5, 0.5 * D**-0.5, 0.5 * FF**-0.5, 0.5 * D**-0.5, 0.2)


def dot(a, b, ca=1, cb=0):
    return lax.dot_general(a, b, (((ca,), (cb,)), ((), ())), preferred_element_type=f32)


def split(x):
    high = x.astype(bf16)
    return high, (x - high.astype(f32)).astype(bf16)


def dot_split(x, w, cb=0):
    high, rest = split(x)
    return dot(high, w, 1, cb) + dot(rest, w, 1, cb)


def iota(shape, dim):
    return lax.broadcasted_iota(jnp.int32, shape, dim)


def stack_rows(rows):
    index = iota((ROWS, rows[0].shape[1]), 0)
    total = jnp.zeros(index.shape, f32)
    for number, row in enumerate(rows):
        total = jnp.where(index == number, row, total)
    return total


def layer_norm(resid):
    centred = resid - jnp.mean(resid, -1, keepdims=True)
    inv_std = lax.rsqrt(jnp.mean(centred * centred, -1, keepdims=True) + 1e-05)
    return centred * inv_std, inv_std


def norm_back(grad_out, normed, inv_std, gain):
    scaled = grad_out * gain
    return inv_std * (
        scaled
        - jnp.mean(scaled, -1, keepdims=True)
        - normed * jnp.mean(scaled * normed, -1, keepdims=True)
    )


def flag(condition):
    return jnp.where(condition, 1.0, 0.0)


def sequence_of(a, rows):
    assert HEADS == 12
    return jnp.where((a >= 0) & (a < rows * HEADS), lax.shift_right_logical(a * 43, 9), 99)


def head_of(a, rows):
    return a - HEADS * sequence_of(a, rows)


def spread_table(rows):
    return flag(sequence_of(iota((SIDE, ROWS), 0), rows) == iota((SIDE, ROWS), 1)).astype(bf16)


def column_table(rows):
    return flag(head_of(iota((SIDE, D), 0), rows) == lax.shift_right_logical(iota((SIDE, D), 1), 6))


def heads_table(rows):
    return flag(head_of(iota((16, SIDE), 1), rows) == iota((16, SIDE), 0)).astype(bf16)


def place_table(rows, first):
    a = iota((LANES, SIDE), 1)
    return flag((iota((LANES, SIDE), 0) == first + a) & (a < rows * HEADS)).astype(bf16)


def expand_table(rows, first, r):
    return flag(iota((LANES, D), 0) == first + r * HEADS + lax.shift_right_logical(iota((LANES, D), 1), 6)).astype(bf16)


def prepare(ids, live, seq, pos, group_rows):
    count = ids.shape[1]
    first = jnp.where(ids < group_rows, 1.0, 0.0)
    high = lax.shift_right_logical(ids, 8)
    index = iota((ROWS, count), 0)
    values = jnp.zeros((ROWS, count), f32)
    pieces = (high.astype(f32), (ids - high * 256).astype(f32), seq.astype(f32), jnp.where(pos == 0, 1.0, 0.0), live)
    for number, row in enumerate(pieces):
        values = jnp.where(index == number, row, values)
    left, right = iota((count, count), 0), iota((count, count), 1)
    ahead = jnp.where(right < left, 1.0, 0.0).astype(bf16)
    same = jnp.where(right == left, 1.0, 0.0).astype(bf16)
    marks = jnp.broadcast_to(first, (ROWS, count)).astype(bf16)
    before = dot(ahead, marks, 1, 1)[:, :1]
    mine = dot(same, marks, 1, 1)[:, :1]
    total = jnp.sum(first, 1, keepdims=True)
    target = jnp.where(mine > 0.5, before, total + iota((count, 1), 0).astype(f32) - before)
    moves = jnp.where(target.astype(jnp.int32) == right, 1.0, 0.0).astype(bf16)
    return dot(values.astype(bf16), moves), total


def attend(xt, w, vec, moved, rows):
    g1, bq, bv, bo, be1 = vec[0:1], vec[3:4], vec[4:5], vec[5:6], vec[6:7]
    seq_id, slot0, live = moved[2:3], moved[3:4], moved[4:5]
    spread, columns = spread_table(rows), column_table(rows)
    index = iota((ROWS, xt.shape[1]), 0).astype(f32)
    pick0 = flag((index == seq_id) & (slot0 > 0.5)).astype(bf16)
    x00 = dot(pick0, xt, 1, 1)
    q = (dot(x00.astype(bf16), w(0)) + bq).astype(bf16)
    q_wide = (dot(spread, q) * columns).astype(bf16)
    qk = dot(q_wide, w(1), 1, 1) * HEAD_DIM ** (-0.5)
    mask = (sequence_of(iota((SIDE, 1), 0), rows).astype(f32) == seq_id) & (live > 0.5)
    scores = jnp.where(mask, dot_split(qk, xt), -1e30)
    raw = jnp.where(mask, jnp.exp(scores - jnp.max(scores, 1, keepdims=True)), 0.0)
    total = jnp.sum(raw, 1, keepdims=True)
    probs = raw / jnp.where(total > 0.0, total, 1.0)
    probs_low = probs.astype(bf16)
    y = dot(probs_low, xt, 1, 1)
    psum = jnp.sum(probs_low.astype(f32), 1, keepdims=True)
    mixed = dot_split(y, w(2)) + psum * bv
    o = dot(spread, (mixed * columns).astype(bf16), 0, 0).astype(bf16)
    normed, inv = layer_norm(x00 + dot(o, w(3)) + bo)
    return normed * g1 + be1, x00.astype(bf16), q, o, probs, psum, normed, inv, qk, y


def attend_back(dx1, normed, inv, probs, psum, xt, w, vec, rows):
    g1, bv = vec[0:1], vec[4:5]
    spread, columns = spread_table(rows), column_table(rows)
    d_res = norm_back(dx1, normed, inv, g1)
    d_a = d_res.astype(bf16)
    d_o = dot(d_a, w(3), 1, 1).astype(bf16)
    d_o_wide = dot(spread, d_o) * columns
    vd = dot(d_o_wide.astype(bf16), w(2), 1, 1)
    dp = dot_split(vd, xt) + jnp.sum(d_o_wide * bv, 1, keepdims=True)
    ds = (probs * (dp - jnp.sum(probs * dp, 1, keepdims=True))).astype(bf16)
    z = dot(ds, xt, 1, 1)
    zw = dot_split(z, w(1)) * (HEAD_DIM ** (-0.5)) * columns
    d_q = dot(spread, zw.astype(bf16), 0, 0).astype(bf16)
    extra = d_res + dot(d_q, w(0), 1, 1)
    sums = [
        jnp.sum(dx1 * normed, 0, keepdims=True),
        jnp.sum(dx1, 0, keepdims=True),
        jnp.sum(d_a.astype(f32), 0, keepdims=True),
        jnp.sum(d_q.astype(f32), 0, keepdims=True),
        jnp.sum(d_o_wide * psum, 0, keepdims=True),
    ]
    return d_a, d_o, d_q, sums, vd, z, extra, ds


def both_halves(value, rows):
    low = value.astype(bf16)
    return dot(place_table(rows, 0), low).T, dot(place_table(rows, SIDE), low).T


def table_block(halves, dest, block):
    first = 2 * block * dest
    return halves[0][first : first + block] + halves[1][first + block : first + 2 * block]


def weight_block(halves, dest, block, wide):
    return halves[0][block * dest : block * (dest + 1)] + halves[1][block * (wide + dest) : block * (wide + dest + 1)]


HEAD_LINES = 8


def pack_heads(value, rows):
    row, head = iota((HEAD_LINES, SIDE), 0), head_of(iota((HEAD_LINES, SIDE), 1), rows)
    most = dot(flag(row == head).astype(bf16), value)
    rest = [dot(flag((row - 4 * k + 8 == head) & (head >= 8) & (head < HEADS)).astype(bf16), value) for k in range(2)]
    cut = lambda t, k: t[:, k * LANES : (k + 1) * LANES]
    chunks = value.shape[1] // LANES
    tiles = [cut(most, k) for k in range(chunks)]
    for k in range(0, chunks, 2):
        tiles.append(cut(rest[0], k) + cut(rest[1], k + 1) if k + 1 < chunks else cut(rest[0], k))
    return jnp.concatenate(tiles, 0).astype(bf16)


def unpack_heads(lines, chunks):
    tile = lambda k: lines[k * HEAD_LINES : (k + 1) * HEAD_LINES].astype(f32)
    most = jnp.concatenate([tile(k) for k in range(chunks)], 1)
    rest = []
    for k in range(chunks):
        value = tile(chunks + k // 2)
        rest.append(pltpu.roll(value, 4, 0) if k % 2 else value)
    rest = jnp.concatenate(rest, 1)
    return jnp.concatenate([most, jnp.where(iota(rest.shape, 0) < HEADS - 8, rest, 0.0)], 0)


def head_lines(chunks):
    return HEAD_LINES * (chunks + (chunks + 1) // 2)


def to_tiles(value):
    return jnp.concatenate([value[:, k : k + LANES] for k in range(0, value.shape[1], LANES)], 0)


def from_tiles(got, first, lines=ROWS):
    pieces = [got[:, first + k * lines : first + (k + 1) * lines, :] for k in range(D // LANES)]
    return jnp.concatenate([p.reshape(-1, LANES) for p in pieces], 1)


def ffn(x1, w_up, w_down, bias):
    u = dot(x1.astype(bf16), w_up) + bias
    h = (0.5 * u * (1.0 + lax.erf(u * 0.5**0.5))).astype(bf16)
    return u, h, dot(h, w_down)


def middle(x1, f, u, w_up, w_down, w, vec, picks):
    g2, gc, b2, be2, bc, bec = vec[1:2], vec[2:3], vec[7:8], vec[8:9], vec[9:10], vec[10:11]
    count = x1.shape[0]
    valid, picks = picks[:, :1].astype(f32), picks[:, 1:]
    normed2, inv2 = layer_norm(x1 + (f + b2))
    pooled = (normed2 * g2 + be2).astype(bf16)
    normed_c, inv_c = layer_norm(dot(pooled, w(4)) + bc)
    e = (normed_c * gc + bec).astype(bf16)
    scores = dot(e, e, 1, 1) * D ** (-0.5)
    col = iota((count, count), 1)
    is_pos = jnp.where(col == picks[:, 0:1], 1.0, 0.0)
    negs = jnp.zeros_like(is_pos)
    for number in range(1, picks.shape[1]):
        negs = negs + jnp.where(col == picks[:, number : number + 1], 1.0, 0.0)
    taken = (is_pos + negs) > 0.0
    top = jnp.max(jnp.where(taken, scores, -1e30), 1, keepdims=True)
    raw = jnp.where(taken, jnp.exp(scores - top), 0.0)
    total = jnp.sum(raw * (is_pos + negs), 1, keepdims=True)
    total = jnp.where(total > 0.0, total, 1.0)
    share = raw / total
    valid_count = jnp.sum(valid, 0, keepdims=True)
    per_query = top + jnp.log(total) - jnp.sum(is_pos * scores, 1, keepdims=True)
    loss = jnp.sum(jnp.where(valid > 0.0, valid * per_query, 0.0), 0, keepdims=True) / valid_count
    weight = valid / valid_count
    d_pos = (weight * (share - 1.0)).astype(bf16).astype(f32)
    d_neg = (weight * share).astype(bf16).astype(f32)
    d_scores = d_pos * is_pos + d_neg * negs
    high, rest = split(d_scores)
    d_e = (dot(high, e) + dot(rest, e) + dot(high, e, 0, 0) + dot(rest, e, 0, 0)) * D ** (-0.5)
    d_c = norm_back(d_e, normed_c, inv_c, gc).astype(bf16)
    d_x2 = dot(d_c, w(4), 1, 1)
    d_res2 = norm_back(d_x2, normed2, inv2, g2)
    d_f = d_res2.astype(bf16)
    lines = u.shape[0]
    d_h = dot(d_f[:lines], w_down, 1, 1)
    slope = 0.5 * (1.0 + lax.erf(u * 0.5**0.5)) + u * jnp.exp(-0.5 * u * u) * (2.0 * np.pi) ** (-0.5)
    d_u = (d_h * slope).astype(bf16)
    d_x1 = dot(d_u, w_up, 1, 1)
    sums = [
        jnp.sum(d_x2 * normed2, 0, keepdims=True),
        jnp.sum(d_e * normed_c, 0, keepdims=True),
        jnp.sum(d_f.astype(f32), 0, keepdims=True),
        jnp.sum(d_x2, 0, keepdims=True),
        jnp.sum(d_c.astype(f32), 0, keepdims=True),
        jnp.sum(d_e, 0, keepdims=True),
    ]
    return loss, pooled, d_c, d_res2, d_f, d_u, d_x1, sums


def update(weight, first, second, gradient, rate, scale_one, scale_two):
    first_new = 0.9 * first + 0.1 * gradient
    second_new = 0.999 * second + 0.001 * gradient * gradient
    first_hat = first_new * scale_one
    second_hat = second_new * scale_two
    return weight - rate * (first_hat / (jnp.sqrt(second_hat) + 1e-08) + 0.01 * weight), first_new, second_new


def shape(dims, kind=f32):
    return jax.ShapeDtypeStruct(dims, kind)


MIB = 1 << 20


def full_block(dims):
    return pl.BlockSpec(dims, lambda i: (0,) * len(dims), pipeline_mode=pl.Buffered(1))


def pinned(x):
    return pltpu.with_memory_space_constraint(x, pltpu.HBM)


def call(kernel, outs, *args, scalars=(), far=(), far_outs=(), after=(), near=(), near_outs=(), scratch=(), vmem=24, name=None, flops=0):
    anywhere = pl.BlockSpec(memory_space=pl.ANY)
    in_specs = [pl.BlockSpec(memory_space=pltpu.SMEM)] * len(scalars) + [anywhere] * len(far)
    in_specs += [full_block(a.shape) for a in args] + [anywhere] * len(after)
    moved = sum(int(np.prod(a.shape)) * a.dtype.itemsize for a in list(args) + list(far) + list(outs) + list(far_outs))
    used = len(scalars) + len(far) + len(args)

    def run(*refs):
        kernel(*refs[:used], *refs[used + len(after) :])

    shapes = [o if k in near_outs else pltpu.HBM(o.shape, o.dtype) for k, o in enumerate(outs)]
    shapes += [pltpu.HBM(o.shape, o.dtype) for o in far_outs]
    args = [a if k in near else pinned(a) for k, a in enumerate(args)]
    return pl.pallas_call(
        run,
        grid=(1,),
        out_shape=shapes,
        in_specs=in_specs,
        out_specs=[full_block(o.shape) for o in outs] + [anywhere] * len(far_outs),
        scratch_shapes=list(scratch),
        compiler_params=pltpu.CompilerParams(vmem_limit_bytes=vmem * MIB),
        cost_estimate=pl.CostEstimate(flops=int(flops), bytes_accessed=moved, transcendentals=0),
        name=name,
    )(*scalars, *(pinned(a) for a in far), *args, *after)


def once(x, other):
    anywhere = pl.BlockSpec(memory_space=pl.ANY)
    return pl.pallas_call(
        lambda *refs: None,
        out_shape=pltpu.HBM(x.shape, x.dtype),
        in_specs=[anywhere, anywhere],
        out_specs=anywhere,
        input_output_aliases={0: 0},
        compiler_params=pltpu.CompilerParams(vmem_limit_bytes=MIB),
        name="once",
    )(pinned(x), other)


def square_weights(mats, first, buffers, signals, order):
    copies = {
        k: pltpu.make_async_copy(mats.at[:, pl.ds(k * D, D)], buffers.at[k - first], signals.at[k - first]) for k in order
    }
    for k in order:
        copies[k].start()
    ready = {}

    def get(k):
        if k not in ready:
            copies[k].wait()
            ready[k] = buffers[k - first]
        return ready[k]

    return get


def weight_scratch(count):
    return [pltpu.VMEM((count, D, D), bf16), pltpu.SemaphoreType.DMA((count,))]


def prepare_kernel(group_rows, rows, passages, queries, negatives, small, vectors, seq, pos, up, packet, moved):
    line_up = lambda ref: [ref[k : k + 1, :] for k in range(ref.shape[0])]
    ids = jnp.concatenate(line_up(passages) + line_up(queries), 1)
    count = ids.shape[1]
    chunks = count // LANES
    entries = small[...]
    live = jnp.zeros((1, count), f32)
    for number in range(rows):
        live = jnp.where((seq[...] == number) & (pos[...] < entries[:, number : number + 1]), 1.0, live)
    got, total = prepare(ids, live, seq[...], pos[...], group_rows)
    moved[...] = got
    code = got[2:3] + 8.0 * got[3:4]
    lane = iota((1, LANES), 1)
    at = 1 + 2 * queries.shape[0]
    after = LANES - at - negatives.shape[0] * negatives.shape[1]
    rest = [jnp.zeros((1, at), jnp.int32)] + line_up(negatives) + [jnp.zeros((1, after), jnp.int32)]
    note = pltpu.roll(entries.astype(f32), LANES - rows + 1, 1)
    note = jnp.where((lane < at) | (lane == LANES - 1), note, jnp.concatenate(rest, 1).astype(f32))
    high = lax.shift_right_logical(total.astype(jnp.int32), 8)
    note = jnp.where(lane == 0, total - 256.0 * high.astype(f32), jnp.where(lane == LANES - 1, high.astype(f32), note))
    lines = [line[:, k * LANES : (k + 1) * LANES] for line in (got[0:1], got[1:2], code) for k in range(chunks)]
    own = vectors.shape[1]
    given = jnp.concatenate([vectors[...], jnp.zeros((1, -own % LANES), f32)], 1)
    lines += [note] + [given[:, k : k + LANES] for k in range(0, given.shape[1], LANES)]
    wide, block = packet.shape[0], up.shape[0]
    hidden = up.shape[1] // (2 * wide)
    first = packet.shape[1] - 2 * block
    index = iota((first, LANES), 0)
    whole = jnp.zeros((first, LANES), f32)
    for number, line in enumerate(lines):
        whole = jnp.where(index == number, line, whole)
    gap = jnp.zeros((block, LANES - hidden), f32)
    for dest in range(wide):
        pieces = [jnp.concatenate([up[:, n * hidden : (n + 1) * hidden], gap], 1) for n in (dest, wide + dest)]
        packet[dest] = jnp.concatenate([whole] + pieces, 0).astype(bf16)


def cast_kernel(attn_in, attn_out, head, down, out, down_out):
    down_out[...] = down[...].astype(bf16)
    out[:, : 3 * D] = attn_in[...].astype(bf16)
    out[:, 3 * D : 4 * D] = attn_out[...].astype(bf16)
    out[:, 4 * D :] = head[...].astype(bf16)


def build_kernel(emb, table):
    feats, vocab = emb.shape
    half = table.shape[0]
    blocks, second = half // LANES, (vocab - half) // LANES
    gap = jnp.zeros((SIDE - feats, LANES), f32)

    def build(b, both):
        start = pl.multiple_of(b * LANES, LANES)
        low = emb[:, pl.ds(start, LANES)]
        high = jnp.zeros_like(low)
        if both:
            high = emb[:, pl.ds(pl.multiple_of(half + start, LANES), LANES)]
        table[pl.ds(start, LANES), :] = jnp.concatenate([low, gap, high, gap], 0).astype(bf16).T.astype(f32)

    unroll = 7

    def step(i, carry):
        for k in range(unroll):
            build(i * unroll + k, True)
        return carry

    lax.fori_loop(0, second // unroll, step, 0)
    for b in range(second // unroll * unroll, blocks):
        build(jnp.int32(b), b < second)


def side_of(packet, s, chunks, group, half_rows, half):
    ids = lanes_of(packet, s, 0, chunks) * 256.0 + lanes_of(packet, s, chunks, chunks)
    local = ids - (group * half_rows).astype(f32)
    inside = (local >= 0.0) & (local < float(half_rows))
    return jnp.where(inside, jnp.where(local >= float(half), 2.0, 1.0), 0.0)


def own_span(first, group, count):
    return jnp.where(group == 0, 0, first), jnp.where(group == 0, first, count)


def number_block(per, count):
    return pl.BlockSpec((1, 1, per * count), lambda i, *s: (i, 0, 0), memory_space=pltpu.SMEM)


def lookup_kernel(half_rows, per, unroll, where, firsts, numbers, packet, table, out, buf):
    feats, count = out.shape[1:]
    group = where[0]
    chunks = count // LANES
    half = table.shape[0]
    at = pl.program_id(0) * per
    for s in range(per):
        low, high = own_span(firsts[at + s], group, count)

        def step(i, carry):
            for k in range(unroll):
                t = i * unroll + k
                buf[pl.ds(s * count + t, 1), :] = table[pl.ds(numbers[0, 0, s * count + t], 1), :]
            return carry

        lax.fori_loop(low // unroll, (high + unroll - 1) // unroll, step, 0)
    for s in range(per):
        side = side_of(packet, s, chunks, group, half_rows, half)
        lines = [buf[s * count + c * LANES : s * count + (c + 1) * LANES, :].astype(bf16).T for c in range(chunks)]
        turned = jnp.concatenate(lines, 1).astype(f32)
        pick = jnp.where(side > 1.5, turned[SIDE : SIDE + feats], turned[:feats])
        value = jnp.where(side > 0.5, pick, 0.0)
        out[s] = value.astype(bf16)


def lanes_of(packet, s, first, chunks):
    return jnp.concatenate([packet[s, first + c : first + c + 1, :].astype(f32) for c in range(chunks)], 1)


def lookup(where, numbers, firsts, packets, table, half_rows, feats, count, per=4, unroll=64):
    sources = packets.shape[0]
    some = lambda dims: pl.BlockSpec((per,) + dims, lambda i, *s: (i, 0, 0))
    return pl.pallas_call(
        partial(lookup_kernel, half_rows, per, unroll),
        out_shape=shape((sources, feats, count), bf16),
        grid_spec=pltpu.PrefetchScalarGridSpec(
            num_scalar_prefetch=2,
            grid=(sources // per,),
            in_specs=[number_block(per, count), some(packets.shape[1:]), pl.BlockSpec(table.shape, lambda i, *s: (0, 0), pipeline_mode=pl.Buffered(1))],
            out_specs=some((feats, count)),
            scratch_shapes=[pltpu.VMEM((per * count, LANES), f32)],
        ),
        compiler_params=pltpu.CompilerParams(vmem_limit_bytes=16 * MIB),
        cost_estimate=pl.CostEstimate(flops=10**9, bytes_accessed=10**7, transcendentals=0),
        name="lookup",
    )(where, firsts, numbers.reshape(-1, 1, per * count), packets, pinned(table))


def spread_kernel(rows, half_rows, feats, per, unroll, copies, at_early, where, firsts, numbers, packet, early_own, early_other, late_own, late_other, p_heads, out, square, *scratch):
    parts, buf = scratch[:copies], scratch[copies]
    group = where[0]
    chunks = buf.shape[0] // (per * LANES)
    count = chunks * LANES
    half = parts[0].shape[0]
    vocab = out.shape[1]
    blocks = half // LANES
    step_at = pl.program_id(0)

    @pl.when(step_at == 0)
    def _():
        def clear(i, carry):
            for part in parts:
                part[pl.ds(pl.multiple_of(i * LANES, LANES), LANES), :] = jnp.zeros((LANES, LANES), f32)
            return carry

        lax.fori_loop(0, blocks, clear, 0)

    gap = jnp.zeros((SIDE - feats, count), f32)
    block = feats // 2
    lane, slot = iota((LANES, 2 * LANES), 0), iota((LANES, 2 * LANES), 1)
    half_of = lax.shift_right_logical(slot, 7)
    slot = slot - half_of * LANES
    seq_of, head = lax.shift_right_logical(slot, 4), slot - lax.shift_right_logical(slot, 4) * STEP
    relane = flag((lane == half_of * SIDE + seq_of * HEADS + head) & (head < HEADS) & (seq_of < rows)).astype(bf16)
    empty = jnp.zeros((LANES - rows * STEP, count), f32)
    is_own = step_at < pl.num_programs(0) // 2

    def pick(own, other, s, first, lines):
        return jnp.where(is_own, own[s, first : first + lines, :], other[s, first : first + lines, :])

    for s in range(per):
        code = lanes_of(packet, s, 2 * chunks, chunks)
        slot0 = code >= 8.0
        seq = jnp.where(slot0, code - 8.0, code)
        scores = unpack_heads(pick(late_own, late_other, s, block + ROWS, head_lines(chunks)), chunks)
        values = unpack_heads(p_heads[s, : head_lines(chunks), :], chunks)
        parts_of = [jnp.where(seq == float(r), scores, 0.0) for r in range(rows)] + [empty]
        parts_of += [jnp.where(seq == float(r), values, 0.0) for r in range(rows)] + [empty]
        both = jnp.concatenate([pick(early_own, early_other, s, at_early, block), pick(late_own, late_other, s, 0, block)], 0)
        wide_rows = dot(both, relane).astype(bf16)
        basis = [jnp.concatenate([wide_rows[k : k + block, :LANES], wide_rows[k : k + block, LANES:]], 0) for k in (0, block)]
        x = dot(jnp.concatenate(basis, 1), jnp.concatenate(parts_of, 0).astype(bf16))
        first = flag((iota((ROWS, count), 0).astype(f32) == seq) & slot0).astype(bf16)
        x = x + dot(pick(late_own, late_other, s, block, ROWS), first, 0, 0)[:feats]
        side = side_of(packet, s, chunks, group, half_rows, half)
        tall = jnp.concatenate([jnp.where(side == 1.0, x, 0.0), gap, jnp.where(side == 2.0, x, 0.0), gap], 0).astype(bf16)
        for c in range(chunks):
            start = s * count + c * LANES
            buf[start : start + LANES, :] = tall[:, c * LANES : (c + 1) * LANES].T.astype(f32)
    for s in range(per):
        low, high = own_span(firsts[step_at * per + s], group, count)

        def step(i, carry):
            for k in range(unroll):
                t = i * unroll + k
                part = parts[k % copies]
                row = numbers[0, 0, s * count + t]
                part[pl.ds(row, 1), :] = part[pl.ds(row, 1), :] + buf[pl.ds(s * count + t, 1), :]
            return carry

        lax.fori_loop(low // unroll, (high + unroll - 1) // unroll, step, 0)

    @pl.when(step_at == pl.num_programs(0) - 1)
    def _():
        def emit(b, total, both):
            start = pl.multiple_of(b * LANES, LANES)
            lines = parts[0][pl.ds(start, LANES), :]
            for part in parts[1:]:
                lines = lines + part[pl.ds(start, LANES), :]
            turned = lines.T
            out[:, pl.ds(start, LANES)] = turned[:feats]
            if both:
                out[:, pl.ds(pl.multiple_of(half + start, LANES), LANES)] = turned[SIDE : SIDE + feats]
            return total + lines * lines

        second = (vocab - half) // LANES
        group_of = 7

        def several(i, total):
            for k in range(group_of):
                total = emit(i * group_of + k, total, True)
            return total

        total = lax.fori_loop(0, second // group_of, several, jnp.zeros((LANES, LANES), f32))
        for b in range(second // group_of * group_of, blocks):
            total = emit(jnp.int32(b), total, b < second)
        square[...] = jnp.sum(total.reshape(LANES // ROWS, ROWS, LANES), 0)


def spread_tokens(where, numbers, firsts, packets, early, late, p_heads, at_early, rows, half_rows, feats, count, per=8, unroll=40, copies=5):
    devices = packets.shape[0]
    block = packets.shape[1:]
    half = -(-half_rows // (2 * LANES)) * LANES
    some = lambda dims: pl.BlockSpec((per,) + dims, lambda i, *s: (i, 0, 0))
    steps = devices // per
    ordered = pl.BlockSpec((per, head_lines(count // LANES), LANES), lambda i, where, *s: ((i + where[0] * (steps // 2)) % steps, 0, 0))
    mine = lambda pair: pl.BlockSpec((per,) + pair[0].shape[1:], lambda i, *s: (jnp.minimum(i, steps // 2 - 1), 0, 0))
    theirs = lambda pair: pl.BlockSpec((per,) + pair[0].shape[1:], lambda i, *s: (jnp.maximum(i - steps // 2, 0), 0, 0))
    return pl.pallas_call(
        partial(spread_kernel, rows, half_rows, feats, per, unroll, copies, at_early),
        out_shape=[pltpu.HBM((feats, half_rows), f32), pltpu.HBM((ROWS, LANES), f32)],
        grid_spec=pltpu.PrefetchScalarGridSpec(
            num_scalar_prefetch=2,
            grid=(steps,),
            in_specs=[number_block(per, count), some(block), mine(early), theirs(early), mine(late), theirs(late), ordered],
            out_specs=[pl.BlockSpec((feats, half_rows), lambda i, *s: (0, 0), pipeline_mode=pl.Buffered(1)), pl.BlockSpec((ROWS, LANES), lambda i, *s: (0, 0))],
            scratch_shapes=[pltpu.VMEM((half, LANES), f32)] * copies + [pltpu.VMEM((per * count, LANES), f32)],
        ),
        compiler_params=pltpu.CompilerParams(vmem_limit_bytes=52 * MIB),
        cost_estimate=pl.CostEstimate(flops=10**9, bytes_accessed=3 * 10**7, transcendentals=0),
        name="spread_tokens",
    )(where, firsts, numbers.reshape(-1, 1, per * count), packets, *early, *late, p_heads)


def attend_kernel(rows, mats, xt, vec, moved, sent, early, known, y_out, probs_out, psum_out, normed_out, inv_out, *scratch):
    w = square_weights(mats, 0, *scratch, (0, 1, 2, 3))
    x1, x00, q, o, probs, psum, normed, inv, qk, y = attend(xt[...], w, vec[...], moved[...], rows)
    tiles = to_tiles(x1)
    halves, heads = both_halves(qk, rows), pack_heads(probs.astype(bf16), rows)
    wide = sent.shape[0]
    block = D // (2 * wide)
    for dest in range(wide):
        sent[dest] = tiles.astype(bf16)
        early[dest] = table_block(halves, dest, block).astype(bf16)
    facts = jnp.concatenate([to_tiles(value.astype(f32)) for value in (x00, q, o)], 0).astype(bf16)
    known[...] = jnp.concatenate([heads, facts], 0)
    y_out[...] = y.astype(bf16)
    probs_out[...], psum_out[...], normed_out[...], inv_out[...] = probs, psum, normed, inv


def attend_back_kernel(rows, place, mats, got, d_res2, sums_up, normed, inv, probs, psum, xt, vec, late_out, last, z_out, *scratch):
    w = square_weights(mats, 0, *scratch, (3, 2, 1, 0))
    wide = late_out.shape[0]
    block = D // (2 * wide)
    feats = 2 * block
    dx1 = d_res2[pl.ds(pl.multiple_of(place[0] * ROWS, ROWS), ROWS), :]
    lines = ROWS * (D // LANES)
    tiles = got[0, :lines, :].astype(f32)
    for k in range(1, wide):
        tiles = tiles + got[k, :lines, :].astype(f32)
    dx1 = dx1 + jnp.concatenate([tiles[k : k + ROWS] for k in range(0, lines, ROWS)], 1)
    d_a, d_o, d_q, sums, vd, z, extra, ds = attend_back(
        dx1, normed[...], inv[...], probs[...], psum[...], xt[...], w, vec[...], rows
    )
    halves = both_halves(vd, rows)
    heads = pack_heads(ds, rows)
    gap = jnp.zeros((ROWS, LANES - feats), f32)
    for dest in range(wide):
        row_part = jnp.concatenate([extra[:, feats * dest : feats * (dest + 1)], gap], 1)
        late_out[dest] = jnp.concatenate([jnp.concatenate([table_block(halves, dest, block), row_part], 0).astype(bf16), heads], 0)
    z_out[...] = z.astype(bf16)
    sums = sums + [sums_up[...]]
    index = iota((ROWS, D), 0)
    spare = ROWS - rows
    values = [d_q.astype(f32), d_o.astype(f32), d_a.astype(f32)]
    for number, row in enumerate(sums):
        values[number // spare] = jnp.where(index == rows + number % spare, row, values[number // spare])
    last[...] = jnp.concatenate([to_tiles(value) for value in values], 0).astype(bf16)


def pack_kernel(rows, last, y, z, d_up, d_up_other, out):
    wide = out.shape[0]
    block = d_up.shape[0] // wide
    hidden = d_up.shape[1] // 2
    values = last[...]
    halves_y, halves_z = both_halves(y[...], rows), both_halves(z[...], rows)
    up = d_up[...] + d_up_other[...].astype(f32)
    gap = jnp.zeros((block, LANES - hidden), f32)
    for dest in range(wide):
        mine = up[block * dest : block * (dest + 1), :]
        pieces = [jnp.concatenate([mine[:, k * hidden : (k + 1) * hidden], gap], 1) for k in range(2)]
        pieces += [weight_block(halves_y, dest, block, wide), weight_block(halves_z, dest, block, wide)]
        out[dest] = jnp.concatenate([values, jnp.concatenate(pieces, 0).astype(bf16)], 0)


def rows_of(own, other):
    return jnp.concatenate([from_tiles(own[...], 0), from_tiles(other[...], 0)], 0)


def by_core(where, own, other):
    first = where[0] == 0
    return jnp.concatenate([jnp.where(first, own[...], other[...]), jnp.where(first, other[...], own[...])], 0)


def ffn_kernel(where, x_own, w_up, down_own, down_other, bias, u_out, h_out, out):
    u, h, f = ffn(from_tiles(x_own[...], 0), w_up[...], by_core(where, down_own, down_other), bias[...])
    u_out[...], h_out[...] = u, h
    out[...] = f.astype(bf16)


def total_kernel(got, out):
    total = got[0].astype(f32)
    for k in range(1, got.shape[0]):
        total = total + got[k].astype(f32)
    lines = to_tiles(total).astype(bf16)
    for k in range(out.shape[0]):
        out[k] = lines


def middle_kernel(where, mats, x_own, x_other, f_own, f_other, u, w_up, down_own, down_other, vec, picks, early, loss, pooled, d_c, d_res2, d_f, d_u, out, sums, sums_up, *scratch):
    w = square_weights(mats, 4, *scratch, (4,))
    x1 = rows_of(x_own, x_other).astype(f32)
    f = rows_of(f_own, f_other).astype(f32)
    got = middle(x1, f, u[...], w_up[...], by_core(where, down_own, down_other), w, vec[...], picks[...])
    lines = u.shape[0]
    loss[...], pooled[...], d_c[...], d_res2[...] = got[:4]
    d_f[...], d_u[...] = got[4][:lines], got[5]
    for dest in range(out.shape[0]):
        part = to_tiles(got[6][dest * ROWS : (dest + 1) * ROWS]).astype(bf16)
        out[dest] = jnp.concatenate([part, early[dest]], 0)
    sums[...] = stack_rows(got[7])
    su = jnp.sum(got[5].astype(f32), 0, keepdims=True)
    sums_up[...] = jnp.concatenate([su, jnp.zeros((1, D - su.shape[1]), f32)], 1)


def own_cols(device, block):
    index = iota((D, LANES), 1)
    return flag((iota((D, LANES), 0) == device * block + index) & (index < block)).astype(bf16)


def own_rows(left, right, mine, block):
    return dot(dot(left, mine).astype(bf16), right, 0, 0)[:block]


def ffn_grads_kernel(where, x_own, h, d_f, d_u, pooled, d_c, down_mine, down_theirs, d_head, up_mine, up_theirs):
    first = where[0] == 0
    hidden = down_mine.shape[0]
    half = up_mine.shape[0]
    d_up = dot(from_tiles(x_own[...], 0), d_u[...], 0, 0)
    up_mine[...] = jnp.where(first, d_up[:half], d_up[half:])
    up_theirs[...] = jnp.where(first, d_up[half:], d_up[:half]).astype(bf16)
    d_down = dot(h[...], d_f[...], 0, 0)
    down_mine[...] = jnp.where(first, d_down[:hidden], d_down[hidden:])
    down_theirs[...] = jnp.where(first, d_down[hidden:], d_down[:hidden]).astype(bf16)
    block = d_head.shape[0]
    d_head[...] = own_rows(pooled[...], d_c[...], own_cols(where[1], block), block)


def grads_kernel(rows, where, known, facts_own, facts_other, d_wh, down_mine, down_other, sums, square, in_out, out_out, up_out, down_out, vec_out, square_out, x00, q_all, o_all, d_q, d_o, d_a, y, z, wide_z):
    group, device = where[0], where[1]
    wide = facts_own.shape[0]
    devices = 2 * wide
    block = in_out.shape[0]
    hidden = FF // devices
    first = group == 0
    lines = ROWS * (D // LANES)
    at_up = 3 * lines
    for base, facts in ((0, facts_own), (1, facts_other)):
        at = slice(base * wide * ROWS, (base + 1) * wide * ROWS)
        kept = known[pl.ds(((base + group) % 2) * wide, wide), known.shape[1] - 3 * lines :, :]
        for k, out in enumerate((x00, q_all, o_all)):
            out[at, :] = from_tiles(kept, k * lines).astype(f32)
        for k, out in enumerate((d_q, d_o, d_a)):
            out[at, :] = from_tiles(facts, k * lines).astype(f32)
        for n in range(wide):
            at = slice((base * wide + n) * block, (base * wide + n + 1) * block)
            y[at, :] = facts[n, at_up + 2 * block : at_up + 3 * block, :].astype(f32)
            z[at, :] = facts[n, at_up + 3 * block : at_up + 4 * block, :].astype(f32)
    for n in range(wide):
        for k in range(2):
            piece = facts_own[n, at_up + k * block : at_up + (k + 1) * block, :].astype(f32)
            at = (k * wide + n) * hidden
            up_out[:, at : at + hidden] = piece[:, :hidden]
    down_out[...] = down_mine[...] + down_other[...].astype(f32)

    def by_heads(source, values):
        total = jnp.zeros((block, D), f32)
        low = source[...].astype(bf16)
        for r in range(rows):
            wide_z[...] = dot(low, expand_table(rows, jnp.where(group == 0, 0, SIDE), r))
            for n in range(devices):
                total = total + wide_z[n * block : (n + 1) * block, :] * values[n * ROWS + r : n * ROWS + r + 1, :]
        return total

    d_wk = by_heads(z, q_all) * HEAD_DIM ** (-0.5)
    d_wv = by_heads(y, d_o)
    mine = own_cols(device, block)
    d_wq = own_rows(x00[...].astype(bf16), d_q[...].astype(bf16), mine, block)
    d_wo = own_rows(o_all[...].astype(bf16), d_a[...].astype(bf16), mine, block)
    square_now = square[...]

    def fold(square_now, value):
        tiles = value * value
        total = jnp.sum(tiles.reshape(tiles.shape[0] // ROWS, ROWS, tiles.shape[1]), 0)
        for k in range(total.shape[1] // LANES):
            square_now = square_now + total[:, k * LANES : (k + 1) * LANES]
        return square_now

    in_out[:, :D], in_out[:, D : 2 * D], in_out[:, 2 * D :] = d_wq, d_wk, d_wv
    out_out[...] = d_wo
    for value in (d_wq, d_wk, d_wv, d_wo, d_wh[...], up_out[...], down_out[...]):
        square_now = fold(square_now, value)
    spare = ROWS - rows
    grouped = [jnp.sum(t[...].reshape(devices, ROWS, D), 0) for t in (d_q, d_o)]
    tail = [grouped[k // spare][rows + k % spare : rows + k % spare + 1] for k in range(5)]
    mids = sums[...]
    pieces = [tail[0], mids[0:1], mids[1:2], tail[3], tail[4], tail[2], tail[1]] + [mids[k : k + 1] for k in range(2, 6)]
    index = iota((16, D), 0)
    total = jnp.zeros((16, D), f32)
    for number, row in enumerate(pieces):
        total = jnp.where(index == number, row, total)
    each = D // hidden
    for k in range(wide):
        lines_of = [(base * wide + k) * ROWS + rows + 5 % spare for base in range(2)]
        source = (d_q, d_o)[5 // spare]
        row = source[lines_of[0] : lines_of[0] + 1, :] + source[lines_of[1] : lines_of[1] + 1, :]
        for core in range(2):
            shift = (hidden * (k % each) - hidden * core) % D
            turned = pltpu.roll(row, shift, 1) if shift else row
            col = iota((1, D), 1)
            turned = jnp.where((col >= hidden * (k % each)) & (col < hidden * (k % each + 1)), turned, 0.0)
            total = total + jnp.where(index == 11 + (core * wide + k) // each, turned, 0.0)
    vec_out[...] = total
    square_now = square_now + fold(jnp.zeros((ROWS, LANES), f32), total) / devices
    for k in range(devices):
        square_out[k] = square_now


def adam_kernel(count, scales, weight, first, second, d_table, got, *refs):
    grads, state = refs[:count], refs[count : 4 * count]
    norm_out, factor_out = refs[4 * count : 4 * count + 2]
    outs = refs[4 * count + 2 : 7 * count + 2]
    far = refs[7 * count + 2 : 7 * count + 5]
    loads, stores, got_in, sent = refs[7 * count + 5 :]
    slots, lines = loads.shape[0], loads.shape[2]
    jobs = weight.shape[0] // lines
    sources = (weight, first, second, d_table)

    def load(j):
        return [pltpu.make_async_copy(ref.at[pl.ds(j * lines, lines), :], loads.at[j % slots, k], got_in.at[j % slots, k]) for k, ref in enumerate(sources)]

    def store(j):
        return [pltpu.make_async_copy(stores.at[j % slots, k], ref.at[pl.ds(j * lines, lines), :], sent.at[j % slots, k]) for k, ref in enumerate(far)]

    for j in range(min(slots, jobs)):
        for copy in load(j):
            copy.start()
    total = got[0]
    for k in range(1, got.shape[0]):
        total = total + got[k]
    total = jnp.sum(jnp.sum(total, 0, keepdims=True), 1, keepdims=True)
    norm = jnp.sqrt(total)
    factor = jnp.minimum(1.0, clip_level / (norm + 1e-06))
    norm_out[...], factor_out[...] = norm, factor
    one, two = scales[0], scales[1]
    for j in range(jobs):
        for copy in load(j):
            copy.wait()
        if j >= slots:
            for copy in store(j - slots):
                copy.wait()
        old = [loads[j % slots, k] for k in range(3)]
        new = update(*old, loads[j % slots, 3] * factor, RATES[0], one, two)
        for k in range(3):
            stores[j % slots, k] = new[k]
        for copy in store(j):
            copy.start()
        if j + slots < jobs:
            for copy in load(j + slots):
                copy.start()
    for number in range(count):
        old = [state[3 * number + k][...] for k in range(3)]
        new = update(*old, grads[number][...] * factor, RATES[number + 1], one, two)
        for k in range(3):
            outs[3 * number + k][...] = new[k]
    for j in range(max(0, jobs - slots), jobs):
        for copy in store(j):
            copy.wait()


def swap(x):
    return lax.ppermute(x, "group", [(0, 1), (1, 0)])


def exchange(x):
    return lax.all_to_all(x, "wide", split_axis=0, concat_axis=0, tiled=True)


def tie(*values):
    return lax.optimization_barrier(values)


def pair(x):
    own = exchange(x)
    return own, swap(own)


def in_order(own, other, group):
    return jnp.where(group == 0, jnp.concatenate([own, other], 0), jnp.concatenate([other, own], 0))


def plain_body(wide, passage_ids, query_ids, passage_len, query_len, positive, negatives, valid, step_count, *state):
    params, firsts, seconds = state[0::3], state[1::3], state[2::3]
    embedding, attn_in, attn_out, w_ffn_up, w_ffn_down, head, vectors = params
    group, place = lax.axis_index("group"), lax.axis_index("wide")
    device, devices = group * wide + place, 2 * wide
    feats, half_rows = embedding.shape
    block, hidden = D // devices, FF // devices
    pas_count, pas_len = passage_ids.shape
    qry_count, qry_len = query_ids.shape
    rows = pas_count + qry_count
    tokens = pas_count * pas_len + qry_count * qry_len
    live = rows * HEADS
    both = lambda x: jnp.concatenate(pair(x), 0)
    gather = lambda x: both(jnp.broadcast_to(x[None], (wide,) + x.shape))
    ids = jnp.concatenate([passage_ids.reshape(-1), query_ids.reshape(-1)])
    seq_np = np.concatenate([np.repeat(np.arange(pas_count), pas_len), pas_count + np.repeat(np.arange(qry_count), qry_len)])
    pos_np = np.concatenate([np.tile(np.arange(pas_len), pas_count), np.tile(np.arange(qry_len), qry_count)])
    lens = jnp.concatenate([jnp.repeat(passage_len, pas_len), jnp.repeat(query_len, qry_len)])
    moved = jnp.zeros((ROWS, tokens), f32).at[2].set(jnp.asarray(seq_np, f32)).at[3].set(jnp.asarray(pos_np == 0, f32))
    moved = moved.at[4].set(flag(jnp.asarray(pos_np) < lens))
    note = jnp.concatenate([ids, valid, positive, negatives.reshape(-1)])
    notes = gather(jnp.pad(note, (0, -note.shape[0] % LANES)).reshape(-1, LANES)).reshape(devices, -1)
    low_vectors = gather(jnp.pad(vectors.astype(bf16), (0, -vectors.shape[0] % LANES)).reshape(-1, LANES))
    vec = in_order(low_vectors[:wide], low_vectors[wide:], group).reshape(devices, -1)[:, : vectors.shape[0]].astype(f32).reshape(-1, D)
    all_ids = notes[:, :tokens]
    valid_rows = jnp.pad(notes[:, tokens : tokens + qry_count].astype(f32), ((0, 0), (pas_count, ROWS - rows))).reshape(-1, 1)
    at = tokens + qry_count
    picked = jnp.concatenate(
        [notes[:, at : at + qry_count, None], notes[:, at + qry_count : at + qry_count + negatives.size].reshape(devices, qry_count, -1)], 2
    )
    pick_dev = picked // pas_count
    pick_row = (((pick_dev // wide) ^ group) * wide + pick_dev % wide) * ROWS + picked % pas_count
    pick_rows = jnp.pad(pick_row, ((0, 0), (pas_count, ROWS - rows), (0, 0)), constant_values=-1).reshape(devices * ROWS, -1)
    mats = lax.all_gather(jnp.concatenate([attn_in, attn_out, head], 1).astype(bf16), ALL, axis=0, tiled=True)
    w = lambda k: mats[:, k * D : (k + 1) * D]
    w_up = lax.all_to_all(
        w_ffn_up.astype(bf16).reshape(block, devices, hidden).transpose(1, 0, 2), ALL, split_axis=0, concat_axis=0, tiled=True
    ).reshape(D, hidden)
    w_down = w_ffn_down.astype(bf16)
    bias_up = lax.dynamic_slice(vec.reshape(-1), (11 * D + device * hidden,), (hidden,))[None]
    local = all_ids - group * half_rows
    inside = ((local >= 0) & (local < half_rows)).reshape(1, -1)
    local = jnp.clip(local, 0, half_rows - 1).reshape(-1)
    looked = jnp.where(inside, jnp.take(embedding.astype(bf16), local, axis=1), jnp.zeros((), bf16))
    looked = looked.reshape(feats, devices, tokens).transpose(1, 0, 2)
    xt = exchange(looked[:wide] + swap(looked[wide:])).reshape(D, tokens)
    x1, x00, q, o, probs, psum, normed1, inv1, qk, y = attend(xt, w, vec, moved, rows)
    p_heads = dot(heads_table(rows), probs.astype(bf16)).astype(bf16)
    x1_all = gather(x1.astype(bf16)).reshape(devices * ROWS, D)

    def to_owner(parts):
        mine = parts[: wide * ROWS] + swap(parts[wide * ROWS :])
        return jnp.sum(exchange(mine.astype(bf16).reshape(wide, ROWS, D)).astype(f32), 0)

    u, h, f_part = ffn(x1_all, w_up, w_down, bias_up)
    f_all = gather(to_owner(f_part).astype(bf16)).reshape(devices * ROWS, D).astype(f32)
    loss, pooled, d_c, d_res2, d_f, d_u, d_x1, sums = middle(x1_all.astype(f32), f_all, u, w_up, w_down, w, vec, jnp.concatenate([valid_rows.astype(jnp.int32), pick_rows], 1))
    d_x1 = lax.dynamic_slice(d_res2, (place * ROWS, 0), (ROWS, D)) + to_owner(d_x1)
    d_a, d_o, d_q, sums_back, vd, z, extra, ds = attend_back(d_x1, normed1, inv1, probs, psum, xt, w, vec, rows)

    to_features = lambda t: both(t.T.astype(bf16).reshape(wide, feats, -1))

    def to_blocks(t):
        parts = t.T.astype(bf16).reshape(2, wide, block, -1).transpose(1, 0, 2, 3).reshape(wide, 2 * block, -1)
        got = both(parts).reshape(devices, 2, block, -1)
        return lax.dynamic_index_in_dim(got, group, 1, keepdims=False)[:, :, :live].reshape(devices, block, rows, HEADS)

    facts = gather(jnp.concatenate([x00, q, o, d_q, d_o, d_a], 0)).reshape(devices, 6, ROWS, D)
    flat_fact = lambda k: facts[:, k].reshape(devices * ROWS, D)
    by_head = lambda k: facts[:, k].reshape(devices, ROWS, HEADS, HEAD_DIM)[:, :rows]
    cut = lambda m: lax.dynamic_slice(m, (0, device * block), (devices * ROWS, block))
    d_wq = dot(cut(flat_fact(0)), flat_fact(3), 0, 0)
    d_wk = jnp.einsum("nfrh,nrhd->fhd", to_blocks(z), by_head(1), preferred_element_type=f32).reshape(block, D) * HEAD_DIM ** (-0.5)
    d_wv = jnp.einsum("nfrh,nrhd->fhd", to_blocks(y), by_head(4), preferred_element_type=f32).reshape(block, D)
    d_wo = dot(cut(flat_fact(2)), flat_fact(5), 0, 0)
    d_wup = dot(x1_all, d_u, 0, 0).astype(bf16).reshape(devices, block, hidden)
    d_wup = lax.all_to_all(d_wup, ALL, split_axis=0, concat_axis=0, tiled=True).astype(f32).transpose(1, 0, 2).reshape(block, FF)
    sums_up = jnp.pad(jnp.sum(d_u.astype(f32), 0, keepdims=True), ((0, 0), (0, D - hidden)))
    tails = gather(stack_rows(sums_back + [sums_up]))
    tail = jnp.sum(tails, 0)
    ups = in_order(tails[:wide], tails[wide:], group)[:, 5, :hidden].reshape(-1)
    mids = [row[0] for row in sums]
    d_vec = jnp.concatenate([tail[0], mids[0], mids[1], tail[3], tail[4], tail[2], tail[1]] + mids[2:] + [ups])
    d_vec = lax.dynamic_slice(d_vec, (device * vectors.shape[0],), vectors.shape)
    basis = jnp.concatenate([to_features(qk), to_features(vd), to_features(extra)], 2)
    lanes = gather(jnp.concatenate([dot(heads_table(rows), ds).astype(bf16), p_heads], 0))
    seq = jnp.asarray(seq_np, jnp.int32)[None]
    here = sequence_of(iota((SIDE, 1), 0), rows) == seq
    widen = lambda t: jnp.where(here[None], jnp.einsum("ha,nht->nat", heads_table(rows), t, preferred_element_type=f32), 0.0).astype(bf16)
    first = ((iota((ROWS, 1), 0) == seq) & jnp.asarray(pos_np == 0)[None]).astype(bf16)
    coef = jnp.concatenate([widen(lanes[:, :16]), widen(lanes[:, 16:]), jnp.broadcast_to(first[None], (devices,) + first.shape)], 1)
    d_tok = jnp.einsum("nfa,nat->fnt", basis, coef, preferred_element_type=f32).reshape(feats, -1)
    d_table = jnp.zeros((feats, half_rows), f32).at[:, local].add(jnp.where(inside, d_tok, 0.0))
    d_head = dot(cut(pooled), d_c, 0, 0)
    grads = (d_table, jnp.concatenate([d_wq, d_wk, d_wv], 1), d_wo, d_wup, dot(h, d_f, 0, 0), d_head, d_vec)
    squares = sum(jnp.sum(g * g) for g in grads)
    grad_norm = jnp.sqrt(jnp.sum(gather(jnp.full((ROWS, LANES), squares))[:, 0, 0]))
    factor = jnp.minimum(1.0, clip_level / (grad_norm + 1e-06))
    step_float = step_count[0].astype(f32)
    one, two = 1.0 / (1.0 - jnp.power(0.9, step_float)), 1.0 / (1.0 - jnp.power(0.999, step_float))
    new = [update(params[k], firsts[k], seconds[k], grads[k] * factor, RATES[k], one, two) for k in range(7)]
    return (loss[0, 0], grad_norm) + tuple(t for group_of in new for t in group_of)


def body(wide, passage_ids, query_ids, passage_len, query_len, positive, negatives, valid, step_count, *state):
    embedding, attn_in, attn_out, w_ffn_up, w_ffn_down, head, vectors = state[0::3]
    group = lax.axis_index("group")
    place = lax.axis_index("wide")
    device = group * wide + place
    devices = 2 * wide
    feats, half_rows = embedding.shape
    block = D // devices
    hidden = FF // devices
    pas_count, pas_len = passage_ids.shape
    qry_count, qry_len = query_ids.shape
    rows = pas_count + qry_count
    tokens = pas_count * pas_len + qry_count * qry_len
    chunks = tokens // LANES
    half = -(-half_rows // (2 * LANES)) * LANES
    where = jnp.stack([group, device]).astype(jnp.int32)
    place_at = place.astype(jnp.int32)[None]
    lines = wide * ROWS

    seq_np = np.concatenate([np.repeat(np.arange(pas_count), pas_len), pas_count + np.repeat(np.arange(qry_count), qry_len)])
    pos_np = np.concatenate([np.tile(np.arange(pas_len), pas_count), np.tile(np.arange(qry_len), qry_count)])
    vec_lines = -(-vectors.shape[0] // LANES)
    packet_lines = -(-(3 * chunks + 1 + vec_lines) // ROWS) * ROWS + 2 * block
    at_note = 3 * chunks
    pieces = [passage_len, query_len, valid, positive]
    size = sum(t.shape[0] for t in pieces)
    assert size + negatives.size < LANES - 1
    small = jnp.concatenate(pieces + [jnp.zeros((LANES - size,), jnp.int32)])[None]
    packet, moved = call(
        partial(prepare_kernel, half_rows, rows),
        [shape((wide, packet_lines, LANES), bf16), shape((ROWS, tokens))],
        passage_ids, query_ids, negatives, small, vectors[None], jnp.asarray(seq_np, jnp.int32)[None], jnp.asarray(pos_np, jnp.int32)[None], w_ffn_up,
        near_outs=(0,), name="prepare",
    )
    packet_own = exchange(packet)
    (table,) = call(build_kernel, [shape((half, LANES))], embedding, name="build", flops=10**8)
    packet_own, table = tie(packet_own, table)
    packet_other = swap(packet_own)
    low_mats, down_low = call(
        cast_kernel, [shape((block, 5 * D), bf16), shape((hidden, D), bf16)],
        attn_in, attn_out, head, w_ffn_down, near_outs=(0,), name="cast",
    )
    mats = lax.all_gather(low_mats, ALL, axis=0, tiled=True)

    def numbers_of(packets):
        ids = packets[:, :chunks].astype(f32) * 256.0 + packets[:, chunks : 2 * chunks].astype(f32)
        local = ids - (group * half_rows).astype(f32)
        row_at = jnp.clip(jnp.where(local >= half, local - half, local), 0, half - 1)
        first = packets[:, at_note, 0].astype(f32) + 256.0 * packets[:, at_note, LANES - 1].astype(f32)
        return row_at.astype(jnp.int32).reshape(-1), first.astype(jnp.int32)

    look = partial(lookup, half_rows=half_rows, feats=feats, count=tokens)
    num_own, num_other = numbers_of(packet_own), numbers_of(packet_other)
    theirs = look(where, *num_other, packet_other, table)
    xt = exchange(look(where, *num_own, packet_own, table) + swap(theirs)).reshape(D, tokens)
    numbers = jnp.concatenate([num_own[0], num_other[0]])
    firsts = jnp.concatenate([num_own[1], num_other[1]])
    packets = jnp.concatenate([packet_own, packet_other], 0)
    ordered = in_order(packet_own, packet_other, group)
    w_up = ordered[:, packet_lines - 2 * block :, :hidden].reshape(devices, 2, block, hidden).transpose(0, 2, 1, 3).reshape(D, 2 * hidden)
    vec = ordered[:, at_note + 1 : at_note + 1 + vec_lines].astype(f32).reshape(devices, -1)
    vec = vec[:, : vectors.shape[0]].reshape(-1, D)
    bias_all = vec[11:].reshape(2, wide, hidden)
    bias_up = lax.dynamic_slice(bias_all, (0, place, 0), (2, 1, hidden)).reshape(1, 2 * hidden)
    notes = packets[:, at_note].astype(f32)
    at = 1 + qry_count
    picked = jnp.concatenate(
        [notes[:, at : at + qry_count, None], notes[:, at + qry_count : at + qry_count + negatives.size].reshape(devices, qry_count, -1)], 2
    ).astype(jnp.int32)
    pick_dev = picked // pas_count
    pick_row = (((pick_dev // wide) ^ group) * wide + pick_dev % wide) * ROWS + picked % pas_count
    pick_row = jnp.concatenate([notes[:, 1 : 1 + qry_count, None].astype(jnp.int32), pick_row], 2)
    pick_rows = jnp.pad(pick_row, ((0, 0), (pas_count, ROWS - rows), (0, 0))).reshape(devices * ROWS, -1)

    xt, vec, bias_up, pick_rows, w_up, packets, numbers, firsts = tie(xt, vec, bias_up, pick_rows, w_up, packets, numbers, firsts)
    tile_lines = ROWS * (D // LANES)
    heads_at, units = head_lines(chunks), 2 * hidden
    sent, early, known, y, probs, psum, normed1, inv1 = call(
        partial(attend_kernel, rows),
        [
            shape((wide, tile_lines, LANES), bf16), shape((wide, block, LANES), bf16), shape((heads_at + 3 * tile_lines, LANES), bf16),
            shape((SIDE, D), bf16), shape((SIDE, tokens)), shape((SIDE, 1)), shape((ROWS, D)), shape((ROWS, 1)),
        ],
        xt, vec, moved,
        far=(mats,), near=(0,), near_outs=(0,), scratch=weight_scratch(4), name="attend", flops=10**9,
    )
    x_own, x_other = pair(sent)
    known_all = lax.all_gather(known, ALL, axis=0, tiled=False)
    down_other = swap(down_low)
    u, h, f_mine = call(
        ffn_kernel, [shape((lines, units)), shape((lines, units), bf16), shape((lines, D), bf16)], x_own, w_up, down_low, down_other, bias_up,
        scalars=(where,), near=(0, 3), near_outs=(2,), name="ffn", flops=10**8, vmem=16,
    )
    f_parts = exchange(f_mine.reshape(wide, ROWS, D))
    (f_sum,) = call(total_kernel, [shape((wide, tile_lines, LANES), bf16)], f_parts, near=(0,), near_outs=(0,), name="total")
    f_own, f_other = pair(f_sum)
    loss, pooled, d_c, d_res2, d_f, d_u, d_sum, sums, sums_up = call(
        middle_kernel,
        [
            shape((1, 1)), shape((devices * ROWS, D), bf16), shape((devices * ROWS, D), bf16), shape((devices * ROWS, D)),
            shape((lines, D), bf16), shape((lines, units), bf16), shape((wide, tile_lines + block, LANES), bf16),
            shape((ROWS, D)), shape((1, D)),
        ],
        x_own, x_other, f_own, f_other, u, w_up, down_low, down_other, vec, pick_rows, early,
        scalars=(where,), far=(mats,), scratch=weight_scratch(1), near=(0, 1, 2, 3), near_outs=(6,), name="middle", flops=10**9, vmem=32,
    )
    got = exchange(d_sum)
    got_other = swap(got)
    down_mine, down_theirs, d_whead, up_mine, up_theirs = call(
        ffn_grads_kernel,
        [shape((hidden, D)), shape((hidden, D), bf16), shape((block, D)), shape((D // 2, units)), shape((D // 2, units), bf16)],
        x_own, h, d_f, d_u, pooled, d_c,
        scalars=(where,), after=(d_sum,), near=(0,), name="ffn_grads", flops=10**8,
    )
    late, last, z = call(
        partial(attend_back_kernel, rows),
        [shape((wide, block + ROWS + heads_at, LANES), bf16), shape((3 * tile_lines, LANES), bf16), shape((SIDE, D), bf16)],
        got, d_res2, sums_up, normed1, inv1, probs, psum, xt, vec,
        scalars=(place_at,), far=(mats,), after=(pinned(up_mine),), near=(0,), near_outs=(0,), scratch=weight_scratch(4), name="attend_back", flops=10**9,
    )
    late_own, late_other = pair(late)
    (packed,) = call(
        partial(pack_kernel, rows), [shape((wide, 3 * tile_lines + 4 * block, LANES), bf16)], last, y, z, up_mine, swap(up_theirs),
        after=(late,), near=(4,), name="pack",
    )
    last_own = exchange(once(packed, late_own))
    d_table, square = spread_tokens(
        where, numbers, firsts, packets, (got, got_other), (late_own, late_other), known_all, tile_lines, rows, half_rows, feats, tokens
    )
    piece = last_own[:1, :ROWS] + (square[None] * 0.0).astype(bf16)
    last_own = lax.dynamic_update_slice(last_own, piece, (0, 0, 0))
    last_other = swap(last_own)
    d_attn_in, d_wo, d_wup, d_down, d_vec, squares = call(
        partial(grads_kernel, rows),
        [shape((block, 3 * D)), shape((block, D)), shape((block, FF)), shape((hidden, D)), shape((16, D)), shape((devices, ROWS, LANES))],
        known_all, last_own, last_other, d_whead, down_mine, swap(down_theirs), sums, square,
        scalars=(where,),
        scratch=[pltpu.VMEM((devices * ROWS, D), f32)] * 6 + [pltpu.VMEM((D, LANES), f32)] * 2 + [pltpu.VMEM((D, D), f32)],
        near=(1, 2, 5), near_outs=(5,), name="grads", flops=10**9, vmem=32,
    )
    squares_got = lax.all_to_all(squares, ALL, split_axis=0, concat_axis=0, tiled=True)
    d_vectors = lax.dynamic_slice(d_vec.reshape(-1), (device * vectors.shape[0],), vectors.shape)
    step_float = step_count[0].astype(f32)
    scales = jnp.stack([1.0 / (1.0 - jnp.power(0.9, step_float)), 1.0 / (1.0 - jnp.power(0.999, step_float))])
    grads = (d_attn_in, d_wo, d_wup, d_down, d_whead)
    middle_state = state[3:18]
    slots, step_rows = 3, ROWS
    norm, factor, *new = call(
        partial(adam_kernel, len(grads)),
        [shape((1, 1)), shape((1, 1))] + [shape(t.shape) for t in middle_state],
        squares_got, *grads, *middle_state,
        scalars=(scales,), far=(*state[:3], d_table), far_outs=[shape(embedding.shape)] * 3,
        scratch=[
            pltpu.VMEM((slots, 4, step_rows, half_rows), f32), pltpu.VMEM((slots, 3, step_rows, half_rows), f32),
            pltpu.SemaphoreType.DMA((slots, 4)), pltpu.SemaphoreType.DMA((slots, 3)),
        ],
        near=(0,), name="adam", vmem=40,
    )
    new_vectors = update(*state[18:], d_vectors * factor[0, 0], RATES[6], scales[0], scales[1])
    return (loss[0, 0], norm[0, 0]) + tuple(new[15:]) + tuple(new[:15]) + new_vectors


def solution(mesh):
    split_rows = P(ALL, None)
    flat = P(ALL)
    table = P("wide", "group")
    mats = (table,) * 3 + (split_rows,) * 15 + (flat,) * 3
    in_specs = (split_rows, split_rows, flat, flat, flat, split_rows, flat, P()) + mats
    wide = mesh.shape["wide"]
    thick = D % (2 * wide * ROWS) == 0 and wide * ROWS <= LANES
    return jax.shard_map(
        partial(body if thick else plain_body, wide), mesh=mesh, in_specs=in_specs, out_specs=(P(), P()) + mats, check_vma=False
    )
```

```python
from functools import partial

import jax
import jax.numpy as jnp
import numpy as np
from jax import lax
from jax.experimental import pallas as pl
from jax.experimental.pallas import tpu as pltpu
from jax.sharding import PartitionSpec as P

D = 768
HEADS = 12
HEAD_DIM = 64
FF = 3072
ROWS = 8
LANES = 128
SIDE = 64
STEP = 16
ALL = ("group", "wide")
clip_level = 0.02
f32 = jnp.float32
bf16 = jnp.bfloat16
RATES = (0.5, 0.5 * D**-0.5, 0.5 * (D // 16) ** -0.5, 0.5 * D**-0.5, 0.5 * FF**-0.5, 0.5 * D**-0.5, 0.2)


def dot(a, b, ca=1, cb=0):
    return lax.dot_general(a, b, (((ca,), (cb,)), ((), ())), preferred_element_type=f32)


def split(x):
    high = x.astype(bf16)
    return high, (x - high.astype(f32)).astype(bf16)


def dot_split(x, w, cb=0):
    high, rest = split(x)
    return dot(high, w, 1, cb) + dot(rest, w, 1, cb)


def iota(shape, dim):
    return lax.broadcasted_iota(jnp.int32, shape, dim)


def stack_rows(rows):
    index = iota((ROWS, rows[0].shape[1]), 0)
    total = jnp.zeros(index.shape, f32)
    for number, row in enumerate(rows):
        total = jnp.where(index == number, row, total)
    return total


def layer_norm(resid):
    centred = resid - jnp.mean(resid, -1, keepdims=True)
    inv_std = lax.rsqrt(jnp.mean(centred * centred, -1, keepdims=True) + 1e-05)
    return centred * inv_std, inv_std


def norm_back(grad_out, normed, inv_std, gain):
    scaled = grad_out * gain
    return inv_std * (
        scaled
        - jnp.mean(scaled, -1, keepdims=True)
        - normed * jnp.mean(scaled * normed, -1, keepdims=True)
    )


def flag(condition):
    return jnp.where(condition, 1.0, 0.0)


def sequence_of(a, rows):
    assert HEADS == 12
    return jnp.where((a >= 0) & (a < rows * HEADS), lax.shift_right_logical(a * 43, 9), 99)


def head_of(a, rows):
    return a - HEADS * sequence_of(a, rows)


def spread_table(rows):
    return flag(sequence_of(iota((SIDE, ROWS), 0), rows) == iota((SIDE, ROWS), 1)).astype(bf16)


def column_table(rows):
    return flag(head_of(iota((SIDE, D), 0), rows) == lax.shift_right_logical(iota((SIDE, D), 1), 6))


def heads_table(rows):
    return flag(head_of(iota((16, SIDE), 1), rows) == iota((16, SIDE), 0)).astype(bf16)


def place_table(rows, first):
    a = iota((LANES, SIDE), 1)
    return flag((iota((LANES, SIDE), 0) == first + a) & (a < rows * HEADS)).astype(bf16)


def expand_table(rows, first, r):
    return flag(iota((LANES, D), 0) == first + r * HEADS + lax.shift_right_logical(iota((LANES, D), 1), 6)).astype(bf16)


def prepare(ids, live, seq, pos, group_rows):
    count = ids.shape[1]
    first = jnp.where(ids < group_rows, 1.0, 0.0)
    high = lax.shift_right_logical(ids, 8)
    index = iota((ROWS, count), 0)
    values = jnp.zeros((ROWS, count), f32)
    pieces = (high.astype(f32), (ids - high * 256).astype(f32), seq.astype(f32), jnp.where(pos == 0, 1.0, 0.0), live)
    for number, row in enumerate(pieces):
        values = jnp.where(index == number, row, values)
    left, right = iota((count, count), 0), iota((count, count), 1)
    ahead = jnp.where(right < left, 1.0, 0.0).astype(bf16)
    same = jnp.where(right == left, 1.0, 0.0).astype(bf16)
    marks = jnp.broadcast_to(first, (ROWS, count)).astype(bf16)
    before = dot(ahead, marks, 1, 1)[:, :1]
    mine = dot(same, marks, 1, 1)[:, :1]
    total = jnp.sum(first, 1, keepdims=True)
    target = jnp.where(mine > 0.5, before, total + iota((count, 1), 0).astype(f32) - before)
    moves = jnp.where(target.astype(jnp.int32) == right, 1.0, 0.0).astype(bf16)
    return dot(values.astype(bf16), moves), total


def attend(xt, w, vec, moved, rows):
    g1, bq, bv, bo, be1 = vec[0:1], vec[3:4], vec[4:5], vec[5:6], vec[6:7]
    seq_id, slot0, live = moved[2:3], moved[3:4], moved[4:5]
    spread, columns = spread_table(rows), column_table(rows)
    index = iota((ROWS, xt.shape[1]), 0).astype(f32)
    pick0 = flag((index == seq_id) & (slot0 > 0.5)).astype(bf16)
    x00 = dot(pick0, xt, 1, 1)
    q = (dot(x00.astype(bf16), w(0)) + bq).astype(bf16)
    q_wide = (dot(spread, q) * columns).astype(bf16)
    qk = dot(q_wide, w(1), 1, 1) * HEAD_DIM ** (-0.5)
    mask = (sequence_of(iota((SIDE, 1), 0), rows).astype(f32) == seq_id) & (live > 0.5)
    scores = jnp.where(mask, dot_split(qk, xt), -1e30)
    raw = jnp.where(mask, jnp.exp(scores - jnp.max(scores, 1, keepdims=True)), 0.0)
    total = jnp.sum(raw, 1, keepdims=True)
    probs = raw / jnp.where(total > 0.0, total, 1.0)
    probs_low = probs.astype(bf16)
    y = dot(probs_low, xt, 1, 1)
    psum = jnp.sum(probs_low.astype(f32), 1, keepdims=True)
    mixed = dot_split(y, w(2)) + psum * bv
    o = dot(spread, (mixed * columns).astype(bf16), 0, 0).astype(bf16)
    normed, inv = layer_norm(x00 + dot(o, w(3)) + bo)
    return normed * g1 + be1, x00.astype(bf16), q, o, probs, psum, normed, inv, qk, y


def attend_back(dx1, normed, inv, probs, psum, xt, w, vec, rows):
    g1, bv = vec[0:1], vec[4:5]
    spread, columns = spread_table(rows), column_table(rows)
    d_res = norm_back(dx1, normed, inv, g1)
    d_a = d_res.astype(bf16)
    d_o = dot(d_a, w(3), 1, 1).astype(bf16)
    d_o_wide = dot(spread, d_o) * columns
    vd = dot(d_o_wide.astype(bf16), w(2), 1, 1)
    dp = dot_split(vd, xt) + jnp.sum(d_o_wide * bv, 1, keepdims=True)
    ds = (probs * (dp - jnp.sum(probs * dp, 1, keepdims=True))).astype(bf16)
    z = dot(ds, xt, 1, 1)
    zw = dot_split(z, w(1)) * (HEAD_DIM ** (-0.5)) * columns
    d_q = dot(spread, zw.astype(bf16), 0, 0).astype(bf16)
    extra = d_res + dot(d_q, w(0), 1, 1)
    sums = [
        jnp.sum(dx1 * normed, 0, keepdims=True),
        jnp.sum(dx1, 0, keepdims=True),
        jnp.sum(d_a.astype(f32), 0, keepdims=True),
        jnp.sum(d_q.astype(f32), 0, keepdims=True),
        jnp.sum(d_o_wide * psum, 0, keepdims=True),
    ]
    return d_a, d_o, d_q, sums, vd, z, extra, ds


def both_halves(value, rows):
    low = value.astype(bf16)
    return dot(place_table(rows, 0), low).T, dot(place_table(rows, SIDE), low).T


def table_block(halves, dest, block):
    first = 2 * block * dest
    return halves[0][first : first + block] + halves[1][first + block : first + 2 * block]


def weight_block(halves, dest, block, wide):
    return halves[0][block * dest : block * (dest + 1)] + halves[1][block * (wide + dest) : block * (wide + dest + 1)]


HEAD_LINES = 8


def pack_heads(value, rows):
    row, head = iota((HEAD_LINES, SIDE), 0), head_of(iota((HEAD_LINES, SIDE), 1), rows)
    most = dot(flag(row == head).astype(bf16), value)
    rest = [dot(flag((row - 4 * k + 8 == head) & (head >= 8) & (head < HEADS)).astype(bf16), value) for k in range(2)]
    cut = lambda t, k: t[:, k * LANES : (k + 1) * LANES]
    chunks = value.shape[1] // LANES
    tiles = [cut(most, k) for k in range(chunks)]
    for k in range(0, chunks, 2):
        tiles.append(cut(rest[0], k) + cut(rest[1], k + 1) if k + 1 < chunks else cut(rest[0], k))
    return jnp.concatenate(tiles, 0).astype(bf16)


def unpack_heads(lines, chunks):
    tile = lambda k: lines[k * HEAD_LINES : (k + 1) * HEAD_LINES].astype(f32)
    most = jnp.concatenate([tile(k) for k in range(chunks)], 1)
    rest = []
    for k in range(chunks):
        value = tile(chunks + k // 2)
        rest.append(pltpu.roll(value, 4, 0) if k % 2 else value)
    rest = jnp.concatenate(rest, 1)
    return jnp.concatenate([most, jnp.where(iota(rest.shape, 0) < HEADS - 8, rest, 0.0)], 0)


def head_lines(chunks):
    return HEAD_LINES * (chunks + (chunks + 1) // 2)


def to_tiles(value):
    return jnp.concatenate([value[:, k : k + LANES] for k in range(0, value.shape[1], LANES)], 0)


def from_tiles(got, first, lines=ROWS):
    pieces = [got[:, first + k * lines : first + (k + 1) * lines, :] for k in range(D // LANES)]
    return jnp.concatenate([p.reshape(-1, LANES) for p in pieces], 1)


def ffn(x1, w_up, w_down, bias):
    u = dot(x1.astype(bf16), w_up) + bias
    h = (0.5 * u * (1.0 + lax.erf(u * 0.5**0.5))).astype(bf16)
    return u, h, dot(h, w_down)


def middle(x1, f, u, w_up, w_down, w, vec, picks):
    g2, gc, b2, be2, bc, bec = vec[1:2], vec[2:3], vec[7:8], vec[8:9], vec[9:10], vec[10:11]
    count = x1.shape[0]
    valid, picks = picks[:, :1].astype(f32), picks[:, 1:]
    normed2, inv2 = layer_norm(x1 + (f + b2))
    pooled = (normed2 * g2 + be2).astype(bf16)
    normed_c, inv_c = layer_norm(dot(pooled, w(4)) + bc)
    e = (normed_c * gc + bec).astype(bf16)
    scores = dot(e, e, 1, 1) * D ** (-0.5)
    col = iota((count, count), 1)
    is_pos = jnp.where(col == picks[:, 0:1], 1.0, 0.0)
    negs = jnp.zeros_like(is_pos)
    for number in range(1, picks.shape[1]):
        negs = negs + jnp.where(col == picks[:, number : number + 1], 1.0, 0.0)
    taken = (is_pos + negs) > 0.0
    top = jnp.max(jnp.where(taken, scores, -1e30), 1, keepdims=True)
    raw = jnp.where(taken, jnp.exp(scores - top), 0.0)
    total = jnp.sum(raw * (is_pos + negs), 1, keepdims=True)
    total = jnp.where(total > 0.0, total, 1.0)
    share = raw / total
    valid_count = jnp.sum(valid, 0, keepdims=True)
    per_query = top + jnp.log(total) - jnp.sum(is_pos * scores, 1, keepdims=True)
    loss = jnp.sum(jnp.where(valid > 0.0, valid * per_query, 0.0), 0, keepdims=True) / valid_count
    weight = valid / valid_count
    d_pos = (weight * (share - 1.0)).astype(bf16).astype(f32)
    d_neg = (weight * share).astype(bf16).astype(f32)
    d_scores = d_pos * is_pos + d_neg * negs
    high, rest = split(d_scores)
    d_e = (dot(high, e) + dot(rest, e) + dot(high, e, 0, 0) + dot(rest, e, 0, 0)) * D ** (-0.5)
    d_c = norm_back(d_e, normed_c, inv_c, gc).astype(bf16)
    d_x2 = dot(d_c, w(4), 1, 1)
    d_res2 = norm_back(d_x2, normed2, inv2, g2)
    d_f = d_res2.astype(bf16)
    lines = u.shape[0]
    d_h = dot(d_f[:lines], w_down, 1, 1)
    slope = 0.5 * (1.0 + lax.erf(u * 0.5**0.5)) + u * jnp.exp(-0.5 * u * u) * (2.0 * np.pi) ** (-0.5)
    d_u = (d_h * slope).astype(bf16)
    d_x1 = dot(d_u, w_up, 1, 1)
    sums = [
        jnp.sum(d_x2 * normed2, 0, keepdims=True),
        jnp.sum(d_e * normed_c, 0, keepdims=True),
        jnp.sum(d_f.astype(f32), 0, keepdims=True),
        jnp.sum(d_x2, 0, keepdims=True),
        jnp.sum(d_c.astype(f32), 0, keepdims=True),
        jnp.sum(d_e, 0, keepdims=True),
    ]
    return loss, pooled, d_c, d_res2, d_f, d_u, d_x1, sums


def update(weight, first, second, gradient, rate, scale_one, scale_two):
    first_new = 0.9 * first + 0.1 * gradient
    second_new = 0.999 * second + 0.001 * gradient * gradient
    first_hat = first_new * scale_one
    second_hat = second_new * scale_two
    return weight - rate * (first_hat / (jnp.sqrt(second_hat) + 1e-08) + 0.01 * weight), first_new, second_new


def shape(dims, kind=f32):
    return jax.ShapeDtypeStruct(dims, kind)


MIB = 1 << 20


def full_block(dims):
    return pl.BlockSpec(dims, lambda i: (0,) * len(dims), pipeline_mode=pl.Buffered(1))


def pinned(x):
    return pltpu.with_memory_space_constraint(x, pltpu.HBM)


def call(kernel, outs, *args, scalars=(), far=(), far_outs=(), after=(), near=(), near_outs=(), scratch=(), vmem=24, name=None, flops=0):
    anywhere = pl.BlockSpec(memory_space=pl.ANY)
    in_specs = [pl.BlockSpec(memory_space=pltpu.SMEM)] * len(scalars) + [anywhere] * len(far)
    in_specs += [full_block(a.shape) for a in args] + [anywhere] * len(after)
    moved = sum(int(np.prod(a.shape)) * a.dtype.itemsize for a in list(args) + list(far) + list(outs) + list(far_outs))
    used = len(scalars) + len(far) + len(args)

    def run(*refs):
        kernel(*refs[:used], *refs[used + len(after) :])

    shapes = [o if k in near_outs else pltpu.HBM(o.shape, o.dtype) for k, o in enumerate(outs)]
    shapes += [pltpu.HBM(o.shape, o.dtype) for o in far_outs]
    args = [a if k in near else pinned(a) for k, a in enumerate(args)]
    return pl.pallas_call(
        run,
        grid=(1,),
        out_shape=shapes,
        in_specs=in_specs,
        out_specs=[full_block(o.shape) for o in outs] + [anywhere] * len(far_outs),
        scratch_shapes=list(scratch),
        compiler_params=pltpu.CompilerParams(vmem_limit_bytes=vmem * MIB),
        cost_estimate=pl.CostEstimate(flops=int(flops), bytes_accessed=moved, transcendentals=0),
        name=name,
    )(*scalars, *(pinned(a) for a in far), *args, *after)


def once(x, other):
    anywhere = pl.BlockSpec(memory_space=pl.ANY)
    return pl.pallas_call(
        lambda *refs: None,
        out_shape=pltpu.HBM(x.shape, x.dtype),
        in_specs=[anywhere, anywhere],
        out_specs=anywhere,
        input_output_aliases={0: 0},
        compiler_params=pltpu.CompilerParams(vmem_limit_bytes=MIB),
        name="once",
    )(pinned(x), other)


def square_weights(mats, first, buffers, signals, order):
    copies = {
        k: pltpu.make_async_copy(mats.at[:, pl.ds(k * D, D)], buffers.at[k - first], signals.at[k - first]) for k in order
    }
    for k in order:
        copies[k].start()
    ready = {}

    def get(k):
        if k not in ready:
            copies[k].wait()
            ready[k] = buffers[k - first]
        return ready[k]

    return get


def weight_scratch(count):
    return [pltpu.VMEM((count, D, D), bf16), pltpu.SemaphoreType.DMA((count,))]


def prepare_kernel(group_rows, rows, passages, queries, negatives, small, vectors, seq, pos, up, packet, moved):
    line_up = lambda ref: [ref[k : k + 1, :] for k in range(ref.shape[0])]
    ids = jnp.concatenate(line_up(passages) + line_up(queries), 1)
    count = ids.shape[1]
    chunks = count // LANES
    entries = small[...]
    live = jnp.zeros((1, count), f32)
    for number in range(rows):
        live = jnp.where((seq[...] == number) & (pos[...] < entries[:, number : number + 1]), 1.0, live)
    got, total = prepare(ids, live, seq[...], pos[...], group_rows)
    moved[...] = got
    code = got[2:3] + 8.0 * got[3:4]
    lane = iota((1, LANES), 1)
    at = 1 + 2 * queries.shape[0]
    after = LANES - at - negatives.shape[0] * negatives.shape[1]
    rest = [jnp.zeros((1, at), jnp.int32)] + line_up(negatives) + [jnp.zeros((1, after), jnp.int32)]
    note = pltpu.roll(entries.astype(f32), LANES - rows + 1, 1)
    note = jnp.where((lane < at) | (lane == LANES - 1), note, jnp.concatenate(rest, 1).astype(f32))
    high = lax.shift_right_logical(total.astype(jnp.int32), 8)
    note = jnp.where(lane == 0, total - 256.0 * high.astype(f32), jnp.where(lane == LANES - 1, high.astype(f32), note))
    lines = [line[:, k * LANES : (k + 1) * LANES] for line in (got[0:1], got[1:2], code) for k in range(chunks)]
    own = vectors.shape[1]
    given = jnp.concatenate([vectors[...], jnp.zeros((1, -own % LANES), f32)], 1)
    lines += [note] + [given[:, k : k + LANES] for k in range(0, given.shape[1], LANES)]
    wide, block = packet.shape[0], up.shape[0]
    hidden = up.shape[1] // (2 * wide)
    first = packet.shape[1] - 2 * block
    index = iota((first, LANES), 0)
    whole = jnp.zeros((first, LANES), f32)
    for number, line in enumerate(lines):
        whole = jnp.where(index == number, line, whole)
    gap = jnp.zeros((block, LANES - hidden), f32)
    for dest in range(wide):
        pieces = [jnp.concatenate([up[:, n * hidden : (n + 1) * hidden], gap], 1) for n in (dest, wide + dest)]
        packet[dest] = jnp.concatenate([whole] + pieces, 0).astype(bf16)


def cast_kernel(attn_in, attn_out, head, down, out, down_out):
    down_out[...] = down[...].astype(bf16)
    out[:, : 3 * D] = attn_in[...].astype(bf16)
    out[:, 3 * D : 4 * D] = attn_out[...].astype(bf16)
    out[:, 4 * D :] = head[...].astype(bf16)


def build_kernel(emb, table):
    feats, vocab = emb.shape
    half = table.shape[0]
    blocks, second = half // LANES, (vocab - half) // LANES
    gap = jnp.zeros((SIDE - feats, LANES), f32)

    def build(b, both):
        start = pl.multiple_of(b * LANES, LANES)
        low = emb[:, pl.ds(start, LANES)]
        high = jnp.zeros_like(low)
        if both:
            high = emb[:, pl.ds(pl.multiple_of(half + start, LANES), LANES)]
        table[pl.ds(start, LANES), :] = jnp.concatenate([low, gap, high, gap], 0).astype(bf16).T.astype(f32)

    unroll = 7

    def step(i, carry):
        for k in range(unroll):
            build(i * unroll + k, True)
        return carry

    lax.fori_loop(0, second // unroll, step, 0)
    for b in range(second // unroll * unroll, blocks):
        build(jnp.int32(b), b < second)


def side_of(packet, s, chunks, group, half_rows, half):
    ids = lanes_of(packet, s, 0, chunks) * 256.0 + lanes_of(packet, s, chunks, chunks)
    local = ids - (group * half_rows).astype(f32)
    inside = (local >= 0.0) & (local < float(half_rows))
    return jnp.where(inside, jnp.where(local >= float(half), 2.0, 1.0), 0.0)


def own_span(first, group, count):
    return jnp.where(group == 0, 0, first), jnp.where(group == 0, first, count)


def number_block(per, count):
    return pl.BlockSpec((1, 1, per * count), lambda i, *s: (i, 0, 0), memory_space=pltpu.SMEM)


def lookup_kernel(half_rows, per, unroll, where, firsts, numbers, packet, table, out, buf):
    feats, count = out.shape[1:]
    group = where[0]
    chunks = count // LANES
    half = table.shape[0]
    at = pl.program_id(0) * per
    for s in range(per):
        low, high = own_span(firsts[at + s], group, count)

        def step(i, carry):
            for k in range(unroll):
                t = i * unroll + k
                buf[pl.ds(s * count + t, 1), :] = table[pl.ds(numbers[0, 0, s * count + t], 1), :]
            return carry

        lax.fori_loop(low // unroll, (high + unroll - 1) // unroll, step, 0)
    for s in range(per):
        side = side_of(packet, s, chunks, group, half_rows, half)
        lines = [buf[s * count + c * LANES : s * count + (c + 1) * LANES, :].astype(bf16).T for c in range(chunks)]
        turned = jnp.concatenate(lines, 1).astype(f32)
        pick = jnp.where(side > 1.5, turned[SIDE : SIDE + feats], turned[:feats])
        value = jnp.where(side > 0.5, pick, 0.0)
        out[s] = value.astype(bf16)


def lanes_of(packet, s, first, chunks):
    return jnp.concatenate([packet[s, first + c : first + c + 1, :].astype(f32) for c in range(chunks)], 1)


def lookup(where, numbers, firsts, packets, table, half_rows, feats, count, per=4, unroll=64):
    sources = packets.shape[0]
    some = lambda dims: pl.BlockSpec((per,) + dims, lambda i, *s: (i, 0, 0))
    return pl.pallas_call(
        partial(lookup_kernel, half_rows, per, unroll),
        out_shape=shape((sources, feats, count), bf16),
        grid_spec=pltpu.PrefetchScalarGridSpec(
            num_scalar_prefetch=2,
            grid=(sources // per,),
            in_specs=[number_block(per, count), some(packets.shape[1:]), pl.BlockSpec(table.shape, lambda i, *s: (0, 0), pipeline_mode=pl.Buffered(1))],
            out_specs=some((feats, count)),
            scratch_shapes=[pltpu.VMEM((per * count, LANES), f32)],
        ),
        compiler_params=pltpu.CompilerParams(vmem_limit_bytes=16 * MIB),
        cost_estimate=pl.CostEstimate(flops=10**9, bytes_accessed=10**7, transcendentals=0),
        name="lookup",
    )(where, firsts, numbers.reshape(-1, 1, per * count), packets, pinned(table))


def spread_kernel(rows, half_rows, feats, per, unroll, copies, at_early, where, firsts, numbers, packet, early_own, early_other, late_own, late_other, p_heads, out, square, *scratch):
    parts, buf = scratch[:copies], scratch[copies]
    group = where[0]
    chunks = buf.shape[0] // (per * LANES)
    count = chunks * LANES
    half = parts[0].shape[0]
    vocab = out.shape[1]
    blocks = half // LANES
    step_at = pl.program_id(0)

    @pl.when(step_at == 0)
    def _():
        at_once = 3

        def clear(i, carry):
            for part in parts:
                for k in range(at_once):
                    part[pl.ds(pl.multiple_of((i * at_once + k) * LANES, LANES), LANES), :] = jnp.zeros((LANES, LANES), f32)
            return carry

        lax.fori_loop(0, blocks // at_once, clear, 0)
        for k in range(blocks // at_once * at_once, blocks):
            for part in parts:
                part[k * LANES : (k + 1) * LANES, :] = jnp.zeros((LANES, LANES), f32)

    gap = jnp.zeros((SIDE - feats, count), f32)
    block = feats // 2
    lane, slot = iota((LANES, 2 * LANES), 0), iota((LANES, 2 * LANES), 1)
    half_of = lax.shift_right_logical(slot, 7)
    slot = slot - half_of * LANES
    seq_of, head = lax.shift_right_logical(slot, 4), slot - lax.shift_right_logical(slot, 4) * STEP
    relane = flag((lane == half_of * SIDE + seq_of * HEADS + head) & (head < HEADS) & (seq_of < rows)).astype(bf16)
    empty = jnp.zeros((LANES - rows * STEP, count), f32)
    is_own = step_at < pl.num_programs(0) // 2

    def pick(own, other, s, first, lines):
        return jnp.where(is_own, own[s, first : first + lines, :], other[s, first : first + lines, :])

    for s in range(per):
        code = lanes_of(packet, s, 2 * chunks, chunks)
        slot0 = code >= 8.0
        seq = jnp.where(slot0, code - 8.0, code)
        scores = unpack_heads(pick(late_own, late_other, s, block + ROWS, head_lines(chunks)), chunks)
        values = unpack_heads(p_heads[s, : head_lines(chunks), :], chunks)
        parts_of = [jnp.where(seq == float(r), scores, 0.0) for r in range(rows)] + [empty]
        parts_of += [jnp.where(seq == float(r), values, 0.0) for r in range(rows)] + [empty]
        both = jnp.concatenate([pick(early_own, early_other, s, at_early, block), pick(late_own, late_other, s, 0, block)], 0)
        wide_rows = dot(both, relane).astype(bf16)
        basis = [jnp.concatenate([wide_rows[k : k + block, :LANES], wide_rows[k : k + block, LANES:]], 0) for k in (0, block)]
        x = dot(jnp.concatenate(basis, 1), jnp.concatenate(parts_of, 0).astype(bf16))
        first = flag((iota((ROWS, count), 0).astype(f32) == seq) & slot0).astype(bf16)
        x = x + dot(pick(late_own, late_other, s, block, ROWS), first, 0, 0)[:feats]
        side = side_of(packet, s, chunks, group, half_rows, half)
        tall = jnp.concatenate([jnp.where(side == 1.0, x, 0.0), gap, jnp.where(side == 2.0, x, 0.0), gap], 0).astype(bf16)
        for c in range(chunks):
            start = s * count + c * LANES
            buf[start : start + LANES, :] = tall[:, c * LANES : (c + 1) * LANES].T.astype(f32)
    for s in range(per):
        low, high = own_span(firsts[step_at * per + s], group, count)

        def step(i, carry):
            for k in range(unroll):
                t = i * unroll + k
                part = parts[k % copies]
                row = numbers[0, 0, s * count + t]
                part[pl.ds(row, 1), :] = part[pl.ds(row, 1), :] + buf[pl.ds(s * count + t, 1), :]
            return carry

        lax.fori_loop(low // unroll, (high + unroll - 1) // unroll, step, 0)

    @pl.when(step_at == pl.num_programs(0) - 1)
    def _():
        def emit(b, total, both):
            start = pl.multiple_of(b * LANES, LANES)
            lines = parts[0][pl.ds(start, LANES), :]
            for part in parts[1:]:
                lines = lines + part[pl.ds(start, LANES), :]
            turned = lines.T
            out[:, pl.ds(start, LANES)] = turned[:feats].astype(bf16)
            if both:
                out[:, pl.ds(pl.multiple_of(half + start, LANES), LANES)] = turned[SIDE : SIDE + feats].astype(bf16)
            return total + lines * lines

        second = (vocab - half) // LANES
        group_of = 14

        def several(i, total):
            for k in range(group_of):
                total = emit(i * group_of + k, total, True)
            return total

        total = lax.fori_loop(0, second // group_of, several, jnp.zeros((LANES, LANES), f32))
        for b in range(second // group_of * group_of, blocks):
            total = emit(jnp.int32(b), total, b < second)
        square[...] = jnp.sum(total.reshape(LANES // ROWS, ROWS, LANES), 0)


def spread_tokens(where, numbers, firsts, packets, early, late, p_heads, at_early, rows, half_rows, feats, count, per=8, unroll=40, copies=5):
    devices = packets.shape[0]
    block = packets.shape[1:]
    half = -(-half_rows // (2 * LANES)) * LANES
    some = lambda dims: pl.BlockSpec((per,) + dims, lambda i, *s: (i, 0, 0))
    steps = devices // per
    ordered = pl.BlockSpec((per, head_lines(count // LANES), LANES), lambda i, where, *s: ((i + where[0] * (steps // 2)) % steps, 0, 0))
    mine = lambda pair: pl.BlockSpec((per,) + pair[0].shape[1:], lambda i, *s: (jnp.minimum(i, steps // 2 - 1), 0, 0))
    theirs = lambda pair: pl.BlockSpec((per,) + pair[0].shape[1:], lambda i, *s: (jnp.maximum(i - steps // 2, 0), 0, 0))
    return pl.pallas_call(
        partial(spread_kernel, rows, half_rows, feats, per, unroll, copies, at_early),
        out_shape=[pltpu.HBM((feats, half_rows), bf16), pltpu.HBM((ROWS, LANES), f32)],
        grid_spec=pltpu.PrefetchScalarGridSpec(
            num_scalar_prefetch=2,
            grid=(steps,),
            in_specs=[number_block(per, count), some(block), mine(early), theirs(early), mine(late), theirs(late), ordered],
            out_specs=[pl.BlockSpec((feats, half_rows), lambda i, *s: (0, 0), pipeline_mode=pl.Buffered(1)), pl.BlockSpec((ROWS, LANES), lambda i, *s: (0, 0))],
            scratch_shapes=[pltpu.VMEM((half, LANES), f32)] * copies + [pltpu.VMEM((per * count, LANES), f32)],
        ),
        compiler_params=pltpu.CompilerParams(vmem_limit_bytes=52 * MIB),
        cost_estimate=pl.CostEstimate(flops=10**9, bytes_accessed=3 * 10**7, transcendentals=0),
        name="spread_tokens",
    )(where, firsts, numbers.reshape(-1, 1, per * count), packets, *early, *late, p_heads)


def attend_kernel(rows, mats, xt, vec, moved, sent, early, known, y_out, probs_out, psum_out, normed_out, inv_out, *scratch):
    w = square_weights(mats, 0, *scratch, (0, 1, 2, 3))
    x1, x00, q, o, probs, psum, normed, inv, qk, y = attend(xt[...], w, vec[...], moved[...], rows)
    tiles = to_tiles(x1)
    halves, heads = both_halves(qk, rows), pack_heads(probs.astype(bf16), rows)
    wide = sent.shape[0]
    block = D // (2 * wide)
    for dest in range(wide):
        sent[dest] = tiles.astype(bf16)
        early[dest] = table_block(halves, dest, block).astype(bf16)
    facts = jnp.concatenate([to_tiles(value.astype(f32)) for value in (x00, q, o)], 0).astype(bf16)
    known[...] = jnp.concatenate([heads, facts], 0)
    y_out[...] = y.astype(bf16)
    probs_out[...], psum_out[...], normed_out[...], inv_out[...] = probs, psum, normed, inv


def attend_back_kernel(rows, place, mats, got, d_res2, sums_up, normed, inv, probs, psum, xt, vec, late_out, last, z_out, *scratch):
    w = square_weights(mats, 0, *scratch, (3, 2, 1, 0))
    wide = late_out.shape[0]
    block = D // (2 * wide)
    feats = 2 * block
    dx1 = d_res2[pl.ds(pl.multiple_of(place[0] * ROWS, ROWS), ROWS), :]
    lines = ROWS * (D // LANES)
    tiles = got[0, :lines, :].astype(f32)
    for k in range(1, wide):
        tiles = tiles + got[k, :lines, :].astype(f32)
    dx1 = dx1 + jnp.concatenate([tiles[k : k + ROWS] for k in range(0, lines, ROWS)], 1)
    d_a, d_o, d_q, sums, vd, z, extra, ds = attend_back(
        dx1, normed[...], inv[...], probs[...], psum[...], xt[...], w, vec[...], rows
    )
    halves = both_halves(vd, rows)
    heads = pack_heads(ds, rows)
    gap = jnp.zeros((ROWS, LANES - feats), f32)
    for dest in range(wide):
        row_part = jnp.concatenate([extra[:, feats * dest : feats * (dest + 1)], gap], 1)
        late_out[dest] = jnp.concatenate([jnp.concatenate([table_block(halves, dest, block), row_part], 0).astype(bf16), heads], 0)
    z_out[...] = z.astype(bf16)
    sums = sums + [sums_up[...]]
    index = iota((ROWS, D), 0)
    spare = ROWS - rows
    values = [d_q.astype(f32), d_o.astype(f32), d_a.astype(f32)]
    for number, row in enumerate(sums):
        values[number // spare] = jnp.where(index == rows + number % spare, row, values[number // spare])
    last[...] = jnp.concatenate([to_tiles(value) for value in values], 0).astype(bf16)


def pack_kernel(rows, last, y, z, d_up, d_up_other, out):
    wide = out.shape[0]
    block = d_up.shape[0] // wide
    hidden = d_up.shape[1] // 2
    values = last[...]
    halves_y, halves_z = both_halves(y[...], rows), both_halves(z[...], rows)
    up = d_up[...] + d_up_other[...].astype(f32)
    gap = jnp.zeros((block, LANES - hidden), f32)
    for dest in range(wide):
        mine = up[block * dest : block * (dest + 1), :]
        pieces = [jnp.concatenate([mine[:, k * hidden : (k + 1) * hidden], gap], 1) for k in range(2)]
        pieces += [weight_block(halves_y, dest, block, wide), weight_block(halves_z, dest, block, wide)]
        out[dest] = jnp.concatenate([values, jnp.concatenate(pieces, 0).astype(bf16)], 0)


def rows_of(own, other):
    return jnp.concatenate([from_tiles(own[...], 0), from_tiles(other[...], 0)], 0)


def by_core(where, own, other):
    first = where[0] == 0
    return jnp.concatenate([jnp.where(first, own[...], other[...]), jnp.where(first, other[...], own[...])], 0)


def ffn_kernel(where, x_own, w_up, down_own, down_other, bias, u_out, h_out, out):
    u, h, f = ffn(from_tiles(x_own[...], 0), w_up[...], by_core(where, down_own, down_other), bias[...])
    u_out[...], h_out[...] = u, h
    out[...] = f.astype(bf16)


def total_kernel(got, out):
    total = got[0].astype(f32)
    for k in range(1, got.shape[0]):
        total = total + got[k].astype(f32)
    lines = to_tiles(total).astype(bf16)
    for k in range(out.shape[0]):
        out[k] = lines


def middle_kernel(where, mats, x_own, x_other, f_own, f_other, u, w_up, down_own, down_other, vec, picks, early, loss, pooled, d_c, d_res2, d_f, d_u, out, sums, sums_up, *scratch):
    w = square_weights(mats, 4, *scratch, (4,))
    x1 = rows_of(x_own, x_other).astype(f32)
    f = rows_of(f_own, f_other).astype(f32)
    got = middle(x1, f, u[...], w_up[...], by_core(where, down_own, down_other), w, vec[...], picks[...])
    lines = u.shape[0]
    loss[...], pooled[...], d_c[...], d_res2[...] = got[:4]
    d_f[...], d_u[...] = got[4][:lines], got[5]
    for dest in range(out.shape[0]):
        part = to_tiles(got[6][dest * ROWS : (dest + 1) * ROWS]).astype(bf16)
        out[dest] = jnp.concatenate([part, early[dest]], 0)
    sums[...] = stack_rows(got[7])
    su = jnp.sum(got[5].astype(f32), 0, keepdims=True)
    sums_up[...] = jnp.concatenate([su, jnp.zeros((1, D - su.shape[1]), f32)], 1)


def own_cols(device, block):
    index = iota((D, LANES), 1)
    return flag((iota((D, LANES), 0) == device * block + index) & (index < block)).astype(bf16)


def own_rows(left, right, mine, block):
    return dot(dot(left, mine).astype(bf16), right, 0, 0)[:block]


def ffn_grads_kernel(where, x_own, h, d_f, d_u, pooled, d_c, down_mine, down_theirs, d_head, up_mine, up_theirs):
    first = where[0] == 0
    hidden = down_mine.shape[0]
    half = up_mine.shape[0]
    d_up = dot(from_tiles(x_own[...], 0), d_u[...], 0, 0)
    up_mine[...] = jnp.where(first, d_up[:half], d_up[half:])
    up_theirs[...] = jnp.where(first, d_up[half:], d_up[:half]).astype(bf16)
    d_down = dot(h[...], d_f[...], 0, 0)
    down_mine[...] = jnp.where(first, d_down[:hidden], d_down[hidden:])
    down_theirs[...] = jnp.where(first, d_down[hidden:], d_down[:hidden]).astype(bf16)
    block = d_head.shape[0]
    d_head[...] = own_rows(pooled[...], d_c[...], own_cols(where[1], block), block)


def grads_kernel(rows, where, known, facts_own, facts_other, d_wh, down_mine, down_other, sums, square, in_out, out_out, up_out, down_out, vec_out, square_out, x00, q_all, o_all, d_q, d_o, d_a, y, z, wide_z):
    group, device = where[0], where[1]
    wide = facts_own.shape[0]
    devices = 2 * wide
    block = in_out.shape[0]
    hidden = FF // devices
    first = group == 0
    lines = ROWS * (D // LANES)
    at_up = 3 * lines
    for base, facts in ((0, facts_own), (1, facts_other)):
        at = slice(base * wide * ROWS, (base + 1) * wide * ROWS)
        kept = known[pl.ds(((base + group) % 2) * wide, wide), known.shape[1] - 3 * lines :, :]
        for k, out in enumerate((x00, q_all, o_all)):
            out[at, :] = from_tiles(kept, k * lines).astype(f32)
        for k, out in enumerate((d_q, d_o, d_a)):
            out[at, :] = from_tiles(facts, k * lines).astype(f32)
        for n in range(wide):
            at = slice((base * wide + n) * block, (base * wide + n + 1) * block)
            y[at, :] = facts[n, at_up + 2 * block : at_up + 3 * block, :].astype(f32)
            z[at, :] = facts[n, at_up + 3 * block : at_up + 4 * block, :].astype(f32)
    for n in range(wide):
        for k in range(2):
            piece = facts_own[n, at_up + k * block : at_up + (k + 1) * block, :].astype(f32)
            at = (k * wide + n) * hidden
            up_out[:, at : at + hidden] = piece[:, :hidden]
    down_out[...] = down_mine[...] + down_other[...].astype(f32)

    def by_heads(source, values):
        total = jnp.zeros((block, D), f32)
        low = source[...].astype(bf16)
        for r in range(rows):
            wide_z[...] = dot(low, expand_table(rows, jnp.where(group == 0, 0, SIDE), r))
            for n in range(devices):
                total = total + wide_z[n * block : (n + 1) * block, :] * values[n * ROWS + r : n * ROWS + r + 1, :]
        return total

    d_wk = by_heads(z, q_all) * HEAD_DIM ** (-0.5)
    d_wv = by_heads(y, d_o)
    mine = own_cols(device, block)
    d_wq = own_rows(x00[...].astype(bf16), d_q[...].astype(bf16), mine, block)
    d_wo = own_rows(o_all[...].astype(bf16), d_a[...].astype(bf16), mine, block)
    square_now = square[...]

    def fold(square_now, value):
        tiles = value * value
        total = jnp.sum(tiles.reshape(tiles.shape[0] // ROWS, ROWS, tiles.shape[1]), 0)
        for k in range(total.shape[1] // LANES):
            square_now = square_now + total[:, k * LANES : (k + 1) * LANES]
        return square_now

    in_out[:, :D], in_out[:, D : 2 * D], in_out[:, 2 * D :] = d_wq, d_wk, d_wv
    out_out[...] = d_wo
    for value in (d_wq, d_wk, d_wv, d_wo, d_wh[...], up_out[...], down_out[...]):
        square_now = fold(square_now, value)
    spare = ROWS - rows
    grouped = [jnp.sum(t[...].reshape(devices, ROWS, D), 0) for t in (d_q, d_o)]
    tail = [grouped[k // spare][rows + k % spare : rows + k % spare + 1] for k in range(5)]
    mids = sums[...]
    pieces = [tail[0], mids[0:1], mids[1:2], tail[3], tail[4], tail[2], tail[1]] + [mids[k : k + 1] for k in range(2, 6)]
    index = iota((16, D), 0)
    total = jnp.zeros((16, D), f32)
    for number, row in enumerate(pieces):
        total = jnp.where(index == number, row, total)
    each = D // hidden
    for k in range(wide):
        lines_of = [(base * wide + k) * ROWS + rows + 5 % spare for base in range(2)]
        source = (d_q, d_o)[5 // spare]
        row = source[lines_of[0] : lines_of[0] + 1, :] + source[lines_of[1] : lines_of[1] + 1, :]
        for core in range(2):
            shift = (hidden * (k % each) - hidden * core) % D
            turned = pltpu.roll(row, shift, 1) if shift else row
            col = iota((1, D), 1)
            turned = jnp.where((col >= hidden * (k % each)) & (col < hidden * (k % each + 1)), turned, 0.0)
            total = total + jnp.where(index == 11 + (core * wide + k) // each, turned, 0.0)
    vec_out[...] = total
    square_now = square_now + fold(jnp.zeros((ROWS, LANES), f32), total) / devices
    for k in range(devices):
        square_out[k] = square_now


def adam_kernel(count, scales, weight, first, second, d_table, got, *refs):
    grads, state = refs[:count], refs[count : 4 * count]
    norm_out, factor_out = refs[4 * count : 4 * count + 2]
    outs = refs[4 * count + 2 : 7 * count + 2]
    far = refs[7 * count + 2 : 7 * count + 5]
    loads, grad_loads, stores, got_in, sent = refs[7 * count + 5 :]
    slots, lines = loads.shape[0], loads.shape[2]
    jobs = weight.shape[0] // lines
    sources = (weight, first, second, d_table)

    def load(j):
        places = [loads.at[j % slots, k] for k in range(3)] + [grad_loads.at[j % slots]]
        return [
            pltpu.make_async_copy(ref.at[pl.ds(j * lines, lines), :], place, got_in.at[j % slots, k])
            for k, (ref, place) in enumerate(zip(sources, places))
        ]

    def store(j):
        return [pltpu.make_async_copy(stores.at[j % slots, k], ref.at[pl.ds(j * lines, lines), :], sent.at[j % slots, k]) for k, ref in enumerate(far)]

    for j in range(min(slots, jobs)):
        for copy in load(j):
            copy.start()
    total = got[0]
    for k in range(1, got.shape[0]):
        total = total + got[k]
    total = jnp.sum(jnp.sum(total, 0, keepdims=True), 1, keepdims=True)
    norm = jnp.sqrt(total)
    factor = jnp.minimum(1.0, clip_level / (norm + 1e-06))
    norm_out[...], factor_out[...] = norm, factor
    one, two = scales[0], scales[1]
    for j in range(jobs):
        for copy in load(j):
            copy.wait()
        if j >= slots:
            for copy in store(j - slots):
                copy.wait()
        old = [loads[j % slots, k] for k in range(3)]
        new = update(*old, grad_loads[j % slots].astype(f32) * factor, RATES[0], one, two)
        for k in range(3):
            stores[j % slots, k] = new[k]
        for copy in store(j):
            copy.start()
        if j + slots < jobs:
            for copy in load(j + slots):
                copy.start()
    for number in range(count):
        old = [state[3 * number + k][...] for k in range(3)]
        new = update(*old, grads[number][...] * factor, RATES[number + 1], one, two)
        for k in range(3):
            outs[3 * number + k][...] = new[k]
    for j in range(max(0, jobs - slots), jobs):
        for copy in store(j):
            copy.wait()


def swap(x):
    return lax.ppermute(x, "group", [(0, 1), (1, 0)])


def exchange(x):
    return lax.all_to_all(x, "wide", split_axis=0, concat_axis=0, tiled=True)


def tie(*values):
    return lax.optimization_barrier(values)


def pair(x):
    own = exchange(x)
    return own, swap(own)


def in_order(own, other, group):
    return jnp.where(group == 0, jnp.concatenate([own, other], 0), jnp.concatenate([other, own], 0))


def plain_body(wide, passage_ids, query_ids, passage_len, query_len, positive, negatives, valid, step_count, *state):
    params, firsts, seconds = state[0::3], state[1::3], state[2::3]
    embedding, attn_in, attn_out, w_ffn_up, w_ffn_down, head, vectors = params
    group, place = lax.axis_index("group"), lax.axis_index("wide")
    device, devices = group * wide + place, 2 * wide
    feats, half_rows = embedding.shape
    block, hidden = D // devices, FF // devices
    pas_count, pas_len = passage_ids.shape
    qry_count, qry_len = query_ids.shape
    rows = pas_count + qry_count
    tokens = pas_count * pas_len + qry_count * qry_len
    live = rows * HEADS
    both = lambda x: jnp.concatenate(pair(x), 0)
    gather = lambda x: both(jnp.broadcast_to(x[None], (wide,) + x.shape))
    ids = jnp.concatenate([passage_ids.reshape(-1), query_ids.reshape(-1)])
    seq_np = np.concatenate([np.repeat(np.arange(pas_count), pas_len), pas_count + np.repeat(np.arange(qry_count), qry_len)])
    pos_np = np.concatenate([np.tile(np.arange(pas_len), pas_count), np.tile(np.arange(qry_len), qry_count)])
    lens = jnp.concatenate([jnp.repeat(passage_len, pas_len), jnp.repeat(query_len, qry_len)])
    moved = jnp.zeros((ROWS, tokens), f32).at[2].set(jnp.asarray(seq_np, f32)).at[3].set(jnp.asarray(pos_np == 0, f32))
    moved = moved.at[4].set(flag(jnp.asarray(pos_np) < lens))
    note = jnp.concatenate([ids, valid, positive, negatives.reshape(-1)])
    notes = gather(jnp.pad(note, (0, -note.shape[0] % LANES)).reshape(-1, LANES)).reshape(devices, -1)
    low_vectors = gather(jnp.pad(vectors.astype(bf16), (0, -vectors.shape[0] % LANES)).reshape(-1, LANES))
    vec = in_order(low_vectors[:wide], low_vectors[wide:], group).reshape(devices, -1)[:, : vectors.shape[0]].astype(f32).reshape(-1, D)
    all_ids = notes[:, :tokens]
    valid_rows = jnp.pad(notes[:, tokens : tokens + qry_count].astype(f32), ((0, 0), (pas_count, ROWS - rows))).reshape(-1, 1)
    at = tokens + qry_count
    picked = jnp.concatenate(
        [notes[:, at : at + qry_count, None], notes[:, at + qry_count : at + qry_count + negatives.size].reshape(devices, qry_count, -1)], 2
    )
    pick_dev = picked // pas_count
    pick_row = (((pick_dev // wide) ^ group) * wide + pick_dev % wide) * ROWS + picked % pas_count
    pick_rows = jnp.pad(pick_row, ((0, 0), (pas_count, ROWS - rows), (0, 0)), constant_values=-1).reshape(devices * ROWS, -1)
    mats = lax.all_gather(jnp.concatenate([attn_in, attn_out, head], 1).astype(bf16), ALL, axis=0, tiled=True)
    w = lambda k: mats[:, k * D : (k + 1) * D]
    w_up = lax.all_to_all(
        w_ffn_up.astype(bf16).reshape(block, devices, hidden).transpose(1, 0, 2), ALL, split_axis=0, concat_axis=0, tiled=True
    ).reshape(D, hidden)
    w_down = w_ffn_down.astype(bf16)
    bias_up = lax.dynamic_slice(vec.reshape(-1), (11 * D + device * hidden,), (hidden,))[None]
    local = all_ids - group * half_rows
    inside = ((local >= 0) & (local < half_rows)).reshape(1, -1)
    local = jnp.clip(local, 0, half_rows - 1).reshape(-1)
    looked = jnp.where(inside, jnp.take(embedding.astype(bf16), local, axis=1), jnp.zeros((), bf16))
    looked = looked.reshape(feats, devices, tokens).transpose(1, 0, 2)
    xt = exchange(looked[:wide] + swap(looked[wide:])).reshape(D, tokens)
    x1, x00, q, o, probs, psum, normed1, inv1, qk, y = attend(xt, w, vec, moved, rows)
    p_heads = dot(heads_table(rows), probs.astype(bf16)).astype(bf16)
    x1_all = gather(x1.astype(bf16)).reshape(devices * ROWS, D)

    def to_owner(parts):
        mine = parts[: wide * ROWS] + swap(parts[wide * ROWS :])
        return jnp.sum(exchange(mine.astype(bf16).reshape(wide, ROWS, D)).astype(f32), 0)

    u, h, f_part = ffn(x1_all, w_up, w_down, bias_up)
    f_all = gather(to_owner(f_part).astype(bf16)).reshape(devices * ROWS, D).astype(f32)
    loss, pooled, d_c, d_res2, d_f, d_u, d_x1, sums = middle(x1_all.astype(f32), f_all, u, w_up, w_down, w, vec, jnp.concatenate([valid_rows.astype(jnp.int32), pick_rows], 1))
    d_x1 = lax.dynamic_slice(d_res2, (place * ROWS, 0), (ROWS, D)) + to_owner(d_x1)
    d_a, d_o, d_q, sums_back, vd, z, extra, ds = attend_back(d_x1, normed1, inv1, probs, psum, xt, w, vec, rows)

    to_features = lambda t: both(t.T.astype(bf16).reshape(wide, feats, -1))

    def to_blocks(t):
        parts = t.T.astype(bf16).reshape(2, wide, block, -1).transpose(1, 0, 2, 3).reshape(wide, 2 * block, -1)
        got = both(parts).reshape(devices, 2, block, -1)
        return lax.dynamic_index_in_dim(got, group, 1, keepdims=False)[:, :, :live].reshape(devices, block, rows, HEADS)

    facts = gather(jnp.concatenate([x00, q, o, d_q, d_o, d_a], 0)).reshape(devices, 6, ROWS, D)
    flat_fact = lambda k: facts[:, k].reshape(devices * ROWS, D)
    by_head = lambda k: facts[:, k].reshape(devices, ROWS, HEADS, HEAD_DIM)[:, :rows]
    cut = lambda m: lax.dynamic_slice(m, (0, device * block), (devices * ROWS, block))
    d_wq = dot(cut(flat_fact(0)), flat_fact(3), 0, 0)
    d_wk = jnp.einsum("nfrh,nrhd->fhd", to_blocks(z), by_head(1), preferred_element_type=f32).reshape(block, D) * HEAD_DIM ** (-0.5)
    d_wv = jnp.einsum("nfrh,nrhd->fhd", to_blocks(y), by_head(4), preferred_element_type=f32).reshape(block, D)
    d_wo = dot(cut(flat_fact(2)), flat_fact(5), 0, 0)
    d_wup = dot(x1_all, d_u, 0, 0).astype(bf16).reshape(devices, block, hidden)
    d_wup = lax.all_to_all(d_wup, ALL, split_axis=0, concat_axis=0, tiled=True).astype(f32).transpose(1, 0, 2).reshape(block, FF)
    sums_up = jnp.pad(jnp.sum(d_u.astype(f32), 0, keepdims=True), ((0, 0), (0, D - hidden)))
    tails = gather(stack_rows(sums_back + [sums_up]))
    tail = jnp.sum(tails, 0)
    ups = in_order(tails[:wide], tails[wide:], group)[:, 5, :hidden].reshape(-1)
    mids = [row[0] for row in sums]
    d_vec = jnp.concatenate([tail[0], mids[0], mids[1], tail[3], tail[4], tail[2], tail[1]] + mids[2:] + [ups])
    d_vec = lax.dynamic_slice(d_vec, (device * vectors.shape[0],), vectors.shape)
    basis = jnp.concatenate([to_features(qk), to_features(vd), to_features(extra)], 2)
    lanes = gather(jnp.concatenate([dot(heads_table(rows), ds).astype(bf16), p_heads], 0))
    seq = jnp.asarray(seq_np, jnp.int32)[None]
    here = sequence_of(iota((SIDE, 1), 0), rows) == seq
    widen = lambda t: jnp.where(here[None], jnp.einsum("ha,nht->nat", heads_table(rows), t, preferred_element_type=f32), 0.0).astype(bf16)
    first = ((iota((ROWS, 1), 0) == seq) & jnp.asarray(pos_np == 0)[None]).astype(bf16)
    coef = jnp.concatenate([widen(lanes[:, :16]), widen(lanes[:, 16:]), jnp.broadcast_to(first[None], (devices,) + first.shape)], 1)
    d_tok = jnp.einsum("nfa,nat->fnt", basis, coef, preferred_element_type=f32).reshape(feats, -1)
    d_table = jnp.zeros((feats, half_rows), f32).at[:, local].add(jnp.where(inside, d_tok, 0.0))
    d_head = dot(cut(pooled), d_c, 0, 0)
    grads = (d_table, jnp.concatenate([d_wq, d_wk, d_wv], 1), d_wo, d_wup, dot(h, d_f, 0, 0), d_head, d_vec)
    squares = sum(jnp.sum(g * g) for g in grads)
    grad_norm = jnp.sqrt(jnp.sum(gather(jnp.full((ROWS, LANES), squares))[:, 0, 0]))
    factor = jnp.minimum(1.0, clip_level / (grad_norm + 1e-06))
    step_float = step_count[0].astype(f32)
    one, two = 1.0 / (1.0 - jnp.power(0.9, step_float)), 1.0 / (1.0 - jnp.power(0.999, step_float))
    new = [update(params[k], firsts[k], seconds[k], grads[k] * factor, RATES[k], one, two) for k in range(7)]
    return (loss[0, 0], grad_norm) + tuple(t for group_of in new for t in group_of)


def body(wide, passage_ids, query_ids, passage_len, query_len, positive, negatives, valid, step_count, *state):
    embedding, attn_in, attn_out, w_ffn_up, w_ffn_down, head, vectors = state[0::3]
    group = lax.axis_index("group")
    place = lax.axis_index("wide")
    device = group * wide + place
    devices = 2 * wide
    feats, half_rows = embedding.shape
    block = D // devices
    hidden = FF // devices
    pas_count, pas_len = passage_ids.shape
    qry_count, qry_len = query_ids.shape
    rows = pas_count + qry_count
    tokens = pas_count * pas_len + qry_count * qry_len
    chunks = tokens // LANES
    half = -(-half_rows // (2 * LANES)) * LANES
    where = jnp.stack([group, device]).astype(jnp.int32)
    place_at = place.astype(jnp.int32)[None]
    lines = wide * ROWS

    seq_np = np.concatenate([np.repeat(np.arange(pas_count), pas_len), pas_count + np.repeat(np.arange(qry_count), qry_len)])
    pos_np = np.concatenate([np.tile(np.arange(pas_len), pas_count), np.tile(np.arange(qry_len), qry_count)])
    vec_lines = -(-vectors.shape[0] // LANES)
    packet_lines = -(-(3 * chunks + 1 + vec_lines) // ROWS) * ROWS + 2 * block
    at_note = 3 * chunks
    pieces = [passage_len, query_len, valid, positive]
    size = sum(t.shape[0] for t in pieces)
    assert size + negatives.size < LANES - 1
    small = jnp.concatenate(pieces + [jnp.zeros((LANES - size,), jnp.int32)])[None]
    packet, moved = call(
        partial(prepare_kernel, half_rows, rows),
        [shape((wide, packet_lines, LANES), bf16), shape((ROWS, tokens))],
        passage_ids, query_ids, negatives, small, vectors[None], jnp.asarray(seq_np, jnp.int32)[None], jnp.asarray(pos_np, jnp.int32)[None], w_ffn_up,
        near_outs=(0,), name="prepare",
    )
    packet_own = exchange(packet)
    (table,) = call(build_kernel, [shape((half, LANES))], embedding, name="build", flops=10**8)
    packet_own, table = tie(packet_own, table)
    packet_other = swap(packet_own)
    low_mats, down_low = call(
        cast_kernel, [shape((block, 5 * D), bf16), shape((hidden, D), bf16)],
        attn_in, attn_out, head, w_ffn_down, near_outs=(0,), name="cast",
    )
    mats = lax.all_gather(low_mats, ALL, axis=0, tiled=True)

    def numbers_of(packets):
        ids = packets[:, :chunks].astype(f32) * 256.0 + packets[:, chunks : 2 * chunks].astype(f32)
        local = ids - (group * half_rows).astype(f32)
        row_at = jnp.clip(jnp.where(local >= half, local - half, local), 0, half - 1)
        first = packets[:, at_note, 0].astype(f32) + 256.0 * packets[:, at_note, LANES - 1].astype(f32)
        return row_at.astype(jnp.int32).reshape(-1), first.astype(jnp.int32)

    look = partial(lookup, half_rows=half_rows, feats=feats, count=tokens)
    num_own, num_other = numbers_of(packet_own), numbers_of(packet_other)
    theirs = look(where, *num_other, packet_other, table)
    xt = exchange(look(where, *num_own, packet_own, table) + swap(theirs)).reshape(D, tokens)
    numbers = jnp.concatenate([num_own[0], num_other[0]])
    firsts = jnp.concatenate([num_own[1], num_other[1]])
    packets = jnp.concatenate([packet_own, packet_other], 0)
    ordered = in_order(packet_own, packet_other, group)
    w_up = ordered[:, packet_lines - 2 * block :, :hidden].reshape(devices, 2, block, hidden).transpose(0, 2, 1, 3).reshape(D, 2 * hidden)
    vec = ordered[:, at_note + 1 : at_note + 1 + vec_lines].astype(f32).reshape(devices, -1)
    vec = vec[:, : vectors.shape[0]].reshape(-1, D)
    bias_all = vec[11:].reshape(2, wide, hidden)
    bias_up = lax.dynamic_slice(bias_all, (0, place, 0), (2, 1, hidden)).reshape(1, 2 * hidden)
    notes = packets[:, at_note].astype(f32)
    at = 1 + qry_count
    picked = jnp.concatenate(
        [notes[:, at : at + qry_count, None], notes[:, at + qry_count : at + qry_count + negatives.size].reshape(devices, qry_count, -1)], 2
    ).astype(jnp.int32)
    pick_dev = picked // pas_count
    pick_row = (((pick_dev // wide) ^ group) * wide + pick_dev % wide) * ROWS + picked % pas_count
    pick_row = jnp.concatenate([notes[:, 1 : 1 + qry_count, None].astype(jnp.int32), pick_row], 2)
    pick_rows = jnp.pad(pick_row, ((0, 0), (pas_count, ROWS - rows), (0, 0))).reshape(devices * ROWS, -1)

    xt, vec, bias_up, pick_rows, w_up, packets, numbers, firsts = tie(xt, vec, bias_up, pick_rows, w_up, packets, numbers, firsts)
    tile_lines = ROWS * (D // LANES)
    heads_at, units = head_lines(chunks), 2 * hidden
    sent, early, known, y, probs, psum, normed1, inv1 = call(
        partial(attend_kernel, rows),
        [
            shape((wide, tile_lines, LANES), bf16), shape((wide, block, LANES), bf16), shape((heads_at + 3 * tile_lines, LANES), bf16),
            shape((SIDE, D), bf16), shape((SIDE, tokens)), shape((SIDE, 1)), shape((ROWS, D)), shape((ROWS, 1)),
        ],
        xt, vec, moved,
        far=(mats,), near=(0,), near_outs=(0,), scratch=weight_scratch(4), name="attend", flops=10**9,
    )
    x_own, x_other = pair(sent)
    known_all = lax.all_gather(known, ALL, axis=0, tiled=False)
    down_other = swap(down_low)
    u, h, f_mine = call(
        ffn_kernel, [shape((lines, units)), shape((lines, units), bf16), shape((lines, D), bf16)], x_own, w_up, down_low, down_other, bias_up,
        scalars=(where,), near=(0, 3), near_outs=(2,), name="ffn", flops=10**8, vmem=16,
    )
    f_parts = exchange(f_mine.reshape(wide, ROWS, D))
    (f_sum,) = call(total_kernel, [shape((wide, tile_lines, LANES), bf16)], f_parts, near=(0,), near_outs=(0,), name="total")
    f_own, f_other = pair(f_sum)
    loss, pooled, d_c, d_res2, d_f, d_u, d_sum, sums, sums_up = call(
        middle_kernel,
        [
            shape((1, 1)), shape((devices * ROWS, D), bf16), shape((devices * ROWS, D), bf16), shape((devices * ROWS, D)),
            shape((lines, D), bf16), shape((lines, units), bf16), shape((wide, tile_lines + block, LANES), bf16),
            shape((ROWS, D)), shape((1, D)),
        ],
        x_own, x_other, f_own, f_other, u, w_up, down_low, down_other, vec, pick_rows, early,
        scalars=(where,), far=(mats,), scratch=weight_scratch(1), near=(0, 1, 2, 3), near_outs=(6,), name="middle", flops=10**9, vmem=32,
    )
    got = exchange(d_sum)
    got_other = swap(got)
    down_mine, down_theirs, d_whead, up_mine, up_theirs = call(
        ffn_grads_kernel,
        [shape((hidden, D)), shape((hidden, D), bf16), shape((block, D)), shape((D // 2, units)), shape((D // 2, units), bf16)],
        x_own, h, d_f, d_u, pooled, d_c,
        scalars=(where,), after=(d_sum,), near=(0,), name="ffn_grads", flops=10**8,
    )
    late, last, z = call(
        partial(attend_back_kernel, rows),
        [shape((wide, block + ROWS + heads_at, LANES), bf16), shape((3 * tile_lines, LANES), bf16), shape((SIDE, D), bf16)],
        got, d_res2, sums_up, normed1, inv1, probs, psum, xt, vec,
        scalars=(place_at,), far=(mats,), after=(pinned(up_mine),), near=(0,), near_outs=(0,), scratch=weight_scratch(4), name="attend_back", flops=10**9,
    )
    late_own, late_other = pair(late)
    (packed,) = call(
        partial(pack_kernel, rows), [shape((wide, 3 * tile_lines + 4 * block, LANES), bf16)], last, y, z, up_mine, swap(up_theirs),
        after=(late,), near=(4,), name="pack",
    )
    last_own = exchange(once(packed, late_own))
    d_table, square = spread_tokens(
        where, numbers, firsts, packets, (got, got_other), (late_own, late_other), known_all, tile_lines, rows, half_rows, feats, tokens
    )
    piece = last_own[:1, :ROWS] + (square[None] * 0.0).astype(bf16)
    last_own = lax.dynamic_update_slice(last_own, piece, (0, 0, 0))
    last_other = swap(last_own)
    d_attn_in, d_wo, d_wup, d_down, d_vec, squares = call(
        partial(grads_kernel, rows),
        [shape((block, 3 * D)), shape((block, D)), shape((block, FF)), shape((hidden, D)), shape((16, D)), shape((devices, ROWS, LANES))],
        known_all, last_own, last_other, d_whead, down_mine, swap(down_theirs), sums, square,
        scalars=(where,),
        scratch=[pltpu.VMEM((devices * ROWS, D), f32)] * 6 + [pltpu.VMEM((D, LANES), f32)] * 2 + [pltpu.VMEM((D, D), f32)],
        near=(1, 2, 5), near_outs=(5,), name="grads", flops=10**9, vmem=32,
    )
    squares_got = lax.all_to_all(squares, ALL, split_axis=0, concat_axis=0, tiled=True)
    d_vectors = lax.dynamic_slice(d_vec.reshape(-1), (device * vectors.shape[0],), vectors.shape)
    step_float = step_count[0].astype(f32)
    scales = jnp.stack([1.0 / (1.0 - jnp.power(0.9, step_float)), 1.0 / (1.0 - jnp.power(0.999, step_float))])
    grads = (d_attn_in, d_wo, d_wup, d_down, d_whead)
    middle_state = state[3:18]
    slots, step_rows = 3, ROWS
    norm, factor, *new = call(
        partial(adam_kernel, len(grads)),
        [shape((1, 1)), shape((1, 1))] + [shape(t.shape) for t in middle_state],
        squares_got, *grads, *middle_state,
        scalars=(scales,), far=(*state[:3], d_table), far_outs=[shape(embedding.shape)] * 3,
        scratch=[
            pltpu.VMEM((slots, 3, step_rows, half_rows), f32), pltpu.VMEM((slots, step_rows, half_rows), bf16),
            pltpu.VMEM((slots, 3, step_rows, half_rows), f32),
            pltpu.SemaphoreType.DMA((slots, 4)), pltpu.SemaphoreType.DMA((slots, 3)),
        ],
        near=(0,), name="adam", vmem=40,
    )
    new_vectors = update(*state[18:], d_vectors * factor[0, 0], RATES[6], scales[0], scales[1])
    return (loss[0, 0], norm[0, 0]) + tuple(new[15:]) + tuple(new[:15]) + new_vectors


def solution(mesh):
    split_rows = P(ALL, None)
    flat = P(ALL)
    table = P("wide", "group")
    mats = (table,) * 3 + (split_rows,) * 15 + (flat,) * 3
    in_specs = (split_rows, split_rows, flat, flat, flat, split_rows, flat, P()) + mats
    wide = mesh.shape["wide"]
    thick = D % (2 * wide * ROWS) == 0 and wide * ROWS <= LANES
    return jax.shard_map(
        partial(body if thick else plain_body, wide), mesh=mesh, in_specs=in_specs, out_specs=(P(), P()) + mats, check_vma=False
    )
```

```python
from functools import partial

import jax
import jax.numpy as jnp
import numpy as np
from jax import lax
from jax.experimental import pallas as pl
from jax.experimental.pallas import tpu as pltpu
from jax.sharding import PartitionSpec as P

D = 768
HEADS = 12
HEAD_DIM = 64
FF = 3072
ROWS = 8
LANES = 128
SIDE = 64
STEP = 16
ALL = ("group", "wide")
clip_level = 0.02
f32 = jnp.float32
bf16 = jnp.bfloat16
RATES = (0.5, 0.5 * D**-0.5, 0.5 * (D // 16) ** -0.5, 0.5 * D**-0.5, 0.5 * FF**-0.5, 0.5 * D**-0.5, 0.2)


def dot(a, b, ca=1, cb=0):
    return lax.dot_general(a, b, (((ca,), (cb,)), ((), ())), preferred_element_type=f32)


def split(x):
    high = x.astype(bf16)
    return high, (x - high.astype(f32)).astype(bf16)


def dot_split(x, w, cb=0):
    high, rest = split(x)
    return dot(high, w, 1, cb) + dot(rest, w, 1, cb)


def iota(shape, dim):
    return lax.broadcasted_iota(jnp.int32, shape, dim)


def stack_rows(rows):
    index = iota((ROWS, rows[0].shape[1]), 0)
    total = jnp.zeros(index.shape, f32)
    for number, row in enumerate(rows):
        total = jnp.where(index == number, row, total)
    return total


def layer_norm(resid):
    centred = resid - jnp.mean(resid, -1, keepdims=True)
    inv_std = lax.rsqrt(jnp.mean(centred * centred, -1, keepdims=True) + 1e-05)
    return centred * inv_std, inv_std


def norm_back(grad_out, normed, inv_std, gain):
    scaled = grad_out * gain
    return inv_std * (
        scaled
        - jnp.mean(scaled, -1, keepdims=True)
        - normed * jnp.mean(scaled * normed, -1, keepdims=True)
    )


def flag(condition):
    return jnp.where(condition, 1.0, 0.0)


def sequence_of(a, rows):
    assert HEADS == 12
    return jnp.where((a >= 0) & (a < rows * HEADS), lax.shift_right_logical(a * 43, 9), 99)


def head_of(a, rows):
    return a - HEADS * sequence_of(a, rows)


def spread_table(rows):
    return flag(sequence_of(iota((SIDE, ROWS), 0), rows) == iota((SIDE, ROWS), 1)).astype(bf16)


def column_table(rows):
    return flag(head_of(iota((SIDE, D), 0), rows) == lax.shift_right_logical(iota((SIDE, D), 1), 6))


def heads_table(rows):
    return flag(head_of(iota((16, SIDE), 1), rows) == iota((16, SIDE), 0)).astype(bf16)


def place_table(rows, first):
    a = iota((LANES, SIDE), 1)
    return flag((iota((LANES, SIDE), 0) == first + a) & (a < rows * HEADS)).astype(bf16)


def expand_table(rows, first, r):
    return flag(iota((LANES, D), 0) == first + r * HEADS + lax.shift_right_logical(iota((LANES, D), 1), 6)).astype(bf16)


def prepare(ids, live, seq, pos, group_rows):
    count = ids.shape[1]
    first = jnp.where(ids < group_rows, 1.0, 0.0)
    high = lax.shift_right_logical(ids, 8)
    index = iota((ROWS, count), 0)
    values = jnp.zeros((ROWS, count), f32)
    pieces = (high.astype(f32), (ids - high * 256).astype(f32), seq.astype(f32), jnp.where(pos == 0, 1.0, 0.0), live)
    for number, row in enumerate(pieces):
        values = jnp.where(index == number, row, values)
    left, right = iota((count, count), 0), iota((count, count), 1)
    ahead = jnp.where(right < left, 1.0, 0.0).astype(bf16)
    same = jnp.where(right == left, 1.0, 0.0).astype(bf16)
    marks = jnp.broadcast_to(first, (ROWS, count)).astype(bf16)
    before = dot(ahead, marks, 1, 1)[:, :1]
    mine = dot(same, marks, 1, 1)[:, :1]
    total = jnp.sum(first, 1, keepdims=True)
    target = jnp.where(mine > 0.5, before, total + iota((count, 1), 0).astype(f32) - before)
    moves = jnp.where(target.astype(jnp.int32) == right, 1.0, 0.0).astype(bf16)
    return dot(values.astype(bf16), moves), total


def attend(xt, w, vec, moved, rows):
    g1, bq, bv, bo, be1 = vec[0:1], vec[3:4], vec[4:5], vec[5:6], vec[6:7]
    seq_id, slot0, live = moved[2:3], moved[3:4], moved[4:5]
    spread, columns = spread_table(rows), column_table(rows)
    index = iota((ROWS, xt.shape[1]), 0).astype(f32)
    pick0 = flag((index == seq_id) & (slot0 > 0.5)).astype(bf16)
    x00 = dot(pick0, xt, 1, 1)
    q = (dot(x00.astype(bf16), w(0)) + bq).astype(bf16)
    q_wide = (dot(spread, q) * columns).astype(bf16)
    qk = dot(q_wide, w(1), 1, 1) * HEAD_DIM ** (-0.5)
    mask = (sequence_of(iota((SIDE, 1), 0), rows).astype(f32) == seq_id) & (live > 0.5)
    scores = jnp.where(mask, dot_split(qk, xt), -1e30)
    raw = jnp.where(mask, jnp.exp(scores - jnp.max(scores, 1, keepdims=True)), 0.0)
    total = jnp.sum(raw, 1, keepdims=True)
    probs = raw / jnp.where(total > 0.0, total, 1.0)
    probs_low = probs.astype(bf16)
    y = dot(probs_low, xt, 1, 1)
    psum = jnp.sum(probs_low.astype(f32), 1, keepdims=True)
    mixed = dot_split(y, w(2)) + psum * bv
    o = dot(spread, (mixed * columns).astype(bf16), 0, 0).astype(bf16)
    normed, inv = layer_norm(x00 + dot(o, w(3)) + bo)
    return normed * g1 + be1, x00.astype(bf16), q, o, probs, psum, normed, inv, qk, y


def attend_back(dx1, normed, inv, probs, psum, xt, w, vec, rows):
    g1, bv = vec[0:1], vec[4:5]
    spread, columns = spread_table(rows), column_table(rows)
    d_res = norm_back(dx1, normed, inv, g1)
    d_a = d_res.astype(bf16)
    d_o = dot(d_a, w(3), 1, 1).astype(bf16)
    d_o_wide = dot(spread, d_o) * columns
    vd = dot(d_o_wide.astype(bf16), w(2), 1, 1)
    dp = dot_split(vd, xt) + jnp.sum(d_o_wide * bv, 1, keepdims=True)
    ds = (probs * (dp - jnp.sum(probs * dp, 1, keepdims=True))).astype(bf16)
    z = dot(ds, xt, 1, 1)
    zw = dot_split(z, w(1)) * (HEAD_DIM ** (-0.5)) * columns
    d_q = dot(spread, zw.astype(bf16), 0, 0).astype(bf16)
    extra = d_res + dot(d_q, w(0), 1, 1)
    sums = [
        jnp.sum(dx1 * normed, 0, keepdims=True),
        jnp.sum(dx1, 0, keepdims=True),
        jnp.sum(d_a.astype(f32), 0, keepdims=True),
        jnp.sum(d_q.astype(f32), 0, keepdims=True),
        jnp.sum(d_o_wide * psum, 0, keepdims=True),
    ]
    return d_a, d_o, d_q, sums, vd, z, extra, ds


def both_halves(value, rows):
    low = value.astype(bf16)
    return dot(place_table(rows, 0), low).T, dot(place_table(rows, SIDE), low).T


def table_block(halves, dest, block):
    first = 2 * block * dest
    return halves[0][first : first + block] + halves[1][first + block : first + 2 * block]


def weight_block(halves, dest, block, wide):
    return halves[0][block * dest : block * (dest + 1)] + halves[1][block * (wide + dest) : block * (wide + dest + 1)]


HEAD_LINES = 8


def pack_heads(value, rows):
    row, head = iota((HEAD_LINES, SIDE), 0), head_of(iota((HEAD_LINES, SIDE), 1), rows)
    most = dot(flag(row == head).astype(bf16), value)
    rest = [dot(flag((row - 4 * k + 8 == head) & (head >= 8) & (head < HEADS)).astype(bf16), value) for k in range(2)]
    cut = lambda t, k: t[:, k * LANES : (k + 1) * LANES]
    chunks = value.shape[1] // LANES
    tiles = [cut(most, k) for k in range(chunks)]
    for k in range(0, chunks, 2):
        tiles.append(cut(rest[0], k) + cut(rest[1], k + 1) if k + 1 < chunks else cut(rest[0], k))
    return jnp.concatenate(tiles, 0).astype(bf16)


def unpack_heads(lines, chunks):
    tile = lambda k: lines[k * HEAD_LINES : (k + 1) * HEAD_LINES].astype(f32)
    most = jnp.concatenate([tile(k) for k in range(chunks)], 1)
    rest = []
    for k in range(chunks):
        value = tile(chunks + k // 2)
        rest.append(pltpu.roll(value, 4, 0) if k % 2 else value)
    rest = jnp.concatenate(rest, 1)
    return jnp.concatenate([most, jnp.where(iota(rest.shape, 0) < HEADS - 8, rest, 0.0)], 0)


def head_lines(chunks):
    return HEAD_LINES * (chunks + (chunks + 1) // 2)


def to_tiles(value):
    return jnp.concatenate([value[:, k : k + LANES] for k in range(0, value.shape[1], LANES)], 0)


def from_tiles(got, first, lines=ROWS):
    pieces = [got[:, first + k * lines : first + (k + 1) * lines, :] for k in range(D // LANES)]
    return jnp.concatenate([p.reshape(-1, LANES) for p in pieces], 1)


def ffn(x1, w_up, w_down, bias):
    u = dot(x1.astype(bf16), w_up) + bias
    h = (0.5 * u * (1.0 + lax.erf(u * 0.5**0.5))).astype(bf16)
    return u, h, dot(h, w_down)


def middle(x1, f, u, w_up, w_down, w, vec, picks):
    g2, gc, b2, be2, bc, bec = vec[1:2], vec[2:3], vec[7:8], vec[8:9], vec[9:10], vec[10:11]
    count = x1.shape[0]
    valid, picks = picks[:, :1].astype(f32), picks[:, 1:]
    normed2, inv2 = layer_norm(x1 + (f + b2))
    pooled = (normed2 * g2 + be2).astype(bf16)
    normed_c, inv_c = layer_norm(dot(pooled, w(4)) + bc)
    e = (normed_c * gc + bec).astype(bf16)
    scores = dot(e, e, 1, 1) * D ** (-0.5)
    col = iota((count, count), 1)
    is_pos = jnp.where(col == picks[:, 0:1], 1.0, 0.0)
    negs = jnp.zeros_like(is_pos)
    for number in range(1, picks.shape[1]):
        negs = negs + jnp.where(col == picks[:, number : number + 1], 1.0, 0.0)
    taken = (is_pos + negs) > 0.0
    top = jnp.max(jnp.where(taken, scores, -1e30), 1, keepdims=True)
    raw = jnp.where(taken, jnp.exp(scores - top), 0.0)
    total = jnp.sum(raw * (is_pos + negs), 1, keepdims=True)
    total = jnp.where(total > 0.0, total, 1.0)
    share = raw / total
    valid_count = jnp.sum(valid, 0, keepdims=True)
    per_query = top + jnp.log(total) - jnp.sum(is_pos * scores, 1, keepdims=True)
    loss = jnp.sum(jnp.where(valid > 0.0, valid * per_query, 0.0), 0, keepdims=True) / valid_count
    weight = valid / valid_count
    d_pos = (weight * (share - 1.0)).astype(bf16).astype(f32)
    d_neg = (weight * share).astype(bf16).astype(f32)
    d_scores = d_pos * is_pos + d_neg * negs
    high, rest = split(d_scores)
    d_e = (dot(high, e) + dot(rest, e) + dot(high, e, 0, 0) + dot(rest, e, 0, 0)) * D ** (-0.5)
    d_c = norm_back(d_e, normed_c, inv_c, gc).astype(bf16)
    d_x2 = dot(d_c, w(4), 1, 1)
    d_res2 = norm_back(d_x2, normed2, inv2, g2)
    d_f = d_res2.astype(bf16)
    lines = u.shape[0]
    d_h = dot(d_f[:lines], w_down, 1, 1)
    slope = 0.5 * (1.0 + lax.erf(u * 0.5**0.5)) + u * jnp.exp(-0.5 * u * u) * (2.0 * np.pi) ** (-0.5)
    d_u = (d_h * slope).astype(bf16)
    d_x1 = dot(d_u, w_up, 1, 1)
    sums = [
        jnp.sum(d_x2 * normed2, 0, keepdims=True),
        jnp.sum(d_e * normed_c, 0, keepdims=True),
        jnp.sum(d_f.astype(f32), 0, keepdims=True),
        jnp.sum(d_x2, 0, keepdims=True),
        jnp.sum(d_c.astype(f32), 0, keepdims=True),
        jnp.sum(d_e, 0, keepdims=True),
    ]
    return loss, pooled, d_c, d_res2, d_f, d_u, d_x1, sums


def update(weight, first, second, gradient, rate, scale_one, scale_two):
    first_new = 0.9 * first + 0.1 * gradient
    second_new = 0.999 * second + 0.001 * gradient * gradient
    first_hat = first_new * scale_one
    second_hat = second_new * scale_two
    return weight - rate * (first_hat / (jnp.sqrt(second_hat) + 1e-08) + 0.01 * weight), first_new, second_new


def shape(dims, kind=f32):
    return jax.ShapeDtypeStruct(dims, kind)


MIB = 1 << 20


def full_block(dims):
    return pl.BlockSpec(dims, lambda i: (0,) * len(dims), pipeline_mode=pl.Buffered(1))


def pinned(x):
    return pltpu.with_memory_space_constraint(x, pltpu.HBM)


def call(kernel, outs, *args, scalars=(), far=(), far_outs=(), after=(), near=(), near_outs=(), scratch=(), vmem=24, name=None, flops=0):
    anywhere = pl.BlockSpec(memory_space=pl.ANY)
    in_specs = [pl.BlockSpec(memory_space=pltpu.SMEM)] * len(scalars) + [anywhere] * len(far)
    in_specs += [full_block(a.shape) for a in args] + [anywhere] * len(after)
    moved = sum(int(np.prod(a.shape)) * a.dtype.itemsize for a in list(args) + list(far) + list(outs) + list(far_outs))
    used = len(scalars) + len(far) + len(args)

    def run(*refs):
        kernel(*refs[:used], *refs[used + len(after) :])

    shapes = [o if k in near_outs else pltpu.HBM(o.shape, o.dtype) for k, o in enumerate(outs)]
    shapes += [pltpu.HBM(o.shape, o.dtype) for o in far_outs]
    args = [a if k in near else pinned(a) for k, a in enumerate(args)]
    return pl.pallas_call(
        run,
        grid=(1,),
        out_shape=shapes,
        in_specs=in_specs,
        out_specs=[full_block(o.shape) for o in outs] + [anywhere] * len(far_outs),
        scratch_shapes=list(scratch),
        compiler_params=pltpu.CompilerParams(vmem_limit_bytes=vmem * MIB),
        cost_estimate=pl.CostEstimate(flops=int(flops), bytes_accessed=moved, transcendentals=0),
        name=name,
    )(*scalars, *(pinned(a) for a in far), *args, *after)


def once(x, other):
    anywhere = pl.BlockSpec(memory_space=pl.ANY)
    return pl.pallas_call(
        lambda *refs: None,
        out_shape=pltpu.HBM(x.shape, x.dtype),
        in_specs=[anywhere, anywhere],
        out_specs=anywhere,
        input_output_aliases={0: 0},
        compiler_params=pltpu.CompilerParams(vmem_limit_bytes=MIB),
        name="once",
    )(pinned(x), other)


def square_weights(mats, first, buffers, signals, order):
    copies = {
        k: pltpu.make_async_copy(mats.at[:, pl.ds(k * D, D)], buffers.at[k - first], signals.at[k - first]) for k in order
    }
    for k in order:
        copies[k].start()
    ready = {}

    def get(k):
        if k not in ready:
            copies[k].wait()
            ready[k] = buffers[k - first]
        return ready[k]

    return get


def weight_scratch(count):
    return [pltpu.VMEM((count, D, D), bf16), pltpu.SemaphoreType.DMA((count,))]


def prepare_kernel(group_rows, rows, passages, queries, negatives, small, vectors, seq, pos, up, packet, moved):
    line_up = lambda ref: [ref[k : k + 1, :] for k in range(ref.shape[0])]
    ids = jnp.concatenate(line_up(passages) + line_up(queries), 1)
    count = ids.shape[1]
    chunks = count // LANES
    entries = small[...]
    live = jnp.zeros((1, count), f32)
    for number in range(rows):
        live = jnp.where((seq[...] == number) & (pos[...] < entries[:, number : number + 1]), 1.0, live)
    got, total = prepare(ids, live, seq[...], pos[...], group_rows)
    moved[...] = got
    code = got[2:3] + 8.0 * got[3:4]
    lane = iota((1, LANES), 1)
    at = 1 + 2 * queries.shape[0]
    after = LANES - at - negatives.shape[0] * negatives.shape[1]
    rest = [jnp.zeros((1, at), jnp.int32)] + line_up(negatives) + [jnp.zeros((1, after), jnp.int32)]
    note = pltpu.roll(entries.astype(f32), LANES - rows + 1, 1)
    note = jnp.where((lane < at) | (lane == LANES - 1), note, jnp.concatenate(rest, 1).astype(f32))
    high = lax.shift_right_logical(total.astype(jnp.int32), 8)
    note = jnp.where(lane == 0, total - 256.0 * high.astype(f32), jnp.where(lane == LANES - 1, high.astype(f32), note))
    lines = [line[:, k * LANES : (k + 1) * LANES] for line in (got[0:1], got[1:2], code) for k in range(chunks)]
    own = vectors.shape[1]
    given = jnp.concatenate([vectors[...], jnp.zeros((1, -own % LANES), f32)], 1)
    lines += [note] + [given[:, k : k + LANES] for k in range(0, given.shape[1], LANES)]
    wide, block = packet.shape[0], up.shape[0]
    hidden = up.shape[1] // (2 * wide)
    first = packet.shape[1] - 2 * block
    index = iota((first, LANES), 0)
    whole = jnp.zeros((first, LANES), f32)
    for number, line in enumerate(lines):
        whole = jnp.where(index == number, line, whole)
    gap = jnp.zeros((block, LANES - hidden), f32)
    for dest in range(wide):
        pieces = [jnp.concatenate([up[:, n * hidden : (n + 1) * hidden], gap], 1) for n in (dest, wide + dest)]
        packet[dest] = jnp.concatenate([whole] + pieces, 0).astype(bf16)


def cast_kernel(attn_in, attn_out, head, down, out, down_out):
    down_out[...] = down[...].astype(bf16)
    out[:, : 3 * D] = attn_in[...].astype(bf16)
    out[:, 3 * D : 4 * D] = attn_out[...].astype(bf16)
    out[:, 4 * D :] = head[...].astype(bf16)


def build_kernel(emb, table):
    feats, vocab = emb.shape
    half = table.shape[0]
    blocks, second = half // LANES, (vocab - half) // LANES
    gap = jnp.zeros((SIDE - feats, LANES), f32)

    def build(b, both):
        start = pl.multiple_of(b * LANES, LANES)
        low = emb[:, pl.ds(start, LANES)]
        high = jnp.zeros_like(low)
        if both:
            high = emb[:, pl.ds(pl.multiple_of(half + start, LANES), LANES)]
        table[pl.ds(start, LANES), :] = jnp.concatenate([low, gap, high, gap], 0).astype(bf16).T.astype(f32)

    unroll = 7

    def step(i, carry):
        for k in range(unroll):
            build(i * unroll + k, True)
        return carry

    lax.fori_loop(0, second // unroll, step, 0)
    for b in range(second // unroll * unroll, blocks):
        build(jnp.int32(b), b < second)


def side_of(packet, s, chunks, group, half_rows, half):
    ids = lanes_of(packet, s, 0, chunks) * 256.0 + lanes_of(packet, s, chunks, chunks)
    local = ids - (group * half_rows).astype(f32)
    inside = (local >= 0.0) & (local < float(half_rows))
    return jnp.where(inside, jnp.where(local >= float(half), 2.0, 1.0), 0.0)


def own_span(first, group, count):
    return jnp.where(group == 0, 0, first), jnp.where(group == 0, first, count)


def number_block(per, count):
    return pl.BlockSpec((1, 1, per * count), lambda i, *s: (i, 0, 0), memory_space=pltpu.SMEM)


def lookup_kernel(half_rows, per, unroll, where, firsts, numbers, packet, table, out, buf):
    feats, count = out.shape[1:]
    group = where[0]
    chunks = count // LANES
    half = table.shape[0]
    at = pl.program_id(0) * per
    for s in range(per):
        low, high = own_span(firsts[at + s], group, count)

        def step(i, carry):
            for k in range(unroll):
                t = i * unroll + k
                buf[pl.ds(s * count + t, 1), :] = table[pl.ds(numbers[0, 0, s * count + t], 1), :]
            return carry

        lax.fori_loop(low // unroll, (high + unroll - 1) // unroll, step, 0)
    for s in range(per):
        side = side_of(packet, s, chunks, group, half_rows, half)
        lines = [buf[s * count + c * LANES : s * count + (c + 1) * LANES, :].astype(bf16).T for c in range(chunks)]
        turned = jnp.concatenate(lines, 1).astype(f32)
        pick = jnp.where(side > 1.5, turned[SIDE : SIDE + feats], turned[:feats])
        value = jnp.where(side > 0.5, pick, 0.0)
        out[s] = value.astype(bf16)


def lanes_of(packet, s, first, chunks):
    return jnp.concatenate([packet[s, first + c : first + c + 1, :].astype(f32) for c in range(chunks)], 1)


def lookup(where, numbers, firsts, packets, table, half_rows, feats, count, per=4, unroll=64):
    sources = packets.shape[0]
    some = lambda dims: pl.BlockSpec((per,) + dims, lambda i, *s: (i, 0, 0))
    return pl.pallas_call(
        partial(lookup_kernel, half_rows, per, unroll),
        out_shape=shape((sources, feats, count), bf16),
        grid_spec=pltpu.PrefetchScalarGridSpec(
            num_scalar_prefetch=2,
            grid=(sources // per,),
            in_specs=[number_block(per, count), some(packets.shape[1:]), pl.BlockSpec(table.shape, lambda i, *s: (0, 0), pipeline_mode=pl.Buffered(1))],
            out_specs=some((feats, count)),
            scratch_shapes=[pltpu.VMEM((per * count, LANES), f32)],
        ),
        compiler_params=pltpu.CompilerParams(vmem_limit_bytes=16 * MIB),
        cost_estimate=pl.CostEstimate(flops=10**9, bytes_accessed=10**7, transcendentals=0),
        name="lookup",
    )(where, firsts, numbers.reshape(-1, 1, per * count), packets, pinned(table))


def spread_kernel(rows, half_rows, feats, per, unroll, copies, at_early, where, firsts, numbers, packet, early_own, early_other, late_own, late_other, p_heads, out, square, *scratch):
    parts, buf = scratch[:copies], scratch[copies]
    group = where[0]
    chunks = buf.shape[0] // (per * LANES)
    count = chunks * LANES
    half = parts[0].shape[0]
    vocab = out.shape[1]
    blocks = half // LANES
    step_at = pl.program_id(0)

    @pl.when(step_at == 0)
    def _():
        at_once = 3

        def clear(i, carry):
            for part in parts:
                for k in range(at_once):
                    part[pl.ds(pl.multiple_of((i * at_once + k) * LANES, LANES), LANES), :] = jnp.zeros((LANES, LANES), f32)
            return carry

        lax.fori_loop(0, blocks // at_once, clear, 0)
        for k in range(blocks // at_once * at_once, blocks):
            for part in parts:
                part[k * LANES : (k + 1) * LANES, :] = jnp.zeros((LANES, LANES), f32)

    gap = jnp.zeros((SIDE - feats, count), f32)
    block = feats // 2
    lane, slot = iota((LANES, 2 * LANES), 0), iota((LANES, 2 * LANES), 1)
    half_of = lax.shift_right_logical(slot, 7)
    slot = slot - half_of * LANES
    seq_of, head = lax.shift_right_logical(slot, 4), slot - lax.shift_right_logical(slot, 4) * STEP
    relane = flag((lane == half_of * SIDE + seq_of * HEADS + head) & (head < HEADS) & (seq_of < rows)).astype(bf16)
    empty = jnp.zeros((LANES - rows * STEP, count), f32)
    is_own = step_at < pl.num_programs(0) // 2

    def pick(own, other, s, first, lines):
        return jnp.where(is_own, own[s, first : first + lines, :], other[s, first : first + lines, :])

    for s in range(per):
        code = lanes_of(packet, s, 2 * chunks, chunks)
        slot0 = code >= 8.0
        seq = jnp.where(slot0, code - 8.0, code)
        scores = unpack_heads(pick(late_own, late_other, s, block + ROWS, head_lines(chunks)), chunks)
        values = unpack_heads(p_heads[s, : head_lines(chunks), :], chunks)
        parts_of = [jnp.where(seq == float(r), scores, 0.0) for r in range(rows)] + [empty]
        parts_of += [jnp.where(seq == float(r), values, 0.0) for r in range(rows)] + [empty]
        both = jnp.concatenate([pick(early_own, early_other, s, at_early, block), pick(late_own, late_other, s, 0, block)], 0)
        wide_rows = dot(both, relane).astype(bf16)
        basis = [jnp.concatenate([wide_rows[k : k + block, :LANES], wide_rows[k : k + block, LANES:]], 0) for k in (0, block)]
        x = dot(jnp.concatenate(basis, 1), jnp.concatenate(parts_of, 0).astype(bf16))
        first = flag((iota((ROWS, count), 0).astype(f32) == seq) & slot0).astype(bf16)
        x = x + dot(pick(late_own, late_other, s, block, ROWS), first, 0, 0)[:feats]
        side = side_of(packet, s, chunks, group, half_rows, half)
        tall = jnp.concatenate([jnp.where(side == 1.0, x, 0.0), gap, jnp.where(side == 2.0, x, 0.0), gap], 0).astype(bf16)
        for c in range(chunks):
            start = s * count + c * LANES
            buf[start : start + LANES, :] = tall[:, c * LANES : (c + 1) * LANES].T.astype(f32)
    for s in range(per):
        low, high = own_span(firsts[step_at * per + s], group, count)

        def step(i, carry):
            for k in range(unroll):
                t = i * unroll + k
                part = parts[k % copies]
                row = numbers[0, 0, s * count + t]
                part[pl.ds(row, 1), :] = part[pl.ds(row, 1), :] + buf[pl.ds(s * count + t, 1), :]
            return carry

        lax.fori_loop(low // unroll, (high + unroll - 1) // unroll, step, 0)

    @pl.when(step_at == pl.num_programs(0) - 1)
    def _():
        def emit(b, total, both):
            start = pl.multiple_of(b * LANES, LANES)
            lines = parts[0][pl.ds(start, LANES), :]
            for part in parts[1:]:
                lines = lines + part[pl.ds(start, LANES), :]
            turned = lines.T
            out[:, pl.ds(start, LANES)] = turned[:feats].astype(bf16)
            if both:
                out[:, pl.ds(pl.multiple_of(half + start, LANES), LANES)] = turned[SIDE : SIDE + feats].astype(bf16)
            return total + lines * lines

        second = (vocab - half) // LANES
        group_of = 14

        def several(i, total):
            for k in range(group_of):
                total = emit(i * group_of + k, total, True)
            return total

        total = lax.fori_loop(0, second // group_of, several, jnp.zeros((LANES, LANES), f32))
        for b in range(second // group_of * group_of, blocks):
            total = emit(jnp.int32(b), total, b < second)
        square[...] = jnp.sum(total.reshape(LANES // ROWS, ROWS, LANES), 0)


def spread_tokens(where, numbers, firsts, packets, early, late, p_heads, at_early, rows, half_rows, feats, count, per=8, unroll=40, copies=5):
    devices = packets.shape[0]
    block = packets.shape[1:]
    half = -(-half_rows // (2 * LANES)) * LANES
    some = lambda dims: pl.BlockSpec((per,) + dims, lambda i, *s: (i, 0, 0))
    steps = devices // per
    ordered = pl.BlockSpec((per, head_lines(count // LANES), LANES), lambda i, where, *s: ((i + where[0] * (steps // 2)) % steps, 0, 0))
    mine = lambda pair: pl.BlockSpec((per,) + pair[0].shape[1:], lambda i, *s: (jnp.minimum(i, steps // 2 - 1), 0, 0))
    theirs = lambda pair: pl.BlockSpec((per,) + pair[0].shape[1:], lambda i, *s: (jnp.maximum(i - steps // 2, 0), 0, 0))
    return pl.pallas_call(
        partial(spread_kernel, rows, half_rows, feats, per, unroll, copies, at_early),
        out_shape=[pltpu.HBM((feats, half_rows), bf16), pltpu.HBM((ROWS, LANES), f32)],
        grid_spec=pltpu.PrefetchScalarGridSpec(
            num_scalar_prefetch=2,
            grid=(steps,),
            in_specs=[number_block(per, count), some(block), mine(early), theirs(early), mine(late), theirs(late), ordered],
            out_specs=[pl.BlockSpec((feats, half_rows), lambda i, *s: (0, 0), pipeline_mode=pl.Buffered(1)), pl.BlockSpec((ROWS, LANES), lambda i, *s: (0, 0))],
            scratch_shapes=[pltpu.VMEM((half, LANES), f32)] * copies + [pltpu.VMEM((per * count, LANES), f32)],
        ),
        compiler_params=pltpu.CompilerParams(vmem_limit_bytes=52 * MIB),
        cost_estimate=pl.CostEstimate(flops=10**9, bytes_accessed=3 * 10**7, transcendentals=0),
        name="spread_tokens",
    )(where, firsts, numbers.reshape(-1, 1, per * count), packets, *early, *late, p_heads)


def attend_kernel(rows, mats, xt, vec, moved, sent, qk_out, facts, y_out, probs_out, psum_out, normed_out, inv_out, *scratch):
    w = square_weights(mats, 0, *scratch, (0, 1, 2, 3))
    x1, x00, q, o, probs, psum, normed, inv, qk, y = attend(xt[...], w, vec[...], moved[...], rows)
    tiles = to_tiles(x1)
    for dest in range(sent.shape[0]):
        sent[dest] = tiles.astype(bf16)
    qk_out[...] = qk.astype(bf16)
    facts[...] = jnp.concatenate([to_tiles(value.astype(f32)) for value in (x00, q, o)], 0).astype(bf16)
    y_out[...] = y.astype(bf16)
    probs_out[...], psum_out[...], normed_out[...], inv_out[...] = probs, psum, normed, inv


def pack_early_kernel(rows, qk, probs, facts, early, known):
    halves = both_halves(qk[...], rows)
    wide = early.shape[0]
    for dest in range(wide):
        early[dest] = table_block(halves, dest, D // (2 * wide)).astype(bf16)
    known[...] = jnp.concatenate([pack_heads(probs[...].astype(bf16), rows), facts[...]], 0)


def attend_back_kernel(rows, place, mats, got, d_res2, sums_up, normed, inv, probs, psum, xt, vec, late_out, last, z_out, *scratch):
    w = square_weights(mats, 0, *scratch, (3, 2, 1, 0))
    wide = late_out.shape[0]
    block = D // (2 * wide)
    feats = 2 * block
    dx1 = d_res2[pl.ds(pl.multiple_of(place[0] * ROWS, ROWS), ROWS), :]
    lines = ROWS * (D // LANES)
    tiles = got[0, :lines, :].astype(f32)
    for k in range(1, wide):
        tiles = tiles + got[k, :lines, :].astype(f32)
    dx1 = dx1 + jnp.concatenate([tiles[k : k + ROWS] for k in range(0, lines, ROWS)], 1)
    d_a, d_o, d_q, sums, vd, z, extra, ds = attend_back(
        dx1, normed[...], inv[...], probs[...], psum[...], xt[...], w, vec[...], rows
    )
    halves = both_halves(vd, rows)
    heads = pack_heads(ds, rows)
    gap = jnp.zeros((ROWS, LANES - feats), f32)
    for dest in range(wide):
        row_part = jnp.concatenate([extra[:, feats * dest : feats * (dest + 1)], gap], 1)
        late_out[dest] = jnp.concatenate([jnp.concatenate([table_block(halves, dest, block), row_part], 0).astype(bf16), heads], 0)
    z_out[...] = z.astype(bf16)
    sums = sums + [sums_up[...]]
    index = iota((ROWS, D), 0)
    spare = ROWS - rows
    values = [d_q.astype(f32), d_o.astype(f32), d_a.astype(f32)]
    for number, row in enumerate(sums):
        values[number // spare] = jnp.where(index == rows + number % spare, row, values[number // spare])
    last[...] = jnp.concatenate([to_tiles(value) for value in values], 0).astype(bf16)


def pack_kernel(rows, last, y, z, d_up, d_up_other, out):
    wide = out.shape[0]
    block = d_up.shape[0] // wide
    hidden = d_up.shape[1] // 2
    values = last[...]
    halves_y, halves_z = both_halves(y[...], rows), both_halves(z[...], rows)
    up = d_up[...] + d_up_other[...].astype(f32)
    gap = jnp.zeros((block, LANES - hidden), f32)
    for dest in range(wide):
        mine = up[block * dest : block * (dest + 1), :]
        pieces = [jnp.concatenate([mine[:, k * hidden : (k + 1) * hidden], gap], 1) for k in range(2)]
        pieces += [weight_block(halves_y, dest, block, wide), weight_block(halves_z, dest, block, wide)]
        out[dest] = jnp.concatenate([values, jnp.concatenate(pieces, 0).astype(bf16)], 0)


def rows_of(own, other):
    return jnp.concatenate([from_tiles(own[...], 0), from_tiles(other[...], 0)], 0)


def by_core(where, own, other):
    first = where[0] == 0
    return jnp.concatenate([jnp.where(first, own[...], other[...]), jnp.where(first, other[...], own[...])], 0)


def ffn_kernel(where, x_own, w_up, down_own, down_other, bias, u_out, h_out, out):
    u, h, f = ffn(from_tiles(x_own[...], 0), w_up[...], by_core(where, down_own, down_other), bias[...])
    u_out[...], h_out[...] = u, h
    out[...] = f.astype(bf16)


def total_kernel(got, out):
    total = got[0].astype(f32)
    for k in range(1, got.shape[0]):
        total = total + got[k].astype(f32)
    lines = to_tiles(total).astype(bf16)
    for k in range(out.shape[0]):
        out[k] = lines


def middle_kernel(where, mats, x_own, x_other, f_own, f_other, u, w_up, down_own, down_other, vec, picks, early, loss, pooled, d_c, d_res2, d_f, d_u, out, sums, sums_up, *scratch):
    w = square_weights(mats, 4, *scratch, (4,))
    x1 = rows_of(x_own, x_other).astype(f32)
    f = rows_of(f_own, f_other).astype(f32)
    got = middle(x1, f, u[...], w_up[...], by_core(where, down_own, down_other), w, vec[...], picks[...])
    lines = u.shape[0]
    loss[...], pooled[...], d_c[...], d_res2[...] = got[:4]
    d_f[...], d_u[...] = got[4][:lines], got[5]
    for dest in range(out.shape[0]):
        part = to_tiles(got[6][dest * ROWS : (dest + 1) * ROWS]).astype(bf16)
        out[dest] = jnp.concatenate([part, early[dest]], 0)
    sums[...] = stack_rows(got[7])
    su = jnp.sum(got[5].astype(f32), 0, keepdims=True)
    sums_up[...] = jnp.concatenate([su, jnp.zeros((1, D - su.shape[1]), f32)], 1)


def own_cols(device, block):
    index = iota((D, LANES), 1)
    return flag((iota((D, LANES), 0) == device * block + index) & (index < block)).astype(bf16)


def own_rows(left, right, mine, block):
    return dot(dot(left, mine).astype(bf16), right, 0, 0)[:block]


def ffn_grads_kernel(where, x_own, h, d_f, d_u, pooled, d_c, down_mine, down_theirs, d_head, up_mine, up_theirs):
    first = where[0] == 0
    hidden = down_mine.shape[0]
    half = up_mine.shape[0]
    d_up = dot(from_tiles(x_own[...], 0), d_u[...], 0, 0)
    up_mine[...] = jnp.where(first, d_up[:half], d_up[half:])
    up_theirs[...] = jnp.where(first, d_up[half:], d_up[:half]).astype(bf16)
    d_down = dot(h[...], d_f[...], 0, 0)
    down_mine[...] = jnp.where(first, d_down[:hidden], d_down[hidden:])
    down_theirs[...] = jnp.where(first, d_down[hidden:], d_down[:hidden]).astype(bf16)
    block = d_head.shape[0]
    d_head[...] = own_rows(pooled[...], d_c[...], own_cols(where[1], block), block)


def grads_kernel(rows, where, known, facts_own, facts_other, d_wh, down_mine, down_other, sums, square, in_out, out_out, up_out, down_out, vec_out, square_out, x00, q_all, o_all, d_q, d_o, d_a, y, z, wide_z):
    group, device = where[0], where[1]
    wide = facts_own.shape[0]
    devices = 2 * wide
    block = in_out.shape[0]
    hidden = FF // devices
    first = group == 0
    lines = ROWS * (D // LANES)
    at_up = 3 * lines
    for base, facts in ((0, facts_own), (1, facts_other)):
        at = slice(base * wide * ROWS, (base + 1) * wide * ROWS)
        kept = known[pl.ds(((base + group) % 2) * wide, wide), known.shape[1] - 3 * lines :, :]
        for k, out in enumerate((x00, q_all, o_all)):
            out[at, :] = from_tiles(kept, k * lines).astype(f32)
        for k, out in enumerate((d_q, d_o, d_a)):
            out[at, :] = from_tiles(facts, k * lines).astype(f32)
        for n in range(wide):
            at = slice((base * wide + n) * block, (base * wide + n + 1) * block)
            y[at, :] = facts[n, at_up + 2 * block : at_up + 3 * block, :].astype(f32)
            z[at, :] = facts[n, at_up + 3 * block : at_up + 4 * block, :].astype(f32)
    for n in range(wide):
        for k in range(2):
            piece = facts_own[n, at_up + k * block : at_up + (k + 1) * block, :].astype(f32)
            at = (k * wide + n) * hidden
            up_out[:, at : at + hidden] = piece[:, :hidden]
    down_out[...] = down_mine[...] + down_other[...].astype(f32)

    def by_heads(source, values):
        total = jnp.zeros((block, D), f32)
        low = source[...].astype(bf16)
        for r in range(rows):
            wide_z[...] = dot(low, expand_table(rows, jnp.where(group == 0, 0, SIDE), r))
            for n in range(devices):
                total = total + wide_z[n * block : (n + 1) * block, :] * values[n * ROWS + r : n * ROWS + r + 1, :]
        return total

    d_wk = by_heads(z, q_all) * HEAD_DIM ** (-0.5)
    d_wv = by_heads(y, d_o)
    mine = own_cols(device, block)
    d_wq = own_rows(x00[...].astype(bf16), d_q[...].astype(bf16), mine, block)
    d_wo = own_rows(o_all[...].astype(bf16), d_a[...].astype(bf16), mine, block)
    square_now = square[...]

    def fold(square_now, value):
        tiles = value * value
        total = jnp.sum(tiles.reshape(tiles.shape[0] // ROWS, ROWS, tiles.shape[1]), 0)
        for k in range(total.shape[1] // LANES):
            square_now = square_now + total[:, k * LANES : (k + 1) * LANES]
        return square_now

    in_out[:, :D], in_out[:, D : 2 * D], in_out[:, 2 * D :] = d_wq, d_wk, d_wv
    out_out[...] = d_wo
    for value in (d_wq, d_wk, d_wv, d_wo, d_wh[...], up_out[...], down_out[...]):
        square_now = fold(square_now, value)
    spare = ROWS - rows
    grouped = [jnp.sum(t[...].reshape(devices, ROWS, D), 0) for t in (d_q, d_o)]
    tail = [grouped[k // spare][rows + k % spare : rows + k % spare + 1] for k in range(5)]
    mids = sums[...]
    pieces = [tail[0], mids[0:1], mids[1:2], tail[3], tail[4], tail[2], tail[1]] + [mids[k : k + 1] for k in range(2, 6)]
    index = iota((16, D), 0)
    total = jnp.zeros((16, D), f32)
    for number, row in enumerate(pieces):
        total = jnp.where(index == number, row, total)
    each = D // hidden
    for k in range(wide):
        lines_of = [(base * wide + k) * ROWS + rows + 5 % spare for base in range(2)]
        source = (d_q, d_o)[5 // spare]
        row = source[lines_of[0] : lines_of[0] + 1, :] + source[lines_of[1] : lines_of[1] + 1, :]
        for core in range(2):
            shift = (hidden * (k % each) - hidden * core) % D
            turned = pltpu.roll(row, shift, 1) if shift else row
            col = iota((1, D), 1)
            turned = jnp.where((col >= hidden * (k % each)) & (col < hidden * (k % each + 1)), turned, 0.0)
            total = total + jnp.where(index == 11 + (core * wide + k) // each, turned, 0.0)
    vec_out[...] = total
    square_now = square_now + fold(jnp.zeros((ROWS, LANES), f32), total) / devices
    for k in range(devices):
        square_out[k] = square_now


def adam_kernel(count, scales, weight, first, second, d_table, got, *refs):
    grads, state = refs[:count], refs[count : 4 * count]
    norm_out, factor_out = refs[4 * count : 4 * count + 2]
    outs = refs[4 * count + 2 : 7 * count + 2]
    far = refs[7 * count + 2 : 7 * count + 5]
    loads, grad_loads, stores, got_in, sent = refs[7 * count + 5 :]
    slots, lines = loads.shape[0], loads.shape[2]
    jobs = weight.shape[0] // lines
    sources = (weight, first, second, d_table)

    def load(j):
        places = [loads.at[j % slots, k] for k in range(3)] + [grad_loads.at[j % slots]]
        return [
            pltpu.make_async_copy(ref.at[pl.ds(j * lines, lines), :], place, got_in.at[j % slots, k])
            for k, (ref, place) in enumerate(zip(sources, places))
        ]

    def store(j):
        return [pltpu.make_async_copy(stores.at[j % slots, k], ref.at[pl.ds(j * lines, lines), :], sent.at[j % slots, k]) for k, ref in enumerate(far)]

    for j in range(min(slots, jobs)):
        for copy in load(j):
            copy.start()
    total = got[0]
    for k in range(1, got.shape[0]):
        total = total + got[k]
    total = jnp.sum(jnp.sum(total, 0, keepdims=True), 1, keepdims=True)
    norm = jnp.sqrt(total)
    factor = jnp.minimum(1.0, clip_level / (norm + 1e-06))
    norm_out[...], factor_out[...] = norm, factor
    one, two = scales[0], scales[1]
    for j in range(jobs):
        for copy in load(j):
            copy.wait()
        if j >= slots:
            for copy in store(j - slots):
                copy.wait()
        old = [loads[j % slots, k] for k in range(3)]
        new = update(*old, grad_loads[j % slots].astype(f32) * factor, RATES[0], one, two)
        for k in range(3):
            stores[j % slots, k] = new[k]
        for copy in store(j):
            copy.start()
        if j + slots < jobs:
            for copy in load(j + slots):
                copy.start()
    for number in range(count):
        old = [state[3 * number + k][...] for k in range(3)]
        new = update(*old, grads[number][...] * factor, RATES[number + 1], one, two)
        for k in range(3):
            outs[3 * number + k][...] = new[k]
    for j in range(max(0, jobs - slots), jobs):
        for copy in store(j):
            copy.wait()


def swap(x):
    return lax.ppermute(x, "group", [(0, 1), (1, 0)])


def exchange(x):
    return lax.all_to_all(x, "wide", split_axis=0, concat_axis=0, tiled=True)


def tie(*values):
    return lax.optimization_barrier(values)


def pair(x):
    own = exchange(x)
    return own, swap(own)


def in_order(own, other, group):
    return jnp.where(group == 0, jnp.concatenate([own, other], 0), jnp.concatenate([other, own], 0))


def plain_body(wide, passage_ids, query_ids, passage_len, query_len, positive, negatives, valid, step_count, *state):
    params, firsts, seconds = state[0::3], state[1::3], state[2::3]
    embedding, attn_in, attn_out, w_ffn_up, w_ffn_down, head, vectors = params
    group, place = lax.axis_index("group"), lax.axis_index("wide")
    device, devices = group * wide + place, 2 * wide
    feats, half_rows = embedding.shape
    block, hidden = D // devices, FF // devices
    pas_count, pas_len = passage_ids.shape
    qry_count, qry_len = query_ids.shape
    rows = pas_count + qry_count
    tokens = pas_count * pas_len + qry_count * qry_len
    live = rows * HEADS
    both = lambda x: jnp.concatenate(pair(x), 0)
    gather = lambda x: both(jnp.broadcast_to(x[None], (wide,) + x.shape))
    ids = jnp.concatenate([passage_ids.reshape(-1), query_ids.reshape(-1)])
    seq_np = np.concatenate([np.repeat(np.arange(pas_count), pas_len), pas_count + np.repeat(np.arange(qry_count), qry_len)])
    pos_np = np.concatenate([np.tile(np.arange(pas_len), pas_count), np.tile(np.arange(qry_len), qry_count)])
    lens = jnp.concatenate([jnp.repeat(passage_len, pas_len), jnp.repeat(query_len, qry_len)])
    moved = jnp.zeros((ROWS, tokens), f32).at[2].set(jnp.asarray(seq_np, f32)).at[3].set(jnp.asarray(pos_np == 0, f32))
    moved = moved.at[4].set(flag(jnp.asarray(pos_np) < lens))
    note = jnp.concatenate([ids, valid, positive, negatives.reshape(-1)])
    notes = gather(jnp.pad(note, (0, -note.shape[0] % LANES)).reshape(-1, LANES)).reshape(devices, -1)
    low_vectors = gather(jnp.pad(vectors.astype(bf16), (0, -vectors.shape[0] % LANES)).reshape(-1, LANES))
    vec = in_order(low_vectors[:wide], low_vectors[wide:], group).reshape(devices, -1)[:, : vectors.shape[0]].astype(f32).reshape(-1, D)
    all_ids = notes[:, :tokens]
    valid_rows = jnp.pad(notes[:, tokens : tokens + qry_count].astype(f32), ((0, 0), (pas_count, ROWS - rows))).reshape(-1, 1)
    at = tokens + qry_count
    picked = jnp.concatenate(
        [notes[:, at : at + qry_count, None], notes[:, at + qry_count : at + qry_count + negatives.size].reshape(devices, qry_count, -1)], 2
    )
    pick_dev = picked // pas_count
    pick_row = (((pick_dev // wide) ^ group) * wide + pick_dev % wide) * ROWS + picked % pas_count
    pick_rows = jnp.pad(pick_row, ((0, 0), (pas_count, ROWS - rows), (0, 0)), constant_values=-1).reshape(devices * ROWS, -1)
    mats = lax.all_gather(jnp.concatenate([attn_in, attn_out, head], 1).astype(bf16), ALL, axis=0, tiled=True)
    w = lambda k: mats[:, k * D : (k + 1) * D]
    w_up = lax.all_to_all(
        w_ffn_up.astype(bf16).reshape(block, devices, hidden).transpose(1, 0, 2), ALL, split_axis=0, concat_axis=0, tiled=True
    ).reshape(D, hidden)
    w_down = w_ffn_down.astype(bf16)
    bias_up = lax.dynamic_slice(vec.reshape(-1), (11 * D + device * hidden,), (hidden,))[None]
    local = all_ids - group * half_rows
    inside = ((local >= 0) & (local < half_rows)).reshape(1, -1)
    local = jnp.clip(local, 0, half_rows - 1).reshape(-1)
    looked = jnp.where(inside, jnp.take(embedding.astype(bf16), local, axis=1), jnp.zeros((), bf16))
    looked = looked.reshape(feats, devices, tokens).transpose(1, 0, 2)
    xt = exchange(looked[:wide] + swap(looked[wide:])).reshape(D, tokens)
    x1, x00, q, o, probs, psum, normed1, inv1, qk, y = attend(xt, w, vec, moved, rows)
    p_heads = dot(heads_table(rows), probs.astype(bf16)).astype(bf16)
    x1_all = gather(x1.astype(bf16)).reshape(devices * ROWS, D)

    def to_owner(parts):
        mine = parts[: wide * ROWS] + swap(parts[wide * ROWS :])
        return jnp.sum(exchange(mine.astype(bf16).reshape(wide, ROWS, D)).astype(f32), 0)

    u, h, f_part = ffn(x1_all, w_up, w_down, bias_up)
    f_all = gather(to_owner(f_part).astype(bf16)).reshape(devices * ROWS, D).astype(f32)
    loss, pooled, d_c, d_res2, d_f, d_u, d_x1, sums = middle(x1_all.astype(f32), f_all, u, w_up, w_down, w, vec, jnp.concatenate([valid_rows.astype(jnp.int32), pick_rows], 1))
    d_x1 = lax.dynamic_slice(d_res2, (place * ROWS, 0), (ROWS, D)) + to_owner(d_x1)
    d_a, d_o, d_q, sums_back, vd, z, extra, ds = attend_back(d_x1, normed1, inv1, probs, psum, xt, w, vec, rows)

    to_features = lambda t: both(t.T.astype(bf16).reshape(wide, feats, -1))

    def to_blocks(t):
        parts = t.T.astype(bf16).reshape(2, wide, block, -1).transpose(1, 0, 2, 3).reshape(wide, 2 * block, -1)
        got = both(parts).reshape(devices, 2, block, -1)
        return lax.dynamic_index_in_dim(got, group, 1, keepdims=False)[:, :, :live].reshape(devices, block, rows, HEADS)

    facts = gather(jnp.concatenate([x00, q, o, d_q, d_o, d_a], 0)).reshape(devices, 6, ROWS, D)
    flat_fact = lambda k: facts[:, k].reshape(devices * ROWS, D)
    by_head = lambda k: facts[:, k].reshape(devices, ROWS, HEADS, HEAD_DIM)[:, :rows]
    cut = lambda m: lax.dynamic_slice(m, (0, device * block), (devices * ROWS, block))
    d_wq = dot(cut(flat_fact(0)), flat_fact(3), 0, 0)
    d_wk = jnp.einsum("nfrh,nrhd->fhd", to_blocks(z), by_head(1), preferred_element_type=f32).reshape(block, D) * HEAD_DIM ** (-0.5)
    d_wv = jnp.einsum("nfrh,nrhd->fhd", to_blocks(y), by_head(4), preferred_element_type=f32).reshape(block, D)
    d_wo = dot(cut(flat_fact(2)), flat_fact(5), 0, 0)
    d_wup = dot(x1_all, d_u, 0, 0).astype(bf16).reshape(devices, block, hidden)
    d_wup = lax.all_to_all(d_wup, ALL, split_axis=0, concat_axis=0, tiled=True).astype(f32).transpose(1, 0, 2).reshape(block, FF)
    sums_up = jnp.pad(jnp.sum(d_u.astype(f32), 0, keepdims=True), ((0, 0), (0, D - hidden)))
    tails = gather(stack_rows(sums_back + [sums_up]))
    tail = jnp.sum(tails, 0)
    ups = in_order(tails[:wide], tails[wide:], group)[:, 5, :hidden].reshape(-1)
    mids = [row[0] for row in sums]
    d_vec = jnp.concatenate([tail[0], mids[0], mids[1], tail[3], tail[4], tail[2], tail[1]] + mids[2:] + [ups])
    d_vec = lax.dynamic_slice(d_vec, (device * vectors.shape[0],), vectors.shape)
    basis = jnp.concatenate([to_features(qk), to_features(vd), to_features(extra)], 2)
    lanes = gather(jnp.concatenate([dot(heads_table(rows), ds).astype(bf16), p_heads], 0))
    seq = jnp.asarray(seq_np, jnp.int32)[None]
    here = sequence_of(iota((SIDE, 1), 0), rows) == seq
    widen = lambda t: jnp.where(here[None], jnp.einsum("ha,nht->nat", heads_table(rows), t, preferred_element_type=f32), 0.0).astype(bf16)
    first = ((iota((ROWS, 1), 0) == seq) & jnp.asarray(pos_np == 0)[None]).astype(bf16)
    coef = jnp.concatenate([widen(lanes[:, :16]), widen(lanes[:, 16:]), jnp.broadcast_to(first[None], (devices,) + first.shape)], 1)
    d_tok = jnp.einsum("nfa,nat->fnt", basis, coef, preferred_element_type=f32).reshape(feats, -1)
    d_table = jnp.zeros((feats, half_rows), f32).at[:, local].add(jnp.where(inside, d_tok, 0.0))
    d_head = dot(cut(pooled), d_c, 0, 0)
    grads = (d_table, jnp.concatenate([d_wq, d_wk, d_wv], 1), d_wo, d_wup, dot(h, d_f, 0, 0), d_head, d_vec)
    squares = sum(jnp.sum(g * g) for g in grads)
    grad_norm = jnp.sqrt(jnp.sum(gather(jnp.full((ROWS, LANES), squares))[:, 0, 0]))
    factor = jnp.minimum(1.0, clip_level / (grad_norm + 1e-06))
    step_float = step_count[0].astype(f32)
    one, two = 1.0 / (1.0 - jnp.power(0.9, step_float)), 1.0 / (1.0 - jnp.power(0.999, step_float))
    new = [update(params[k], firsts[k], seconds[k], grads[k] * factor, RATES[k], one, two) for k in range(7)]
    return (loss[0, 0], grad_norm) + tuple(t for group_of in new for t in group_of)


def body(wide, passage_ids, query_ids, passage_len, query_len, positive, negatives, valid, step_count, *state):
    embedding, attn_in, attn_out, w_ffn_up, w_ffn_down, head, vectors = state[0::3]
    group = lax.axis_index("group")
    place = lax.axis_index("wide")
    device = group * wide + place
    devices = 2 * wide
    feats, half_rows = embedding.shape
    block = D // devices
    hidden = FF // devices
    pas_count, pas_len = passage_ids.shape
    qry_count, qry_len = query_ids.shape
    rows = pas_count + qry_count
    tokens = pas_count * pas_len + qry_count * qry_len
    chunks = tokens // LANES
    half = -(-half_rows // (2 * LANES)) * LANES
    where = jnp.stack([group, device]).astype(jnp.int32)
    place_at = place.astype(jnp.int32)[None]
    lines = wide * ROWS

    seq_np = np.concatenate([np.repeat(np.arange(pas_count), pas_len), pas_count + np.repeat(np.arange(qry_count), qry_len)])
    pos_np = np.concatenate([np.tile(np.arange(pas_len), pas_count), np.tile(np.arange(qry_len), qry_count)])
    vec_lines = -(-vectors.shape[0] // LANES)
    packet_lines = -(-(3 * chunks + 1 + vec_lines) // ROWS) * ROWS + 2 * block
    at_note = 3 * chunks
    pieces = [passage_len, query_len, valid, positive]
    size = sum(t.shape[0] for t in pieces)
    assert size + negatives.size < LANES - 1
    small = jnp.concatenate(pieces + [jnp.zeros((LANES - size,), jnp.int32)])[None]
    packet, moved = call(
        partial(prepare_kernel, half_rows, rows),
        [shape((wide, packet_lines, LANES), bf16), shape((ROWS, tokens))],
        passage_ids, query_ids, negatives, small, vectors[None], jnp.asarray(seq_np, jnp.int32)[None], jnp.asarray(pos_np, jnp.int32)[None], w_ffn_up,
        near_outs=(0,), name="prepare",
    )
    packet_own = exchange(packet)
    (table,) = call(build_kernel, [shape((half, LANES))], embedding, name="build", flops=10**8)
    packet_own, table = tie(packet_own, table)
    packet_other = swap(packet_own)
    low_mats, down_low = call(
        cast_kernel, [shape((block, 5 * D), bf16), shape((hidden, D), bf16)],
        attn_in, attn_out, head, w_ffn_down, near_outs=(0,), name="cast",
    )
    mats = lax.all_gather(low_mats, ALL, axis=0, tiled=True)

    def numbers_of(packets):
        ids = packets[:, :chunks].astype(f32) * 256.0 + packets[:, chunks : 2 * chunks].astype(f32)
        local = ids - (group * half_rows).astype(f32)
        row_at = jnp.clip(jnp.where(local >= half, local - half, local), 0, half - 1)
        first = packets[:, at_note, 0].astype(f32) + 256.0 * packets[:, at_note, LANES - 1].astype(f32)
        return row_at.astype(jnp.int32).reshape(-1), first.astype(jnp.int32)

    look = partial(lookup, half_rows=half_rows, feats=feats, count=tokens)
    num_own, num_other = numbers_of(packet_own), numbers_of(packet_other)
    theirs = look(where, *num_other, packet_other, table)
    xt = exchange(look(where, *num_own, packet_own, table) + swap(theirs)).reshape(D, tokens)
    numbers = jnp.concatenate([num_own[0], num_other[0]])
    firsts = jnp.concatenate([num_own[1], num_other[1]])
    packets = jnp.concatenate([packet_own, packet_other], 0)
    ordered = in_order(packet_own, packet_other, group)
    w_up = ordered[:, packet_lines - 2 * block :, :hidden].reshape(devices, 2, block, hidden).transpose(0, 2, 1, 3).reshape(D, 2 * hidden)
    vec = ordered[:, at_note + 1 : at_note + 1 + vec_lines].astype(f32).reshape(devices, -1)
    vec = vec[:, : vectors.shape[0]].reshape(-1, D)
    bias_all = vec[11:].reshape(2, wide, hidden)
    bias_up = lax.dynamic_slice(bias_all, (0, place, 0), (2, 1, hidden)).reshape(1, 2 * hidden)
    notes = packets[:, at_note].astype(f32)
    at = 1 + qry_count
    picked = jnp.concatenate(
        [notes[:, at : at + qry_count, None], notes[:, at + qry_count : at + qry_count + negatives.size].reshape(devices, qry_count, -1)], 2
    ).astype(jnp.int32)
    pick_dev = picked // pas_count
    pick_row = (((pick_dev // wide) ^ group) * wide + pick_dev % wide) * ROWS + picked % pas_count
    pick_row = jnp.concatenate([notes[:, 1 : 1 + qry_count, None].astype(jnp.int32), pick_row], 2)
    pick_rows = jnp.pad(pick_row, ((0, 0), (pas_count, ROWS - rows), (0, 0))).reshape(devices * ROWS, -1)

    xt, vec, bias_up, pick_rows, w_up, packets, numbers, firsts = tie(xt, vec, bias_up, pick_rows, w_up, packets, numbers, firsts)
    tile_lines = ROWS * (D // LANES)
    heads_at, units = head_lines(chunks), 2 * hidden
    sent, qk, facts, y, probs, psum, normed1, inv1 = call(
        partial(attend_kernel, rows),
        [
            shape((wide, tile_lines, LANES), bf16), shape((SIDE, D), bf16), shape((3 * tile_lines, LANES), bf16),
            shape((SIDE, D), bf16), shape((SIDE, tokens)), shape((SIDE, 1)), shape((ROWS, D)), shape((ROWS, 1)),
        ],
        xt, vec, moved,
        far=(mats,), near=(0,), near_outs=(0,), scratch=weight_scratch(4), name="attend", flops=10**9,
    )
    x_own, x_other = pair(sent)
    early, known = call(
        partial(pack_early_kernel, rows), [shape((wide, block, LANES), bf16), shape((heads_at + 3 * tile_lines, LANES), bf16)],
        qk, probs, facts, after=(sent,), name="pack_early", flops=10**8,
    )
    known_all = lax.all_gather(known, ALL, axis=0, tiled=False)
    down_other = swap(down_low)
    u, h, f_mine = call(
        ffn_kernel, [shape((lines, units)), shape((lines, units), bf16), shape((lines, D), bf16)], x_own, w_up, down_low, down_other, bias_up,
        scalars=(where,), after=(pinned(early),), near=(0, 3), near_outs=(2,), name="ffn", flops=10**8, vmem=16,
    )
    f_parts = exchange(f_mine.reshape(wide, ROWS, D))
    (f_sum,) = call(total_kernel, [shape((wide, tile_lines, LANES), bf16)], f_parts, near=(0,), near_outs=(0,), name="total")
    f_own, f_other = pair(f_sum)
    loss, pooled, d_c, d_res2, d_f, d_u, d_sum, sums, sums_up = call(
        middle_kernel,
        [
            shape((1, 1)), shape((devices * ROWS, D), bf16), shape((devices * ROWS, D), bf16), shape((devices * ROWS, D)),
            shape((lines, D), bf16), shape((lines, units), bf16), shape((wide, tile_lines + block, LANES), bf16),
            shape((ROWS, D)), shape((1, D)),
        ],
        x_own, x_other, f_own, f_other, u, w_up, down_low, down_other, vec, pick_rows, early,
        scalars=(where,), far=(mats,), scratch=weight_scratch(1), near=(0, 1, 2, 3), near_outs=(6,), name="middle", flops=10**9, vmem=32,
    )
    got = exchange(d_sum)
    got_other = swap(got)
    down_mine, down_theirs, d_whead, up_mine, up_theirs = call(
        ffn_grads_kernel,
        [shape((hidden, D)), shape((hidden, D), bf16), shape((block, D)), shape((D // 2, units)), shape((D // 2, units), bf16)],
        x_own, h, d_f, d_u, pooled, d_c,
        scalars=(where,), after=(d_sum,), near=(0,), name="ffn_grads", flops=10**8,
    )
    late, last, z = call(
        partial(attend_back_kernel, rows),
        [shape((wide, block + ROWS + heads_at, LANES), bf16), shape((3 * tile_lines, LANES), bf16), shape((SIDE, D), bf16)],
        got, d_res2, sums_up, normed1, inv1, probs, psum, xt, vec,
        scalars=(place_at,), far=(mats,), after=(pinned(up_mine),), near=(0,), near_outs=(0,), scratch=weight_scratch(4), name="attend_back", flops=10**9,
    )
    late_own, late_other = pair(late)
    (packed,) = call(
        partial(pack_kernel, rows), [shape((wide, 3 * tile_lines + 4 * block, LANES), bf16)], last, y, z, up_mine, swap(up_theirs),
        after=(late,), near=(4,), name="pack",
    )
    last_own = exchange(once(packed, late_own))
    d_table, square = spread_tokens(
        where, numbers, firsts, packets, (got, got_other), (late_own, late_other), known_all, tile_lines, rows, half_rows, feats, tokens
    )
    piece = last_own[:1, :ROWS] + (square[None] * 0.0).astype(bf16)
    last_own = lax.dynamic_update_slice(last_own, piece, (0, 0, 0))
    last_other = swap(last_own)
    d_attn_in, d_wo, d_wup, d_down, d_vec, squares = call(
        partial(grads_kernel, rows),
        [shape((block, 3 * D)), shape((block, D)), shape((block, FF)), shape((hidden, D)), shape((16, D)), shape((devices, ROWS, LANES))],
        known_all, last_own, last_other, d_whead, down_mine, swap(down_theirs), sums, square,
        scalars=(where,),
        scratch=[pltpu.VMEM((devices * ROWS, D), f32)] * 6 + [pltpu.VMEM((D, LANES), f32)] * 2 + [pltpu.VMEM((D, D), f32)],
        near=(1, 2, 5), near_outs=(5,), name="grads", flops=10**9, vmem=32,
    )
    squares_got = lax.all_to_all(squares, ALL, split_axis=0, concat_axis=0, tiled=True)
    d_vectors = lax.dynamic_slice(d_vec.reshape(-1), (device * vectors.shape[0],), vectors.shape)
    step_float = step_count[0].astype(f32)
    scales = jnp.stack([1.0 / (1.0 - jnp.power(0.9, step_float)), 1.0 / (1.0 - jnp.power(0.999, step_float))])
    grads = (d_attn_in, d_wo, d_wup, d_down, d_whead)
    middle_state = state[3:18]
    slots, step_rows = 3, ROWS
    norm, factor, *new = call(
        partial(adam_kernel, len(grads)),
        [shape((1, 1)), shape((1, 1))] + [shape(t.shape) for t in middle_state],
        squares_got, *grads, *middle_state,
        scalars=(scales,), far=(*state[:3], d_table), far_outs=[shape(embedding.shape)] * 3,
        scratch=[
            pltpu.VMEM((slots, 3, step_rows, half_rows), f32), pltpu.VMEM((slots, step_rows, half_rows), bf16),
            pltpu.VMEM((slots, 3, step_rows, half_rows), f32),
            pltpu.SemaphoreType.DMA((slots, 4)), pltpu.SemaphoreType.DMA((slots, 3)),
        ],
        near=(0,), name="adam", vmem=40,
    )
    new_vectors = update(*state[18:], d_vectors * factor[0, 0], RATES[6], scales[0], scales[1])
    return (loss[0, 0], norm[0, 0]) + tuple(new[15:]) + tuple(new[:15]) + new_vectors


def solution(mesh):
    split_rows = P(ALL, None)
    flat = P(ALL)
    table = P("wide", "group")
    mats = (table,) * 3 + (split_rows,) * 15 + (flat,) * 3
    in_specs = (split_rows, split_rows, flat, flat, flat, split_rows, flat, P()) + mats
    wide = mesh.shape["wide"]
    thick = D % (2 * wide * ROWS) == 0 and wide * ROWS <= LANES
    return jax.shard_map(
        partial(body if thick else plain_body, wide), mesh=mesh, in_specs=in_specs, out_specs=(P(), P()) + mats, check_vma=False
    )
```
